32 devices in a mesh: row: 8 (over y, x, core), col: 4 (over z).
Axes of the slice: x: 2, y: 2, z: 4, core: 2. Of those that a mesh axis runs over, the one named last changes fastest.
Arguments:
- left_panels: float32 [8, 4, 16, 128, 128], P('row', 'col'), may hold values from -6 to 6
- right_panels: float32 [2, 4, 8, 12, 128, 128], P(None, 'col', 'row'), may hold values from -0.25 to 0.25
- product_lists: int32 [8, 4, 8, 96, 3], P('row', 'col'), may hold values from -1 to 23, as said below
Outputs:
- product_blocks: float32 [8, 4, 24, 128, 128], P('row', 'col')
The draws below stay inside these ranges and needn't reach their ends.
Inputs may be any that keep to these rules, and one draw needn't show every extreme that they name: `product_lists`: each entry is (left slot < 16, right slot < 12, output slot < 24). In each list the first entries, at least half of 96 and at most 96, are live with distinct (left, right) pairs, the rest are -1 in all three columns; some list holds 96 live entries.
All inputs are finite; a program needn't handle non-finite values.
Results may differ from the reference program's by a relative error of at most 0.0003.
Values sent between devices are 32-bit elements; how exact they have to be, the bound alone decides.
A program may use at most 128 MiB of HBM per device.

```python
import jax
import jax.numpy as jnp
from jax import lax

BLK = 128
LCAP = 16
RCAP = 12
PCAP = 96
OCAP = 24
STEPS = 8
QP = 2
N_ROW = 8
N_COL = 4


def draw_product_lists(key, part):
    cells = N_ROW * N_COL * STEPS
    keys = jax.random.split(key, 6)
    pair_keys = jax.random.split(keys[0], cells)
    pairs = jax.vmap(lambda one_key: jax.random.permutation(one_key, LCAP * RCAP)[:PCAP])(pair_keys)
    out_slots = jax.random.randint(keys[1], (cells, PCAP), 0, OCAP)
    half_count = PCAP // 2
    first = jax.random.randint(keys[2], (cells,), 0, PCAP - half_count + 1)
    second = jax.random.randint(keys[3], (cells,), 0, PCAP - half_count + 1)
    counts = half_count + jnp.minimum(first, second)
    chosen = jax.random.randint(keys[5], (), 0, cells)
    counts = jnp.where(jnp.arange(cells) == chosen, PCAP, counts)
    live_mask = jnp.arange(PCAP)[None, :] < counts[:, None]
    left_col = jnp.where(live_mask, pairs // RCAP, -1)
    right_col = jnp.where(live_mask, pairs % RCAP, -1)
    out_col = jnp.where(live_mask, out_slots, -1)
    stacked = jnp.stack([left_col, right_col, out_col], axis=-1).astype(jnp.int32)
    return stacked.reshape(N_ROW, N_COL, STEPS, PCAP, 3)


def steps_of(rng, shape, pieces, low, top_value):
    factor_of, own = 1.0, jax.random.fold_in(rng, 6)
    for dim, shards_of in pieces:
        steps = jnp.exp(jax.random.uniform(jax.random.fold_in(own, dim), (shards_of,), jnp.float32, low / len(pieces), top_value / len(pieces)))
        factor_of = factor_of * jnp.repeat(steps, shape[dim] // shards_of).reshape([-1 if axis == dim else 1 for axis in range(len(shape))])
    return factor_of


def noise(rng, extent, scale, bound, cuts=(), kind=jnp.bfloat16):
    values = scale * jax.random.normal(rng, extent, jnp.float32)
    if cuts:
        values = values * steps_of(rng, extent, cuts, -0.22, 0.18)
    return jnp.clip(values, -bound, bound).astype(kind)


def setup_inputs(seed: int = 0) -> dict:
    seeds = jax.random.split(jax.random.key(seed), 4)
    left_panels = noise(seeds[0], (N_ROW, N_COL, LCAP, BLK, BLK), 1.0, 6.0, ((0, 8), (1, 4)), jnp.float32)
    right_panels = noise(seeds[1], (QP, N_COL, N_ROW, RCAP, BLK, BLK), (4 * BLK) ** -0.5, 0.25, ((1, 4), (2, 8)), jnp.float32)
    product_lists = draw_product_lists(jax.random.fold_in(seeds[3], 71), 0)
    return {"left_panels": left_panels, "right_panels": right_panels, "product_lists": product_lists}


def contribute(left_stack, right_panel, entries, slot_count):
    live_mask = entries[:, 0] >= 0
    left_slot = jnp.maximum(entries[:, 0], 0)
    right_slot = jnp.maximum(entries[:, 1], 0)
    taken_left = jnp.take(left_stack, left_slot, axis=0)
    taken_right = jnp.take(right_panel, right_slot, axis=0)
    blocks = jnp.einsum("pik,pkj->pij", taken_left, taken_right, precision=lax.Precision.HIGHEST)
    slot_ids = jnp.arange(slot_count, dtype=jnp.int32)
    onehot = ((entries[:, 2][None, :] == slot_ids[:, None]) & live_mask[None, :]).astype(blocks.dtype)
    return jnp.einsum("op,pij->oij", onehot, blocks, precision=lax.Precision.HIGHEST)


def reference(left_panels, right_panels, product_lists):
    def device_block(device_index):
        row_pos = device_index // N_COL
        col_pos = device_index % N_COL
        running = jnp.zeros((OCAP, BLK, BLK), left_panels.dtype)
        for step_num in range(STEPS):
            kgroup = (row_pos + col_pos + step_num) % N_ROW
            left_stack = left_panels[kgroup, col_pos]
            right_panel = right_panels[kgroup // N_COL, kgroup % N_COL, row_pos]
            running = running + contribute(left_stack, right_panel, product_lists[row_pos, col_pos, step_num], OCAP)
        return running

    results = lax.map(device_block, jnp.arange(N_ROW * N_COL, dtype=jnp.int32))
    return results.reshape(N_ROW, N_COL, OCAP, BLK, BLK)
```

```python
import functools

import jax
import jax.numpy as jnp
from jax import lax
from jax.experimental import pallas as pl
from jax.experimental.pallas import tpu as pltpu
from jax.sharding import PartitionSpec as P

OCAP = 24
UNROLL = 16
AHEAD = 3
MESH = pl.DeviceIdType.MESH
PARTS = 4
END_ODD = (0, 4, 1, 5, 2, 6, 3, 7)
END_EVEN = (0, 4, 2, 6)
INNER_ODD = (1, 5, 0, 2, 4, 6, 3, 7)
INNER_EVEN = (1, 5, 0, 2, 9, 13, 11, 15, 4, 6, 3, 7)


def arrange(lists_ref, table, step, slot_count):
    step_count, count = lists_ref.shape[1], lists_ref.shape[2]
    width = table.shape[1]
    left, right, out = (lists_ref[part, pl.ds(step, 1), :] for part in range(3))
    live = left >= 0
    slots = jnp.where(live, out, slot_count)
    lane = lax.broadcasted_iota(jnp.int32, (count, count), 1)
    same = lax.broadcasted_iota(jnp.int32, (count, count), 0) == lane

    def column(row):
        return jnp.sum(jnp.where(same, jnp.broadcast_to(row, (count, count)), 0), axis=1, keepdims=True)

    key = jnp.broadcast_to(slots, (count, count)) * count + lane
    key_column = jnp.sum(jnp.where(same, key, 0), axis=1, keepdims=True)
    rank = jnp.sum((key < key_column).astype(jnp.int32), axis=1, keepdims=True)
    packed = column(jnp.where(live, left + right * 256, 0) + slots * 65536)
    wide = lax.broadcasted_iota(jnp.int32, (count, width), 1)
    table[pl.ds(step, 1), :] = jnp.sum(jnp.where(rank == wide, packed, 0), axis=0, keepdims=True)
    slot_column = column(slots)
    upto = (slot_column <= wide).astype(jnp.int32) + (slot_column == wide).astype(jnp.int32) * 65536
    table[pl.ds(step_count + step, 1), :] = jnp.sum(upto, axis=0, keepdims=True)


def kernel(row_count, col_count, lists_ref, left_ref, right_ref, out_ref,
           left_all, right_all, lhs, rhs, sums, table, code_ref, zsend, zrecv, lsend, psend, hsend, lrecv, hrecv, local_sem):
    row = lax.axis_index("row")
    col = lax.axis_index("col")
    q_count = right_ref.shape[0]
    left_blocks, blk = left_ref.shape[2], left_ref.shape[3]
    right_blocks = right_ref.shape[3]
    step_count, pair_count = lists_ref.shape[1], lists_ref.shape[2]
    slot_count = out_ref.shape[0]
    groups = row_count // 2
    group, parity = row // 2, row % 2
    partner = group * 2 + 1 - parity
    square = groups == 4
    direct = (1, 2) if square else tuple(range(1, groups))

    def group_at(i):
        return (group // 2 * 2 + 1 - group % 2 if i == 1 else lax.rem(group + 2, groups)) if square and i in (1, 2) else (
            groups - 1 - group if square and i == 3 else lax.rem(group + i, groups))

    def row_at(i, same):
        return group_at(i) * 2 + (parity if same else 1 - parity)

    barrier = pltpu.get_barrier_semaphore()
    for i in direct:
        pl.semaphore_signal(barrier, inc=1, device_id=(row_at(i, True), col), device_id_type=MESH)
    pl.semaphore_signal(barrier, inc=1, device_id=(partner, col), device_id_type=MESH)

    @pl.when(col > 0)
    def _():
        pl.semaphore_signal(barrier, inc=1, device_id=(row, col - 1), device_id_type=MESH)

    @pl.when(col < col_count - 1)
    def _():
        pl.semaphore_signal(barrier, inc=1, device_id=(row, col + 1), device_id_type=MESH)

    own = [pltpu.make_async_copy(left_ref.at[0, 0], left_all.at[row], local_sem.at[0])]
    for q in range(q_count):
        own.append(pltpu.make_async_copy(right_ref.at[q, 0, 0], right_all.at[q, col], local_sem.at[1 + q]))
    for copy in own:
        copy.start()

    ends = (col == 0).astype(jnp.int32) + (col == col_count - 1).astype(jnp.int32)
    pl.semaphore_wait(barrier, len(direct) + 3 - ends)

    def along(direction, q, source, from_ref):
        return pltpu.make_async_remote_copy(
            src_ref=from_ref,
            dst_ref=right_all.at[q, source],
            send_sem=zsend.at[direction, q, source],
            recv_sem=zrecv.at[q, source],
            device_id=(row, col + (1 if direction else -1)),
            device_id_type=MESH,
        )

    def own_panel(direction, q):
        return along(direction, q, col, right_ref.at[q, 0, 0])

    def relayed(direction, q, source):
        return along(direction, q, source, right_all.at[q, source])

    def across(i):
        return pltpu.make_async_remote_copy(
            src_ref=left_ref.at[0, 0],
            dst_ref=left_all.at[row],
            send_sem=lsend.at[i],
            recv_sem=lrecv.at[row],
            device_id=(row_at(i, True), col),
            device_id_type=MESH,
        )

    def handed(i):
        source = row_at(i, True)
        return pltpu.make_async_remote_copy(
            src_ref=left_ref.at[0, 0] if i == 0 else left_all.at[source],
            dst_ref=left_all.at[source],
            send_sem=psend.at[i],
            recv_sem=lrecv.at[source],
            device_id=(partner, col),
            device_id_type=MESH,
        )

    def arrived_left(source):
        return pltpu.make_async_remote_copy(
            src_ref=left_all.at[source],
            dst_ref=left_all.at[source],
            send_sem=psend.at[0],
            recv_sem=lrecv.at[source],
            device_id=(partner, col),
            device_id_type=MESH,
        )

    half = left_blocks // 2
    pieces = (pl.ds(0, half), pl.ds(half, left_blocks - half))

    def half_of(i, piece, target):
        source = row_at(i, True)
        return pltpu.make_async_remote_copy(
            src_ref=left_all.at[source, pieces[piece]],
            dst_ref=left_all.at[source, pieces[piece]],
            send_sem=hsend.at[piece],
            recv_sem=hrecv.at[piece],
            device_id=(row_at(target, True), col),
            device_id_type=MESH,
        )

    for q in range(q_count):
        @pl.when(col > 0)
        def _():
            own_panel(0, q).start()

        @pl.when(col < col_count - 1)
        def _():
            own_panel(1, q).start()

    for i in direct:
        across(i).start()
    handed(0).start()

    lax.fori_loop(0, step_count, lambda step, c: (arrange(lists_ref, table, step, slot_count), c)[1], 0)
    out_ref[...] = jnp.zeros_like(out_ref)
    rhs[:, blk:, blk:] = jnp.zeros((right_blocks, blk, blk), rhs.dtype)
    for copy in own:
        copy.wait()

    sides = jnp.minimum(col, col_count - 1 - col)

    def item_of(item):
        rest = item - q_count
        later = rest - 2 * q_count * sides
        both = later < 0
        distance = jnp.where(both, rest // (2 * q_count) + 1, sides + 1 + later // q_count)
        q = jnp.where(both, rest % (2 * q_count) // 2, later % q_count)
        lower = jnp.where(both, rest % 2 == 0, col * 2 > col_count - 1)
        source = jnp.where(lower, col - distance, col + distance)
        own_item = rest < 0
        return jnp.where(own_item, col, source), jnp.where(own_item, item, q)

    def relay(item):
        source, q = item_of(item)

        @pl.when(source != col)
        def _():
            relayed(0, q, source).wait_recv()

        @pl.when((source < col) & (col < col_count - 1))
        def _():
            relayed(1, q, source).start()

        @pl.when((source > col) & (col > 0))
        def _():
            relayed(0, q, source).start()

    forwards = 1 - ends
    first = q_count * (2 + jnp.minimum(sides, 1))

    def relay_many(start, stop):
        lax.fori_loop(start, stop, lambda item, c: (relay(item), c)[1], 0)

    for i in direct:
        arrived_left(row_at(i, True)).wait_recv()
        if square:
            half_of(i, i - 1, 3 - i).start()
        handed(i).start()
    relay_many(q_count, first)
    listed = pltpu.make_async_copy(table, code_ref, local_sem.at[1 + q_count])
    listed.start()
    if square:
        half_of(3, 0, 1).wait_recv()
        half_of(3, 1, 1).wait_recv()
        handed(3).start()
    for i in range(groups):
        arrived_left(row_at(i, False)).wait_recv()
    listed.wait()

    def job(item, carry):
        source, q = item_of(item)
        kgroup = q * col_count + source
        step = lax.rem(kgroup - row - col + 2 * row_count, row_count)

        @pl.when(step < step_count)
        def _():
            def split_left(i, c):
                x = left_all[kgroup, i]
                high = x.astype(jnp.bfloat16)
                lhs[i, :, :blk] = high
                lhs[i, :, blk:] = (x - high.astype(jnp.float32)).astype(jnp.bfloat16)
                return c

            lax.fori_loop(0, left_blocks, split_left, 0)

        ahead = item + AHEAD * forwards

        @pl.when((ahead >= first) & (ahead < row_count))
        def _():
            relay(ahead)

        @pl.when(step < step_count)
        def _():
            def split_right(i, c):
                x = right_all[q, source, i]
                high = x.astype(jnp.bfloat16)
                rhs[i, :blk, :blk] = high
                rhs[i, blk:, :blk] = high
                rhs[i, :blk, blk:] = (x - high.astype(jnp.float32)).astype(jnp.bfloat16)
                return c

            lax.fori_loop(0, right_blocks, split_right, 0)

            def some(batch, carry):
                total, before = carry
                for u in range(UNROLL):
                    p = batch * UNROLL + u
                    code = code_ref[step, p]
                    both = jnp.dot(
                        lhs[code & 255], rhs[(code >> 8) & 255], preferred_element_type=jnp.float32
                    )
                    slot = code >> 16
                    keep = (slot == before).astype(jnp.float32)
                    total = total * keep + (both[:, :blk] + both[:, blk:])
                    sums[p] = total
                    before = slot
                return total, before

            lax.fori_loop(0, pair_count // UNROLL, some, (jnp.zeros((blk, blk), jnp.float32), jnp.int32(-1)))

            def put(o, c):
                code = code_ref[step_count + step, o]
                found = ((code >> 16) > 0).astype(jnp.float32)
                out_ref[o] = out_ref[o] + sums[jnp.maximum((code & 65535) - 1, 0)] * found
                return c

            lax.fori_loop(0, slot_count, put, 0)

        return carry

    lax.fori_loop(0, row_count, job, 0)

    for q in range(q_count):
        @pl.when(col > 0)
        def _():
            own_panel(0, q).wait_send()

        @pl.when(col < col_count - 1)
        def _():
            own_panel(1, q).wait_send()

    def sent(item, carry):
        source, q = item_of(item)

        @pl.when((source < col) & (col < col_count - 1))
        def _():
            relayed(1, q, source).wait_send()

        @pl.when((source > col) & (col > 0))
        def _():
            relayed(0, q, source).wait_send()

        return carry

    lax.fori_loop(q_count, row_count, sent, 0)
    for i in direct:
        across(i).wait_send()
    if square:
        half_of(1, 0, 2).wait_send()
        half_of(2, 1, 1).wait_send()
    for i in range(groups):
        handed(i).wait_send()


def fold_kernel(row_count, col_count, lists_ref, left_ref, right_ref, out_ref,
                left_all, right_all, lhs, rhs, sums, acc, table, table_in, code_ref,
                zsend, zrecv, lsend, psend, hsend, lrecv, hrecv, esend, erecv, ehrecv, tsem, ssend, srecv, local_sem):
    row = lax.axis_index("row")
    col = lax.axis_index("col")
    q_count = right_ref.shape[0]
    left_blocks, blk = left_ref.shape[2], left_ref.shape[3]
    right_blocks = right_ref.shape[3]
    step_count, pair_count = lists_ref.shape[1], lists_ref.shape[2]
    slot_count = out_ref.shape[0]
    groups = row_count // 2
    group, parity = row // 2, row % 2
    partner = group * 2 + 1 - parity
    low = col * 2 < col_count
    at_end = (col == 0) | (col == col_count - 1)
    even = parity == 0
    odd = parity == 1
    inward = jnp.where(low, col + 1, col - 1)
    outward = jnp.where(low, col - 1, col + 1)
    near = jnp.where(low, 0, col_count - 1)

    def source_of(place):
        return jnp.where(low, place, col_count - 1 - place)

    def group_at(i):
        return (group, group // 2 * 2 + 1 - group % 2, lax.rem(group + 2, groups), groups - 1 - group)[i]

    def row_at(i, same):
        return group_at(i) * 2 + (parity if same else 1 - parity)

    barrier = pltpu.get_barrier_semaphore()
    for i in (1, 2):
        pl.semaphore_signal(barrier, inc=1, device_id=(row_at(i, True), col), device_id_type=MESH)
    pl.semaphore_signal(barrier, inc=1, device_id=(partner, col), device_id_type=MESH)
    pl.semaphore_signal(barrier, inc=1, device_id=(row, inward), device_id_type=MESH)

    @pl.when(jnp.logical_not(at_end))
    def _():
        pl.semaphore_signal(barrier, inc=1, device_id=(row, outward), device_id_type=MESH)

    own = [pltpu.make_async_copy(left_ref.at[0, 0], left_all.at[row], local_sem.at[0])]
    for q in range(q_count):
        own.append(pltpu.make_async_copy(right_ref.at[q, 0, 0], right_all.at[q, col], local_sem.at[1 + q]))
    for copy in own:
        copy.start()
    pl.semaphore_wait(barrier, jnp.where(at_end, 4, 5))

    def panel(direction, q, source, from_ref):
        return pltpu.make_async_remote_copy(
            src_ref=from_ref,
            dst_ref=right_all.at[q, source],
            send_sem=zsend.at[direction, q, source],
            recv_sem=zrecv.at[q, source],
            device_id=(row, inward if direction else outward),
            device_id_type=MESH,
        )

    def own_panel(direction, q):
        return panel(direction, q, col, right_ref.at[q, 0, 0])

    def relayed(direction, q, source):
        return panel(direction, q, source, right_all.at[q, source])

    def left_copy(source_ref, index, send_sem, recv_sem, device):
        return pltpu.make_async_remote_copy(
            src_ref=source_ref,
            dst_ref=left_all.at[index],
            send_sem=send_sem,
            recv_sem=recv_sem,
            device_id=device,
            device_id_type=MESH,
        )

    def across(i):
        return left_copy(left_ref.at[0, 0], row, lsend.at[i], lrecv.at[row], (row_at(i, True), col))

    def handed(i):
        source = row_at(i, True)
        return left_copy(left_ref.at[0, 0] if i == 0 else left_all.at[source], source,
                         psend.at[i], lrecv.at[source], (partner, col))

    def arrived_left(source):
        return left_copy(left_all.at[source], source, psend.at[0], lrecv.at[source], (partner, col))

    half = left_blocks // 2
    pieces = (pl.ds(0, half), pl.ds(half, left_blocks - half))

    def half_copy(index, piece, send_sem, recv_sem, target):
        return pltpu.make_async_remote_copy(
            src_ref=left_all.at[index, pieces[piece]],
            dst_ref=left_all.at[index, pieces[piece]],
            send_sem=send_sem,
            recv_sem=recv_sem,
            device_id=(row_at(target, True), col),
            device_id_type=MESH,
        )

    def half_of(i, piece, target):
        return half_copy(row_at(i, True), piece, hsend.at[piece], hrecv.at[piece], target)

    lent = row + (col == 0).astype(jnp.int32)

    def extra_out():
        return left_copy(left_all.at[lent], row_count + group, esend.at[0], erecv.at[group], (row, inward))

    def extra_across(i):
        index = row_count + group
        return left_copy(left_all.at[index], index, esend.at[i], erecv.at[group], (row_at(i, True), col))

    def extra_arrived(i):
        index = row_count + group_at(i)
        return left_copy(left_all.at[index], index, esend.at[0], erecv.at[group_at(i)], (row_at(1, True), col))

    def extra_half(i, piece, target):
        return half_copy(row_count + group_at(i), piece, esend.at[3 + piece], ehrecv.at[piece], target)

    def table_out():
        return pltpu.make_async_remote_copy(
            src_ref=table,
            dst_ref=table_in,
            send_sem=tsem.at[0],
            recv_sem=tsem.at[1],
            device_id=(row, inward),
            device_id_type=MESH,
        )

    part = slot_count // PARTS

    def partial_sum(i):
        where = pl.ds(slot_count + i * part, part)
        return pltpu.make_async_remote_copy(
            src_ref=acc.at[where],
            dst_ref=acc.at[where],
            send_sem=ssend.at[i],
            recv_sem=srecv.at[i],
            device_id=(row, near),
            device_id_type=MESH,
        )

    inner = jnp.logical_not(at_end)
    folding = inner & even
    folded = at_end & even

    @pl.when(inner & odd)
    def _():
        for q in range(q_count):
            own_panel(0, q).start()

    for q in range(q_count):
        own_panel(1, q).start()
    for i in (1, 2):
        across(i).start()
    handed(0).start()

    lax.fori_loop(0, step_count, lambda step, c: (arrange(lists_ref, table, step, slot_count), c)[1], 0)

    @pl.when(folded)
    def _():
        table_out().start()

    for copy in own:
        copy.wait()
    arrived_left(partner).wait_recv()

    @pl.when(folded)
    def _():
        extra_out().start()

    listed = pltpu.make_async_copy(table, code_ref.at[pl.ds(0, 2 * step_count)], local_sem.at[1 + q_count])
    listed.start()
    zero = jnp.zeros((blk, blk), jnp.float32)

    def clear(o, c):
        acc[o] = zero
        return c

    lax.fori_loop(0, jnp.where(folding, 2 * slot_count, slot_count), clear, 0)
    rhs[:, blk:, blk:] = jnp.zeros((right_blocks, blk, blk), rhs.dtype)

    def receive(place, q):
        relayed(0, q, source_of(place)).wait_recv()

    def receive_inner(place, q):
        receive(place, q)
        if place == 0:
            relayed(1, q, source_of(place)).start()
        elif place == 2:
            relayed(0, q, source_of(place)).start()
        else:
            @pl.when(odd)
            def _():
                relayed(0, q, source_of(place)).start()

    @pl.when(inner)
    def _():
        receive_inner(0, 0)
        receive_inner(2, 0)

    for i in (1, 2):
        arrived_left(row_at(i, True)).wait_recv()
        half_of(i, i - 1, 3 - i).start()
        handed(i).start()

    @pl.when(folding)
    def _():
        extra_arrived(0).wait_recv()
        extra_across(1).start()
        extra_across(2).start()
        table_out().wait_recv()
        fetched = pltpu.make_async_copy(table_in, code_ref.at[pl.ds(2 * step_count, 2 * step_count)], local_sem.at[2 + q_count])
        fetched.start()
        fetched.wait()

    @pl.when(inner)
    def _():
        for q in range(1, q_count):
            receive_inner(0, q)
            receive_inner(2, q)

    half_of(3, 0, 1).wait_recv()
    half_of(3, 1, 1).wait_recv()
    handed(3).start()
    for i in range(1, groups):
        arrived_left(row_at(i, False)).wait_recv()
    listed.wait()

    def job(item, carry):
        def pick(choices):
            value = jnp.int32(choices[-1])
            for at in range(len(choices) - 1):
                value = jnp.where(item == at, choices[at], value)
            return value

        code = jnp.where(
            at_end,
            jnp.where(even, pick(END_EVEN), pick(END_ODD)),
            jnp.where(even, pick(INNER_EVEN), pick(INNER_ODD)),
        )
        place, q, extra = code % 4, code // 4 % 2, code // 8
        source = source_of(place)
        kgroup = q * col_count + source
        owner = jnp.where(extra == 1, near, col)
        step = lax.rem(kgroup - row - owner + 2 * row_count, row_count)
        code_row = step + extra * 2 * step_count
        left_at = jnp.where(extra == 1, row_count + kgroup // 2, kgroup)
        base = extra * slot_count

        @pl.when(at_end & (place > 0))
        def _():
            relayed(0, q, source).wait_recv()

        @pl.when(folding & (item == 2))
        def _():
            extra_arrived(1).wait_recv()
            extra_arrived(2).wait_recv()
            extra_half(1, 0, 2).start()
            extra_half(2, 1, 1).start()

        @pl.when(folding & (item == 4))
        def _():
            extra_half(3, 0, 1).wait_recv()
            extra_half(3, 1, 1).wait_recv()

        for turn in range(2):
            @pl.when(inner & (item == jnp.where(even, 6 + turn, 4 + 2 * turn)))
            def _():
                receive_inner(3, turn)

        def split_left(i, c):
            x = left_all[left_at, i]
            high = x.astype(jnp.bfloat16)
            lhs[i, :, :blk] = high
            lhs[i, :, blk:] = (x - high.astype(jnp.float32)).astype(jnp.bfloat16)
            return c

        lax.fori_loop(0, left_blocks, split_left, 0)

        def split_right(i, c):
            x = right_all[q, source, i]
            high = x.astype(jnp.bfloat16)
            rhs[i, :blk, :blk] = high
            rhs[i, blk:, :blk] = high
            rhs[i, :blk, blk:] = (x - high.astype(jnp.float32)).astype(jnp.bfloat16)
            return c

        lax.fori_loop(0, right_blocks, split_right, 0)

        def some(batch, carry):
            total, before = carry
            for u in range(UNROLL):
                p = batch * UNROLL + u
                entry = code_ref[code_row, p]
                both = jnp.dot(lhs[entry & 255], rhs[(entry >> 8) & 255], preferred_element_type=jnp.float32)
                slot = entry >> 16
                keep = (slot == before).astype(jnp.float32)
                total = total * keep + (both[:, :blk] + both[:, blk:])
                sums[p] = total
                before = slot
            return total, before

        lax.fori_loop(0, pair_count // UNROLL, some, (zero, jnp.int32(-1)))

        def put(o, c):
            entry = code_ref[step_count + code_row, o]
            found = ((entry >> 16) > 0).astype(jnp.float32)
            acc[base + o] = acc[base + o] + sums[jnp.maximum((entry & 65535) - 1, 0)] * found
            return c

        lax.fori_loop(0, slot_count, put, 0)

        @pl.when(folding & (item == 7))
        def _():
            for i in range(PARTS):
                partial_sum(i).start()

        return carry

    job_count = jnp.where(
        at_end,
        jnp.where(even, len(END_EVEN), len(END_ODD)),
        jnp.where(even, len(INNER_EVEN), len(INNER_ODD)),
    )
    lax.fori_loop(0, job_count, job, 0)

    @pl.when(folded)
    def _():
        for i in range(PARTS):
            partial_sum(i).wait_recv()

            def add(o, c):
                out_ref[o] = acc[o] + acc[slot_count + o]
                return c

            lax.fori_loop(i * part, (i + 1) * part, add, 0)

    @pl.when(jnp.logical_not(folded))
    def _():
        def move(o, c):
            out_ref[o] = acc[o]
            return c

        lax.fori_loop(0, slot_count, move, 0)

    for q in range(q_count):
        own_panel(1, q).wait_send()

    @pl.when(inner)
    def _():
        for q in range(q_count):
            relayed(1, q, source_of(0)).wait_send()
            relayed(0, q, source_of(2)).wait_send()

    @pl.when(inner & odd)
    def _():
        for q in range(q_count):
            own_panel(0, q).wait_send()
            relayed(0, q, source_of(3)).wait_send()

    @pl.when(folded)
    def _():
        table_out().wait_send()
        extra_out().wait_send()

    @pl.when(folding)
    def _():
        for i in (1, 2):
            extra_across(i).wait_send()
        extra_half(1, 0, 2).wait_send()
        extra_half(2, 1, 1).wait_send()
        for i in range(PARTS):
            partial_sum(i).wait_send()

    for i in (1, 2):
        across(i).wait_send()
    half_of(1, 0, 2).wait_send()
    half_of(2, 1, 1).wait_send()
    for i in range(groups):
        handed(i).wait_send()


def folded_call(row_count, col_count, lists, left_panels, right_panels, width):
    left_blocks, blk = left_panels.shape[2], left_panels.shape[3]
    q_count, right_blocks = right_panels.shape[0], right_panels.shape[3]
    step_count, pair_count = lists.shape[1], lists.shape[2]
    groups = row_count // 2
    dma = pltpu.SemaphoreType.DMA
    out = pl.pallas_call(
        functools.partial(fold_kernel, row_count, col_count),
        out_shape=jax.ShapeDtypeStruct((OCAP, blk, blk), jnp.float32),
        in_specs=[pl.BlockSpec(memory_space=pltpu.VMEM)] + [pl.BlockSpec(memory_space=pltpu.HBM)] * 2,
        out_specs=pl.BlockSpec(memory_space=pltpu.VMEM),
        scratch_shapes=[
            pltpu.VMEM((row_count + groups, left_blocks, blk, blk), jnp.float32),
            pltpu.VMEM((q_count, col_count, right_blocks, blk, blk), jnp.float32),
            pltpu.VMEM((left_blocks, blk, 2 * blk), jnp.bfloat16),
            pltpu.VMEM((right_blocks, 2 * blk, 2 * blk), jnp.bfloat16),
            pltpu.VMEM((pair_count, blk, blk), jnp.float32),
            pltpu.VMEM((2 * OCAP, blk, blk), jnp.float32),
            pltpu.VMEM((2 * step_count, width), jnp.int32),
            pltpu.VMEM((2 * step_count, width), jnp.int32),
            pltpu.SMEM((4 * step_count, width), jnp.int32),
            dma((2, q_count, col_count)),
            dma((q_count, col_count)),
            dma((groups,)),
            dma((groups,)),
            dma((2,)),
            dma((row_count,)),
            dma((2,)),
            dma((5,)),
            dma((groups,)),
            dma((2,)),
            dma((2,)),
            dma((PARTS,)),
            dma((PARTS,)),
            dma((3 + q_count,)),
        ],
        compiler_params=pltpu.CompilerParams(
            collective_id=0, has_side_effects=True, vmem_limit_bytes=50 * 1024 * 1024
        ),
    )(lists, left_panels, right_panels)
    return out[None, None]


def shards(row_count, col_count, left_panels, right_panels, product_lists):
    left_blocks, blk = left_panels.shape[2], left_panels.shape[3]
    q_count, right_blocks = right_panels.shape[0], right_panels.shape[3]
    pair_count = product_lists.shape[3]
    lists = jnp.transpose(product_lists[0, 0], (2, 0, 1))
    step_count = lists.shape[1]
    width = pl.cdiv(max(pair_count, OCAP), 128) * 128
    groups = row_count // 2
    if groups == 4 and col_count == 4 and q_count * col_count == row_count == step_count and OCAP % PARTS == 0:
        return folded_call(row_count, col_count, lists, left_panels, right_panels, width)
    out = pl.pallas_call(
        functools.partial(kernel, row_count, col_count),
        out_shape=jax.ShapeDtypeStruct((OCAP, blk, blk), jnp.float32),
        in_specs=[pl.BlockSpec(memory_space=pltpu.VMEM)] + [pl.BlockSpec(memory_space=pltpu.HBM)] * 2,
        out_specs=pl.BlockSpec(memory_space=pltpu.VMEM),
        scratch_shapes=[
            pltpu.VMEM((row_count, left_blocks, blk, blk), jnp.float32),
            pltpu.VMEM((q_count, col_count, right_blocks, blk, blk), jnp.float32),
            pltpu.VMEM((left_blocks, blk, 2 * blk), jnp.bfloat16),
            pltpu.VMEM((right_blocks, 2 * blk, 2 * blk), jnp.bfloat16),
            pltpu.VMEM((pair_count, blk, blk), jnp.float32),
            pltpu.VMEM((2 * step_count, width), jnp.int32),
            pltpu.SMEM((2 * step_count, width), jnp.int32),
            pltpu.SemaphoreType.DMA((2, q_count, col_count)),
            pltpu.SemaphoreType.DMA((q_count, col_count)),
            pltpu.SemaphoreType.DMA((groups,)),
            pltpu.SemaphoreType.DMA((groups,)),
            pltpu.SemaphoreType.DMA((2,)),
            pltpu.SemaphoreType.DMA((row_count,)),
            pltpu.SemaphoreType.DMA((2,)),
            pltpu.SemaphoreType.DMA((2 + q_count,)),
        ],
        compiler_params=pltpu.CompilerParams(
            collective_id=0, has_side_effects=True, vmem_limit_bytes=50 * 1024 * 1024
        ),
    )(lists, left_panels, right_panels)
    return out[None, None]


def solution(mesh):
    return jax.shard_map(
        functools.partial(shards, mesh.shape["row"], mesh.shape["col"]),
        mesh=mesh,
        in_specs=(
            P("row", "col", None, None, None),
            P(None, "col", "row", None, None, None),
            P("row", "col", None, None, None),
        ),
        out_specs=P("row", "col", None, None, None),
        check_vma=False,
    )
```

```python
import functools

import jax
import jax.numpy as jnp
from jax import lax
from jax.experimental import pallas as pl
from jax.experimental.pallas import tpu as pltpu
from jax.sharding import PartitionSpec as P

OCAP = 24
UNROLL = 16
AHEAD = 3
MESH = pl.DeviceIdType.MESH
PARTS = 4
END_ODD = (0, 4, 1, 5, 2, 6, 3, 7)
END_EVEN = (0, 4, 2, 6)
INNER_ODD = (0, 6, 4, 3, 7)
INNER_EVEN = (15, 0, 6, 4, 3, 7)


def arrange(lists_ref, table, step, slot_count):
    step_count, count = lists_ref.shape[1], lists_ref.shape[2]
    width = table.shape[1]
    left, right, out = (lists_ref[part, pl.ds(step, 1), :] for part in range(3))
    live = left >= 0
    slots = jnp.where(live, out, slot_count)
    lane = lax.broadcasted_iota(jnp.int32, (count, count), 1)
    same = lax.broadcasted_iota(jnp.int32, (count, count), 0) == lane

    def column(row):
        return jnp.sum(jnp.where(same, jnp.broadcast_to(row, (count, count)), 0), axis=1, keepdims=True)

    key = jnp.broadcast_to(slots, (count, count)) * count + lane
    key_column = jnp.sum(jnp.where(same, key, 0), axis=1, keepdims=True)
    rank = jnp.sum((key < key_column).astype(jnp.int32), axis=1, keepdims=True)
    packed = column(jnp.where(live, left + right * 256, 0) + slots * 65536)
    wide = lax.broadcasted_iota(jnp.int32, (count, width), 1)
    table[pl.ds(step, 1), :] = jnp.sum(jnp.where(rank == wide, packed, 0), axis=0, keepdims=True)
    slot_column = column(slots)
    upto = (slot_column <= wide).astype(jnp.int32) + (slot_column == wide).astype(jnp.int32) * 65536
    table[pl.ds(step_count + step, 1), :] = jnp.sum(upto, axis=0, keepdims=True)


def kernel(row_count, col_count, lists_ref, left_ref, right_ref, out_ref,
           left_all, right_all, lhs, rhs, sums, table, code_ref, zsend, zrecv, lsend, psend, hsend, lrecv, hrecv, local_sem):
    row = lax.axis_index("row")
    col = lax.axis_index("col")
    q_count = right_ref.shape[0]
    left_blocks, blk = left_ref.shape[2], left_ref.shape[3]
    right_blocks = right_ref.shape[3]
    step_count, pair_count = lists_ref.shape[1], lists_ref.shape[2]
    slot_count = out_ref.shape[0]
    groups = row_count // 2
    group, parity = row // 2, row % 2
    partner = group * 2 + 1 - parity
    square = groups == 4
    direct = (1, 2) if square else tuple(range(1, groups))

    def group_at(i):
        return (group // 2 * 2 + 1 - group % 2 if i == 1 else lax.rem(group + 2, groups)) if square and i in (1, 2) else (
            groups - 1 - group if square and i == 3 else lax.rem(group + i, groups))

    def row_at(i, same):
        return group_at(i) * 2 + (parity if same else 1 - parity)

    barrier = pltpu.get_barrier_semaphore()
    for i in direct:
        pl.semaphore_signal(barrier, inc=1, device_id=(row_at(i, True), col), device_id_type=MESH)
    pl.semaphore_signal(barrier, inc=1, device_id=(partner, col), device_id_type=MESH)

    @pl.when(col > 0)
    def _():
        pl.semaphore_signal(barrier, inc=1, device_id=(row, col - 1), device_id_type=MESH)

    @pl.when(col < col_count - 1)
    def _():
        pl.semaphore_signal(barrier, inc=1, device_id=(row, col + 1), device_id_type=MESH)

    own = [pltpu.make_async_copy(left_ref.at[0, 0], left_all.at[row], local_sem.at[0])]
    for q in range(q_count):
        own.append(pltpu.make_async_copy(right_ref.at[q, 0, 0], right_all.at[q, col], local_sem.at[1 + q]))
    for copy in own:
        copy.start()

    ends = (col == 0).astype(jnp.int32) + (col == col_count - 1).astype(jnp.int32)
    pl.semaphore_wait(barrier, len(direct) + 3 - ends)

    def along(direction, q, source, from_ref):
        return pltpu.make_async_remote_copy(
            src_ref=from_ref,
            dst_ref=right_all.at[q, source],
            send_sem=zsend.at[direction, q, source],
            recv_sem=zrecv.at[q, source],
            device_id=(row, col + (1 if direction else -1)),
            device_id_type=MESH,
        )

    def own_panel(direction, q):
        return along(direction, q, col, right_ref.at[q, 0, 0])

    def relayed(direction, q, source):
        return along(direction, q, source, right_all.at[q, source])

    def across(i):
        return pltpu.make_async_remote_copy(
            src_ref=left_ref.at[0, 0],
            dst_ref=left_all.at[row],
            send_sem=lsend.at[i],
            recv_sem=lrecv.at[row],
            device_id=(row_at(i, True), col),
            device_id_type=MESH,
        )

    def handed(i):
        source = row_at(i, True)
        return pltpu.make_async_remote_copy(
            src_ref=left_ref.at[0, 0] if i == 0 else left_all.at[source],
            dst_ref=left_all.at[source],
            send_sem=psend.at[i],
            recv_sem=lrecv.at[source],
            device_id=(partner, col),
            device_id_type=MESH,
        )

    def arrived_left(source):
        return pltpu.make_async_remote_copy(
            src_ref=left_all.at[source],
            dst_ref=left_all.at[source],
            send_sem=psend.at[0],
            recv_sem=lrecv.at[source],
            device_id=(partner, col),
            device_id_type=MESH,
        )

    half = left_blocks // 2
    pieces = (pl.ds(0, half), pl.ds(half, left_blocks - half))

    def half_of(i, piece, target):
        source = row_at(i, True)
        return pltpu.make_async_remote_copy(
            src_ref=left_all.at[source, pieces[piece]],
            dst_ref=left_all.at[source, pieces[piece]],
            send_sem=hsend.at[piece],
            recv_sem=hrecv.at[piece],
            device_id=(row_at(target, True), col),
            device_id_type=MESH,
        )

    for q in range(q_count):
        @pl.when(col > 0)
        def _():
            own_panel(0, q).start()

        @pl.when(col < col_count - 1)
        def _():
            own_panel(1, q).start()

    for i in direct:
        across(i).start()
    handed(0).start()

    lax.fori_loop(0, step_count, lambda step, c: (arrange(lists_ref, table, step, slot_count), c)[1], 0)
    out_ref[...] = jnp.zeros_like(out_ref)
    rhs[:, blk:, blk:] = jnp.zeros((right_blocks, blk, blk), rhs.dtype)
    for copy in own:
        copy.wait()

    sides = jnp.minimum(col, col_count - 1 - col)

    def item_of(item):
        rest = item - q_count
        later = rest - 2 * q_count * sides
        both = later < 0
        distance = jnp.where(both, rest // (2 * q_count) + 1, sides + 1 + later // q_count)
        q = jnp.where(both, rest % (2 * q_count) // 2, later % q_count)
        lower = jnp.where(both, rest % 2 == 0, col * 2 > col_count - 1)
        source = jnp.where(lower, col - distance, col + distance)
        own_item = rest < 0
        return jnp.where(own_item, col, source), jnp.where(own_item, item, q)

    def relay(item):
        source, q = item_of(item)

        @pl.when(source != col)
        def _():
            relayed(0, q, source).wait_recv()

        @pl.when((source < col) & (col < col_count - 1))
        def _():
            relayed(1, q, source).start()

        @pl.when((source > col) & (col > 0))
        def _():
            relayed(0, q, source).start()

    forwards = 1 - ends
    first = q_count * (2 + jnp.minimum(sides, 1))

    def relay_many(start, stop):
        lax.fori_loop(start, stop, lambda item, c: (relay(item), c)[1], 0)

    for i in direct:
        arrived_left(row_at(i, True)).wait_recv()
        if square:
            half_of(i, i - 1, 3 - i).start()
        handed(i).start()
    relay_many(q_count, first)
    listed = pltpu.make_async_copy(table, code_ref, local_sem.at[1 + q_count])
    listed.start()
    if square:
        half_of(3, 0, 1).wait_recv()
        half_of(3, 1, 1).wait_recv()
        handed(3).start()
    for i in range(groups):
        arrived_left(row_at(i, False)).wait_recv()
    listed.wait()

    def job(item, carry):
        source, q = item_of(item)
        kgroup = q * col_count + source
        step = lax.rem(kgroup - row - col + 2 * row_count, row_count)

        @pl.when(step < step_count)
        def _():
            def split_left(i, c):
                x = left_all[kgroup, i]
                high = x.astype(jnp.bfloat16)
                lhs[i, :, :blk] = high
                lhs[i, :, blk:] = (x - high.astype(jnp.float32)).astype(jnp.bfloat16)
                return c

            lax.fori_loop(0, left_blocks, split_left, 0)

        ahead = item + AHEAD * forwards

        @pl.when((ahead >= first) & (ahead < row_count))
        def _():
            relay(ahead)

        @pl.when(step < step_count)
        def _():
            def split_right(i, c):
                x = right_all[q, source, i]
                high = x.astype(jnp.bfloat16)
                rhs[i, :blk, :blk] = high
                rhs[i, blk:, :blk] = high
                rhs[i, :blk, blk:] = (x - high.astype(jnp.float32)).astype(jnp.bfloat16)
                return c

            lax.fori_loop(0, right_blocks, split_right, 0)

            def some(batch, carry):
                total, before = carry
                for u in range(UNROLL):
                    p = batch * UNROLL + u
                    code = code_ref[step, p]
                    both = jnp.dot(
                        lhs[code & 255], rhs[(code >> 8) & 255], preferred_element_type=jnp.float32
                    )
                    slot = code >> 16
                    keep = (slot == before).astype(jnp.float32)
                    total = total * keep + (both[:, :blk] + both[:, blk:])
                    sums[p] = total
                    before = slot
                return total, before

            lax.fori_loop(0, pair_count // UNROLL, some, (jnp.zeros((blk, blk), jnp.float32), jnp.int32(-1)))

            def put(o, c):
                code = code_ref[step_count + step, o]
                found = ((code >> 16) > 0).astype(jnp.float32)
                out_ref[o] = out_ref[o] + sums[jnp.maximum((code & 65535) - 1, 0)] * found
                return c

            lax.fori_loop(0, slot_count, put, 0)

        return carry

    lax.fori_loop(0, row_count, job, 0)

    for q in range(q_count):
        @pl.when(col > 0)
        def _():
            own_panel(0, q).wait_send()

        @pl.when(col < col_count - 1)
        def _():
            own_panel(1, q).wait_send()

    def sent(item, carry):
        source, q = item_of(item)

        @pl.when((source < col) & (col < col_count - 1))
        def _():
            relayed(1, q, source).wait_send()

        @pl.when((source > col) & (col > 0))
        def _():
            relayed(0, q, source).wait_send()

        return carry

    lax.fori_loop(q_count, row_count, sent, 0)
    for i in direct:
        across(i).wait_send()
    if square:
        half_of(1, 0, 2).wait_send()
        half_of(2, 1, 1).wait_send()
    for i in range(groups):
        handed(i).wait_send()


def fold_kernel(row_count, col_count, lists_in, left_ref, right_ref, out_ref,
                left_all, right_all, lhs, rhs, sums, acc, table, table_in, code_ref,
                zsend, zrecv, lsend, psend, hsend, lrecv, precv, hrecv, esend, erecv, ehrecv, tsem, ssend, srecv, local_sem, turn_sem, lists_ref):
    row = lax.axis_index("row")
    col = lax.axis_index("col")
    q_count = right_ref.shape[0]
    left_blocks, blk = left_ref.shape[2], left_ref.shape[3]
    right_blocks = right_ref.shape[3]
    step_count, pair_count = lists_in.shape[1], lists_in.shape[2]
    slot_count = out_ref.shape[0]
    groups = row_count // 2
    group, parity = row // 2, row % 2
    partner = group * 2 + 1 - parity
    low = col * 2 < col_count
    at_end = (col == 0) | (col == col_count - 1)
    even = parity == 0
    odd = parity == 1
    inward = jnp.where(low, col + 1, col - 1)
    outward = jnp.where(low, col - 1, col + 1)
    near = jnp.where(low, 0, col_count - 1)

    def source_of(place):
        return jnp.where(low, place, col_count - 1 - place)

    def group_at(i):
        return (group, group // 2 * 2 + 1 - group % 2, lax.rem(group + 2, groups), groups - 1 - group)[i]

    def row_at(i, same):
        return group_at(i) * 2 + (parity if same else 1 - parity)

    barrier = pltpu.get_barrier_semaphore()
    for i in (1, 2):
        pl.semaphore_signal(barrier, inc=1, device_id=(row_at(i, True), col), device_id_type=MESH)
    pl.semaphore_signal(barrier, inc=1, device_id=(partner, col), device_id_type=MESH)
    pl.semaphore_signal(barrier, inc=1, device_id=(row, inward), device_id_type=MESH)

    @pl.when(jnp.logical_not(at_end))
    def _():
        pl.semaphore_signal(barrier, inc=1, device_id=(row, outward), device_id_type=MESH)

    own = [pltpu.make_async_copy(left_ref.at[0, 0], left_all.at[row], local_sem.at[0])]
    for q in range(q_count):
        own.append(pltpu.make_async_copy(right_ref.at[q, 0, 0], right_all.at[q, col], local_sem.at[1 + q]))
    for copy in own:
        copy.start()
    entries = pltpu.make_async_copy(lists_in, lists_ref, local_sem.at[3 + q_count])
    entries.start()
    pl.semaphore_wait(barrier, jnp.where(at_end, 4, 5))

    def panel(direction, q, source, from_ref):
        return pltpu.make_async_remote_copy(
            src_ref=from_ref,
            dst_ref=right_all.at[q, source],
            send_sem=zsend.at[direction, q, source],
            recv_sem=zrecv.at[q, source],
            device_id=(row, inward if direction else outward),
            device_id_type=MESH,
        )

    def own_panel(direction, q):
        return panel(direction, q, col, right_ref.at[q, 0, 0])

    def relayed(direction, q, source):
        return panel(direction, q, source, right_all.at[q, source])

    def left_copy(source_ref, index, send_sem, recv_sem, device):
        return pltpu.make_async_remote_copy(
            src_ref=source_ref,
            dst_ref=left_all.at[index],
            send_sem=send_sem,
            recv_sem=recv_sem,
            device_id=device,
            device_id_type=MESH,
        )

    def handed(i):
        source = row_at(i, True)
        return left_copy(left_ref.at[0, 0] if i == 0 else left_all.at[source], source,
                         psend.at[i], lrecv.at[source], (partner, col))

    def arrived_left(source):
        return left_copy(left_all.at[source], source, psend.at[0], lrecv.at[source], (partner, col))

    half = left_blocks // 2
    pieces = (pl.ds(0, half), pl.ds(half, left_blocks - half))

    def across(i, piece):
        return pltpu.make_async_remote_copy(
            src_ref=left_ref.at[0, 0, pieces[piece]],
            dst_ref=left_all.at[row, pieces[piece]],
            send_sem=lsend.at[i - 1, piece],
            recv_sem=precv.at[i - 1, piece],
            device_id=(row_at(i, True), col),
            device_id_type=MESH,
        )

    def half_copy(index, piece, send_sem, recv_sem, target):
        return pltpu.make_async_remote_copy(
            src_ref=left_all.at[index, pieces[piece]],
            dst_ref=left_all.at[index, pieces[piece]],
            send_sem=send_sem,
            recv_sem=recv_sem,
            device_id=(row_at(target, True), col),
            device_id_type=MESH,
        )

    def half_of(i, piece, target):
        return half_copy(row_at(i, True), piece, hsend.at[piece], hrecv.at[piece], target)

    lent = row + (col == 0).astype(jnp.int32)

    def extra_out():
        return left_copy(left_all.at[lent], row_count + group, esend.at[0], erecv.at[0], (row, inward))

    def extra_arrived():
        index = row_count + group
        return left_copy(left_all.at[index], index, esend.at[0], erecv.at[0], (row_at(1, True), col))

    def extra_across(i, piece):
        return half_copy(row_count + group, piece, esend.at[2 * i + piece - 1], erecv.at[2 * i + piece - 1], i)

    def extra_half(i, piece, target):
        return half_copy(row_count + group_at(i), piece, esend.at[5 + piece], ehrecv.at[piece], target)

    def table_out():
        return pltpu.make_async_remote_copy(
            src_ref=table,
            dst_ref=table_in,
            send_sem=tsem.at[0],
            recv_sem=tsem.at[1],
            device_id=(row, inward),
            device_id_type=MESH,
        )

    part = slot_count // PARTS

    def partial_sum(i):
        where = pl.ds(slot_count + i * part, part)
        return pltpu.make_async_remote_copy(
            src_ref=acc.at[where],
            dst_ref=acc.at[where],
            send_sem=ssend.at[i],
            recv_sem=srecv.at[i],
            device_id=(row, near),
            device_id_type=MESH,
        )

    inner = jnp.logical_not(at_end)
    folding = inner & even
    folded = at_end & even

    @pl.when(inner & odd)
    def _():
        for q in range(q_count):
            own_panel(0, q).start()

    @pl.when(inner)
    def _():
        for q in range(q_count):
            own_panel(1, q).start()

    handed(0).start()
    for piece in range(2):
        for i in (1, 2):
            across(i, (i - 1 + piece) % 2).start()
    for copy in own:
        copy.wait()
    arrived_left(partner).wait_recv()

    @pl.when(folded)
    def _():
        extra_out().start()

    entries.wait()
    lax.fori_loop(0, step_count, lambda step, c: (arrange(lists_ref, table, step, slot_count), c)[1], 0)

    @pl.when(folded)
    def _():
        table_out().start()
        extra_out().wait_send()
        for q in range(q_count):
            own_panel(1, q).start()
        pl.semaphore_signal(turn_sem, inc=1, device_id=(partner, col), device_id_type=MESH)

    @pl.when(at_end & odd)
    def _():
        pl.semaphore_wait(turn_sem, 1)
        own_panel(1, 0).start()

    listed = pltpu.make_async_copy(table, code_ref.at[pl.ds(0, 2 * step_count)], local_sem.at[1 + q_count])
    listed.start()
    zero = jnp.zeros((blk, blk), jnp.float32)

    def clear(o, c):
        acc[o] = zero
        return c

    lax.fori_loop(0, jnp.where(folding, 2 * slot_count, slot_count), clear, 0)
    rhs[:, blk:, blk:] = jnp.zeros((right_blocks, blk, blk), rhs.dtype)

    def receive(place, q):
        relayed(0, q, source_of(place)).wait_recv()

    def receive_inner(place, q):
        receive(place, q)
        if place == 0:
            relayed(1, q, source_of(place)).start()
        elif place == 2:
            relayed(0, q, source_of(place)).start()
        else:
            @pl.when(odd)
            def _():
                relayed(0, q, source_of(place)).start()

    for i in (1, 2):
        across(i, i - 1).wait_recv()
        half_of(i, i - 1, 3 - i).start()

    @pl.when(folding)
    def _():
        extra_arrived().wait_recv()
        for piece in range(2):
            for i in (1, 2):
                extra_across(i, (i - 1 + piece) % 2).start()

    @pl.when(inner)
    def _():
        receive_inner(2, 0)

    for i in (1, 2):
        across(i, 2 - i).wait_recv()
        handed(i).start()

    for i in (1, 2):
        arrived_left(row_at(i, False)).wait_recv()
    listed.wait()

    def rest_of_left():
        @pl.when(inner & odd)
        def _():
            receive_inner(0, 0)

        @pl.when(inner)
        def _():
            receive_inner(2, 1)

        @pl.when(folding)
        def _():
            receive_inner(0, 0)

        half_of(3, 0, 1).wait_recv()
        half_of(3, 1, 1).wait_recv()
        handed(3).start()

        @pl.when(folding)
        def _():
            for i in (1, 2):
                extra_across(i, i - 1).wait_recv()
                extra_half(i, i - 1, 3 - i).start()
            table_out().wait_recv()
            fetched = pltpu.make_async_copy(table_in, code_ref.at[pl.ds(2 * step_count, 2 * step_count)], local_sem.at[2 + q_count])
            fetched.start()
            fetched.wait()

        arrived_left(row_at(3, False)).wait_recv()

        @pl.when(folding)
        def _():
            receive_inner(0, 1)
            for i in (1, 2):
                extra_across(i, 2 - i).wait_recv()

    late = [(q * col_count + source_of(1)) // 2 == group_at(3) for q in range(2)]
    head = (jnp.where(late[0], 5, 1), jnp.where(late[0] | late[1], 2, 5), jnp.where(late[0], 1, jnp.where(late[1], 5, 2)))
    lent_head = (
        jnp.where(late[0], 13, 9),
        jnp.where(late[0] | late[1], 11, 13),
        jnp.where(late[0], 9, jnp.where(late[1], 13, 11)),
    )

    def job(item, carry):
        def pick(choices):
            value = jnp.int32(choices[-1])
            for at in range(len(choices) - 1):
                value = jnp.where(item == at, choices[at], value)
            return value

        code = jnp.where(
            at_end,
            jnp.where(even, pick(END_EVEN), pick(END_ODD)),
            jnp.where(even, pick(head[:2] + lent_head + INNER_EVEN[:1] + head[2:] + INNER_EVEN[1:]), pick(head + INNER_ODD)),
        )
        place, q, extra = code % 4, code // 4 % 2, code // 8
        source = source_of(place)
        kgroup = q * col_count + source
        owner = jnp.where(extra == 1, near, col)
        step = lax.rem(kgroup - row - owner + 2 * row_count, row_count)
        code_row = step + extra * 2 * step_count
        left_at = jnp.where(extra == 1, row_count + kgroup // 2, kgroup)
        base = extra * slot_count

        @pl.when(at_end & odd & (item == 1))
        def _():
            own_panel(1, 1).start()

        @pl.when(at_end & (place > 0))
        def _():
            relayed(0, q, source).wait_recv()

        pl.when(item == jnp.where(inner, 2, 0))(rest_of_left)

        @pl.when(inner & odd & (item == 5))
        def _():
            receive_inner(0, 1)

        @pl.when(folding & (item == 4))
        def _():
            extra_half(3, 0, 1).wait_recv()
            extra_half(3, 1, 1).wait_recv()

        for turn in range(2):
            @pl.when(inner & (item == jnp.where(even, 3 + 2 * turn, 3 + 4 * turn)))
            def _():
                receive_inner(3, turn)

        def split_left(i, c):
            x = left_all[left_at, i]
            high = x.astype(jnp.bfloat16)
            lhs[i, :, :blk] = high
            lhs[i, :, blk:] = (x - high.astype(jnp.float32)).astype(jnp.bfloat16)
            return c

        lax.fori_loop(0, left_blocks, split_left, 0)

        def split_right(i, c):
            x = right_all[q, source, i]
            high = x.astype(jnp.bfloat16)
            rhs[i, :blk, :blk] = high
            rhs[i, blk:, :blk] = high
            rhs[i, :blk, blk:] = (x - high.astype(jnp.float32)).astype(jnp.bfloat16)
            return c

        lax.fori_loop(0, right_blocks, split_right, 0)

        def some(batch, carry):
            total, before = carry
            for u in range(UNROLL):
                p = batch * UNROLL + u
                entry = code_ref[code_row, p]
                both = jnp.dot(lhs[entry & 255], rhs[(entry >> 8) & 255], preferred_element_type=jnp.float32)
                slot = entry >> 16
                keep = (slot == before).astype(jnp.float32)
                total = total * keep + (both[:, :blk] + both[:, blk:])
                sums[p] = total
                before = slot
            return total, before

        lax.fori_loop(0, pair_count // UNROLL, some, (zero, jnp.int32(-1)))

        def put(o, c):
            entry = code_ref[step_count + code_row, o]
            found = ((entry >> 16) > 0).astype(jnp.float32)
            acc[base + o] = acc[base + o] + sums[jnp.maximum((entry & 65535) - 1, 0)] * found
            return c

        lax.fori_loop(0, slot_count, put, 0)

        @pl.when(folding & (item == 5))
        def _():
            for i in range(PARTS):
                partial_sum(i).start()

        return carry

    job_count = jnp.where(
        at_end,
        jnp.where(even, len(END_EVEN), len(END_ODD)),
        jnp.where(even, 6 + len(INNER_EVEN), 3 + len(INNER_ODD)),
    )
    lax.fori_loop(0, job_count, job, 0)

    @pl.when(folded)
    def _():
        for i in range(PARTS):
            partial_sum(i).wait_recv()

            def add(o, c):
                out_ref[o] = acc[o] + acc[slot_count + o]
                return c

            lax.fori_loop(i * part, (i + 1) * part, add, 0)

    @pl.when(jnp.logical_not(folded))
    def _():
        def move(o, c):
            out_ref[o] = acc[o]
            return c

        lax.fori_loop(0, slot_count, move, 0)

    for q in range(q_count):
        own_panel(1, q).wait_send()

    @pl.when(inner)
    def _():
        for q in range(q_count):
            relayed(1, q, source_of(0)).wait_send()
            relayed(0, q, source_of(2)).wait_send()

    @pl.when(inner & odd)
    def _():
        for q in range(q_count):
            own_panel(0, q).wait_send()
            relayed(0, q, source_of(3)).wait_send()

    @pl.when(folded)
    def _():
        table_out().wait_send()

    @pl.when(folding)
    def _():
        for i in (1, 2):
            for piece in range(2):
                extra_across(i, piece).wait_send()
        extra_half(1, 0, 2).wait_send()
        extra_half(2, 1, 1).wait_send()
        for i in range(PARTS):
            partial_sum(i).wait_send()

    for i in (1, 2):
        for piece in range(2):
            across(i, piece).wait_send()
    half_of(1, 0, 2).wait_send()
    half_of(2, 1, 1).wait_send()
    for i in range(groups):
        handed(i).wait_send()


def folded_call(row_count, col_count, lists, left_panels, right_panels, width):
    left_blocks, blk = left_panels.shape[2], left_panels.shape[3]
    q_count, right_blocks = right_panels.shape[0], right_panels.shape[3]
    step_count, pair_count = lists.shape[1], lists.shape[2]
    groups = row_count // 2
    dma = pltpu.SemaphoreType.DMA
    out = pl.pallas_call(
        functools.partial(fold_kernel, row_count, col_count),
        out_shape=jax.ShapeDtypeStruct((OCAP, blk, blk), jnp.float32),
        in_specs=[pl.BlockSpec(memory_space=pltpu.HBM)] * 3,
        out_specs=pl.BlockSpec(memory_space=pltpu.VMEM),
        scratch_shapes=[
            pltpu.VMEM((row_count + groups, left_blocks, blk, blk), jnp.float32),
            pltpu.VMEM((q_count, col_count, right_blocks, blk, blk), jnp.float32),
            pltpu.VMEM((left_blocks, blk, 2 * blk), jnp.bfloat16),
            pltpu.VMEM((right_blocks, 2 * blk, 2 * blk), jnp.bfloat16),
            pltpu.VMEM((pair_count, blk, blk), jnp.float32),
            pltpu.VMEM((2 * OCAP, blk, blk), jnp.float32),
            pltpu.VMEM((2 * step_count, width), jnp.int32),
            pltpu.VMEM((2 * step_count, width), jnp.int32),
            pltpu.SMEM((4 * step_count, width), jnp.int32),
            dma((2, q_count, col_count)),
            dma((q_count, col_count)),
            dma((2, 2)),
            dma((groups,)),
            dma((2,)),
            dma((row_count,)),
            dma((2, 2)),
            dma((2,)),
            dma((7,)),
            dma((5,)),
            dma((2,)),
            dma((2,)),
            dma((PARTS,)),
            dma((PARTS,)),
            dma((4 + q_count,)),
            pltpu.SemaphoreType.REGULAR,
            pltpu.VMEM(lists.shape, jnp.int32),
        ],
        compiler_params=pltpu.CompilerParams(
            collective_id=0, has_side_effects=True, vmem_limit_bytes=60 * 1024 * 1024
        ),
    )(lists, left_panels, right_panels)
    return out[None, None]


def shards(row_count, col_count, left_panels, right_panels, product_lists):
    left_blocks, blk = left_panels.shape[2], left_panels.shape[3]
    q_count, right_blocks = right_panels.shape[0], right_panels.shape[3]
    pair_count = product_lists.shape[3]
    lists = jnp.transpose(product_lists[0, 0], (2, 0, 1))
    step_count = lists.shape[1]
    width = pl.cdiv(max(pair_count, OCAP), 128) * 128
    groups = row_count // 2
    if groups == 4 and col_count == 4 and q_count * col_count == row_count == step_count and OCAP % PARTS == 0:
        return folded_call(row_count, col_count, lists, left_panels, right_panels, width)
    out = pl.pallas_call(
        functools.partial(kernel, row_count, col_count),
        out_shape=jax.ShapeDtypeStruct((OCAP, blk, blk), jnp.float32),
        in_specs=[pl.BlockSpec(memory_space=pltpu.VMEM)] + [pl.BlockSpec(memory_space=pltpu.HBM)] * 2,
        out_specs=pl.BlockSpec(memory_space=pltpu.VMEM),
        scratch_shapes=[
            pltpu.VMEM((row_count, left_blocks, blk, blk), jnp.float32),
            pltpu.VMEM((q_count, col_count, right_blocks, blk, blk), jnp.float32),
            pltpu.VMEM((left_blocks, blk, 2 * blk), jnp.bfloat16),
            pltpu.VMEM((right_blocks, 2 * blk, 2 * blk), jnp.bfloat16),
            pltpu.VMEM((pair_count, blk, blk), jnp.float32),
            pltpu.VMEM((2 * step_count, width), jnp.int32),
            pltpu.SMEM((2 * step_count, width), jnp.int32),
            pltpu.SemaphoreType.DMA((2, q_count, col_count)),
            pltpu.SemaphoreType.DMA((q_count, col_count)),
            pltpu.SemaphoreType.DMA((groups,)),
            pltpu.SemaphoreType.DMA((groups,)),
            pltpu.SemaphoreType.DMA((2,)),
            pltpu.SemaphoreType.DMA((row_count,)),
            pltpu.SemaphoreType.DMA((2,)),
            pltpu.SemaphoreType.DMA((2 + q_count,)),
        ],
        compiler_params=pltpu.CompilerParams(
            collective_id=0, has_side_effects=True, vmem_limit_bytes=50 * 1024 * 1024
        ),
    )(lists, left_panels, right_panels)
    return out[None, None]


def solution(mesh):
    return jax.shard_map(
        functools.partial(shards, mesh.shape["row"], mesh.shape["col"]),
        mesh=mesh,
        in_specs=(
            P("row", "col", None, None, None),
            P(None, "col", "row", None, None, None),
            P("row", "col", None, None, None),
        ),
        out_specs=P("row", "col", None, None, None),
        check_vma=False,
    )
```

```python
import functools

import jax
import jax.numpy as jnp
from jax import lax
from jax.experimental import pallas as pl
from jax.experimental.pallas import tpu as pltpu
from jax.sharding import PartitionSpec as P

OCAP = 24
UNROLL = 16
AHEAD = 3
MESH = pl.DeviceIdType.MESH
PARTS = 4
END_JOBS = (0, 4, 1, 5, 2, 6, 3, 7)
INNER_ODD = (6, 0, 3, 4, 7)


def arrange(lists_ref, table, step, slot_count):
    step_count, count = lists_ref.shape[1], lists_ref.shape[2]
    width = table.shape[1]
    left, right, out = (lists_ref[part, pl.ds(step, 1), :] for part in range(3))
    live = left >= 0
    slots = jnp.where(live, out, slot_count)
    lane = lax.broadcasted_iota(jnp.int32, (count, count), 1)
    same = lax.broadcasted_iota(jnp.int32, (count, count), 0) == lane

    def column(row):
        return jnp.sum(jnp.where(same, jnp.broadcast_to(row, (count, count)), 0), axis=1, keepdims=True)

    key = jnp.broadcast_to(slots, (count, count)) * count + lane
    key_column = jnp.sum(jnp.where(same, key, 0), axis=1, keepdims=True)
    rank = jnp.sum((key < key_column).astype(jnp.int32), axis=1, keepdims=True)
    packed = column(jnp.where(live, left + right * 256, 0) + slots * 65536)
    wide = lax.broadcasted_iota(jnp.int32, (count, width), 1)
    table[pl.ds(step, 1), :] = jnp.sum(jnp.where(rank == wide, packed, 0), axis=0, keepdims=True)
    slot_column = column(slots)
    upto = (slot_column <= wide).astype(jnp.int32) + (slot_column == wide).astype(jnp.int32) * 65536
    table[pl.ds(step_count + step, 1), :] = jnp.sum(upto, axis=0, keepdims=True)


def kernel(row_count, col_count, lists_ref, left_ref, right_ref, out_ref,
           left_all, right_all, lhs, rhs, sums, table, code_ref, zsend, zrecv, lsend, psend, hsend, lrecv, hrecv, local_sem):
    row = lax.axis_index("row")
    col = lax.axis_index("col")
    q_count = right_ref.shape[0]
    left_blocks, blk = left_ref.shape[2], left_ref.shape[3]
    right_blocks = right_ref.shape[3]
    step_count, pair_count = lists_ref.shape[1], lists_ref.shape[2]
    slot_count = out_ref.shape[0]
    groups = row_count // 2
    group, parity = row // 2, row % 2
    partner = group * 2 + 1 - parity
    square = groups == 4
    direct = (1, 2) if square else tuple(range(1, groups))

    def group_at(i):
        return (group // 2 * 2 + 1 - group % 2 if i == 1 else lax.rem(group + 2, groups)) if square and i in (1, 2) else (
            groups - 1 - group if square and i == 3 else lax.rem(group + i, groups))

    def row_at(i, same):
        return group_at(i) * 2 + (parity if same else 1 - parity)

    barrier = pltpu.get_barrier_semaphore()
    for i in direct:
        pl.semaphore_signal(barrier, inc=1, device_id=(row_at(i, True), col), device_id_type=MESH)
    pl.semaphore_signal(barrier, inc=1, device_id=(partner, col), device_id_type=MESH)

    @pl.when(col > 0)
    def _():
        pl.semaphore_signal(barrier, inc=1, device_id=(row, col - 1), device_id_type=MESH)

    @pl.when(col < col_count - 1)
    def _():
        pl.semaphore_signal(barrier, inc=1, device_id=(row, col + 1), device_id_type=MESH)

    own = [pltpu.make_async_copy(left_ref.at[0, 0], left_all.at[row], local_sem.at[0])]
    for q in range(q_count):
        own.append(pltpu.make_async_copy(right_ref.at[q, 0, 0], right_all.at[q, col], local_sem.at[1 + q]))
    for copy in own:
        copy.start()

    ends = (col == 0).astype(jnp.int32) + (col == col_count - 1).astype(jnp.int32)
    pl.semaphore_wait(barrier, len(direct) + 3 - ends)

    def along(direction, q, source, from_ref):
        return pltpu.make_async_remote_copy(
            src_ref=from_ref,
            dst_ref=right_all.at[q, source],
            send_sem=zsend.at[direction, q, source],
            recv_sem=zrecv.at[q, source],
            device_id=(row, col + (1 if direction else -1)),
            device_id_type=MESH,
        )

    def own_panel(direction, q):
        return along(direction, q, col, right_ref.at[q, 0, 0])

    def relayed(direction, q, source):
        return along(direction, q, source, right_all.at[q, source])

    def across(i):
        return pltpu.make_async_remote_copy(
            src_ref=left_ref.at[0, 0],
            dst_ref=left_all.at[row],
            send_sem=lsend.at[i],
            recv_sem=lrecv.at[row],
            device_id=(row_at(i, True), col),
            device_id_type=MESH,
        )

    def handed(i):
        source = row_at(i, True)
        return pltpu.make_async_remote_copy(
            src_ref=left_ref.at[0, 0] if i == 0 else left_all.at[source],
            dst_ref=left_all.at[source],
            send_sem=psend.at[i],
            recv_sem=lrecv.at[source],
            device_id=(partner, col),
            device_id_type=MESH,
        )

    def arrived_left(source):
        return pltpu.make_async_remote_copy(
            src_ref=left_all.at[source],
            dst_ref=left_all.at[source],
            send_sem=psend.at[0],
            recv_sem=lrecv.at[source],
            device_id=(partner, col),
            device_id_type=MESH,
        )

    half = left_blocks // 2
    pieces = (pl.ds(0, half), pl.ds(half, left_blocks - half))

    def half_of(i, piece, target):
        source = row_at(i, True)
        return pltpu.make_async_remote_copy(
            src_ref=left_all.at[source, pieces[piece]],
            dst_ref=left_all.at[source, pieces[piece]],
            send_sem=hsend.at[piece],
            recv_sem=hrecv.at[piece],
            device_id=(row_at(target, True), col),
            device_id_type=MESH,
        )

    for q in range(q_count):
        @pl.when(col > 0)
        def _():
            own_panel(0, q).start()

        @pl.when(col < col_count - 1)
        def _():
            own_panel(1, q).start()

    for i in direct:
        across(i).start()
    handed(0).start()

    lax.fori_loop(0, step_count, lambda step, c: (arrange(lists_ref, table, step, slot_count), c)[1], 0)
    out_ref[...] = jnp.zeros_like(out_ref)
    rhs[:, blk:, blk:] = jnp.zeros((right_blocks, blk, blk), rhs.dtype)
    for copy in own:
        copy.wait()

    sides = jnp.minimum(col, col_count - 1 - col)

    def item_of(item):
        rest = item - q_count
        later = rest - 2 * q_count * sides
        both = later < 0
        distance = jnp.where(both, rest // (2 * q_count) + 1, sides + 1 + later // q_count)
        q = jnp.where(both, rest % (2 * q_count) // 2, later % q_count)
        lower = jnp.where(both, rest % 2 == 0, col * 2 > col_count - 1)
        source = jnp.where(lower, col - distance, col + distance)
        own_item = rest < 0
        return jnp.where(own_item, col, source), jnp.where(own_item, item, q)

    def relay(item):
        source, q = item_of(item)

        @pl.when(source != col)
        def _():
            relayed(0, q, source).wait_recv()

        @pl.when((source < col) & (col < col_count - 1))
        def _():
            relayed(1, q, source).start()

        @pl.when((source > col) & (col > 0))
        def _():
            relayed(0, q, source).start()

    forwards = 1 - ends
    first = q_count * (2 + jnp.minimum(sides, 1))

    def relay_many(start, stop):
        lax.fori_loop(start, stop, lambda item, c: (relay(item), c)[1], 0)

    for i in direct:
        arrived_left(row_at(i, True)).wait_recv()
        if square:
            half_of(i, i - 1, 3 - i).start()
        handed(i).start()
    relay_many(q_count, first)
    listed = pltpu.make_async_copy(table, code_ref, local_sem.at[1 + q_count])
    listed.start()
    if square:
        half_of(3, 0, 1).wait_recv()
        half_of(3, 1, 1).wait_recv()
        handed(3).start()
    for i in range(groups):
        arrived_left(row_at(i, False)).wait_recv()
    listed.wait()

    def job(item, carry):
        source, q = item_of(item)
        kgroup = q * col_count + source
        step = lax.rem(kgroup - row - col + 2 * row_count, row_count)

        @pl.when(step < step_count)
        def _():
            def split_left(i, c):
                x = left_all[kgroup, i]
                high = x.astype(jnp.bfloat16)
                lhs[i, :, :blk] = high
                lhs[i, :, blk:] = (x - high.astype(jnp.float32)).astype(jnp.bfloat16)
                return c

            lax.fori_loop(0, left_blocks, split_left, 0)

        ahead = item + AHEAD * forwards

        @pl.when((ahead >= first) & (ahead < row_count))
        def _():
            relay(ahead)

        @pl.when(step < step_count)
        def _():
            def split_right(i, c):
                x = right_all[q, source, i]
                high = x.astype(jnp.bfloat16)
                rhs[i, :blk, :blk] = high
                rhs[i, blk:, :blk] = high
                rhs[i, :blk, blk:] = (x - high.astype(jnp.float32)).astype(jnp.bfloat16)
                return c

            lax.fori_loop(0, right_blocks, split_right, 0)

            def some(batch, carry):
                total, before = carry
                for u in range(UNROLL):
                    p = batch * UNROLL + u
                    code = code_ref[step, p]
                    both = jnp.dot(
                        lhs[code & 255], rhs[(code >> 8) & 255], preferred_element_type=jnp.float32
                    )
                    slot = code >> 16
                    keep = (slot == before).astype(jnp.float32)
                    total = total * keep + (both[:, :blk] + both[:, blk:])
                    sums[p] = total
                    before = slot
                return total, before

            lax.fori_loop(0, pair_count // UNROLL, some, (jnp.zeros((blk, blk), jnp.float32), jnp.int32(-1)))

            def put(o, c):
                code = code_ref[step_count + step, o]
                found = ((code >> 16) > 0).astype(jnp.float32)
                out_ref[o] = out_ref[o] + sums[jnp.maximum((code & 65535) - 1, 0)] * found
                return c

            lax.fori_loop(0, slot_count, put, 0)

        return carry

    lax.fori_loop(0, row_count, job, 0)

    for q in range(q_count):
        @pl.when(col > 0)
        def _():
            own_panel(0, q).wait_send()

        @pl.when(col < col_count - 1)
        def _():
            own_panel(1, q).wait_send()

    def sent(item, carry):
        source, q = item_of(item)

        @pl.when((source < col) & (col < col_count - 1))
        def _():
            relayed(1, q, source).wait_send()

        @pl.when((source > col) & (col > 0))
        def _():
            relayed(0, q, source).wait_send()

        return carry

    lax.fori_loop(q_count, row_count, sent, 0)
    for i in direct:
        across(i).wait_send()
    if square:
        half_of(1, 0, 2).wait_send()
        half_of(2, 1, 1).wait_send()
    for i in range(groups):
        handed(i).wait_send()


def batched(count, body, most=4):
    width = next(w for w in range(most, 0, -1) if count % w == 0)

    def batch(i, c):
        for u in range(width):
            body(i * width + u)
        return c

    lax.fori_loop(0, count // width, batch, 0)


def fold_kernel(row_count, col_count, lists_in, left_ref, right_ref, out_ref,
                left_all, right_all, packed, total_in, lhs, rhs, sums, acc, table, table_in, code_ref,
                zsend, zrecv, lsend, psend, hsend, lrecv, precv, hrecv, esend, erecv, ehrecv, bsend, brecv, tsem, ssend, srecv, local_sem, lists_ref):
    row = lax.axis_index("row")
    col = lax.axis_index("col")
    q_count = right_ref.shape[0]
    left_blocks, blk = left_ref.shape[2], left_ref.shape[3]
    right_blocks = right_ref.shape[3]
    step_count, pair_count = lists_in.shape[1], lists_in.shape[2]
    slot_count = out_ref.shape[0]
    groups = row_count // 2
    group, parity = row // 2, row % 2
    partner = group * 2 + 1 - parity
    low = col * 2 < col_count
    at_end = (col == 0) | (col == col_count - 1)
    even = parity == 0
    odd = parity == 1
    inward = jnp.where(low, col + 1, col - 1)
    outward = jnp.where(low, col - 1, col + 1)
    near = jnp.where(low, 0, col_count - 1)

    def source_of(place):
        return jnp.where(low, place, col_count - 1 - place)

    def group_at(i):
        return (group, group // 2 * 2 + 1 - group % 2, lax.rem(group + 2, groups), groups - 1 - group)[i]

    def row_at(i, same):
        return group_at(i) * 2 + (parity if same else 1 - parity)

    barrier = pltpu.get_barrier_semaphore()
    for i in (1, 2):
        pl.semaphore_signal(barrier, inc=1, device_id=(row_at(i, True), col), device_id_type=MESH)
    pl.semaphore_signal(barrier, inc=1, device_id=(partner, col), device_id_type=MESH)
    pl.semaphore_signal(barrier, inc=1, device_id=(row, inward), device_id_type=MESH)

    @pl.when(jnp.logical_not(at_end))
    def _():
        pl.semaphore_signal(barrier, inc=1, device_id=(row, outward), device_id_type=MESH)

    @pl.when((col == 1) & even)
    def _():
        pl.semaphore_signal(barrier, inc=1, device_id=(row + 1, 0), device_id_type=MESH)

    own = [pltpu.make_async_copy(left_ref.at[0, 0], left_all.at[row], local_sem.at[0])]
    for q in range(q_count):
        own.append(pltpu.make_async_copy(right_ref.at[q, 0, 0], right_all.at[q, col], local_sem.at[1 + q]))
    for copy in own:
        copy.start()
    entries = pltpu.make_async_copy(lists_in, lists_ref, local_sem.at[3 + q_count])
    entries.start()
    pl.semaphore_wait(barrier, jnp.where(at_end & ((col > 0) | even), 4, 5))

    def panel(direction, q, source, from_ref):
        return pltpu.make_async_remote_copy(
            src_ref=from_ref,
            dst_ref=right_all.at[q, source],
            send_sem=zsend.at[direction, q, source],
            recv_sem=zrecv.at[q, source],
            device_id=(row, inward if direction else outward),
            device_id_type=MESH,
        )

    def own_panel(direction, q):
        return panel(direction, q, col, right_ref.at[q, 0, 0])

    def relayed(direction, q, source):
        return panel(direction, q, source, right_all.at[q, source])

    def left_copy(source_ref, index, send_sem, recv_sem, device):
        return pltpu.make_async_remote_copy(
            src_ref=source_ref,
            dst_ref=left_all.at[index],
            send_sem=send_sem,
            recv_sem=recv_sem,
            device_id=device,
            device_id_type=MESH,
        )

    def handed(i):
        source = row_at(i, True)
        return left_copy(left_ref.at[0, 0] if i == 0 else left_all.at[source], source,
                         psend.at[i], lrecv.at[source], (partner, col))

    def arrived_left(source):
        return left_copy(left_all.at[source], source, psend.at[0], lrecv.at[source], (partner, col))

    half = left_blocks // 2
    pieces = (pl.ds(0, half), pl.ds(half, left_blocks - half))

    def across(i, piece):
        return pltpu.make_async_remote_copy(
            src_ref=left_ref.at[0, 0, pieces[piece]],
            dst_ref=left_all.at[row, pieces[piece]],
            send_sem=lsend.at[i - 1, piece],
            recv_sem=precv.at[i - 1, piece],
            device_id=(row_at(i, True), col),
            device_id_type=MESH,
        )

    def half_copy(index, piece, send_sem, recv_sem, target):
        return pltpu.make_async_remote_copy(
            src_ref=left_all.at[index, pieces[piece]],
            dst_ref=left_all.at[index, pieces[piece]],
            send_sem=send_sem,
            recv_sem=recv_sem,
            device_id=(row_at(target, True), col),
            device_id_type=MESH,
        )

    def half_of(i, piece, target):
        return half_copy(row_at(i, True), piece, hsend.at[piece], hrecv.at[piece], target)

    def first_of(i):
        return group_at(i) * 2 + (near == 0).astype(jnp.int32)

    def second_of(i):
        return group_at(i) * 2 + (near != 0).astype(jnp.int32)

    def lend_first():
        index = row_count + first_of(0)
        return left_copy(left_ref.at[0, 0], index, esend.at[0], erecv.at[0], (group * 2, inward))

    def lend(index, number):
        return left_copy(left_all.at[index], row_count + index, esend.at[number], erecv.at[{7: 5, 10: 7}[number]], (row, inward))

    def lent(index, number):
        at = row_count + index
        return left_copy(left_all.at[at], at, esend.at[number], erecv.at[{0: 0, 7: 5, 10: 7}[number]], (row_at(1, True), col))

    def extra_across(i, piece):
        return half_copy(row_count + first_of(0), piece, esend.at[2 * i + piece - 1], erecv.at[2 * i + piece - 1], i)

    def extra_half(i, piece, target):
        return half_copy(row_count + first_of(i), piece, esend.at[5 + piece], ehrecv.at[piece], target)

    def second_to(i, owner):
        at = row_count + second_of(owner)
        return left_copy(left_all.at[at], at, esend.at[7 + i], erecv.at[5 + i], (row_at(i, True), col))

    fold = blk // 2
    lanes = lax.broadcasted_iota(jnp.int32, (blk, blk), 1)
    pack_blocks = right_blocks // 2

    def packed_copy(place, q):
        index = (place - 1) * q_count + q
        return pltpu.make_async_remote_copy(
            src_ref=packed.at[index],
            dst_ref=packed.at[index],
            send_sem=bsend.at[index],
            recv_sem=brecv.at[index],
            device_id=(row, near),
            device_id_type=MESH,
        )

    def pack(place, q):
        index = (place - 1) * q_count + q
        source = source_of(place)

        def one(b, c):
            moved = pltpu.roll(right_all[q, source, b], fold, 1)
            packed[index, b] = jnp.where(lanes < fold, moved, right_all[q, source, pack_blocks + b])
            return c

        lax.fori_loop(0, pack_blocks, one, 0)
        packed_copy(place, q).start()

    def table_out():
        return pltpu.make_async_remote_copy(
            src_ref=table,
            dst_ref=table_in,
            send_sem=tsem.at[0],
            recv_sem=tsem.at[1],
            device_id=(row, inward),
            device_id_type=MESH,
        )

    sum_blocks = slot_count // 2
    part = sum_blocks // PARTS

    def partial_sum(i):
        where = pl.ds(i * part, part)
        return pltpu.make_async_remote_copy(
            src_ref=total_in.at[where],
            dst_ref=total_in.at[where],
            send_sem=ssend.at[i],
            recv_sem=srecv.at[i],
            device_id=(row, near),
            device_id_type=MESH,
        )

    inner = jnp.logical_not(at_end)
    folding = inner & even
    folded = at_end & even
    lending = at_end & (row == first_of(0))
    twofold = (group % 2 == 1) == (near == 0)

    @pl.when(inner & odd)
    def _():
        for q in range(q_count):
            own_panel(0, q).start()

    @pl.when(inner)
    def _():
        for q in range(q_count):
            own_panel(1, q).start()

    @pl.when(lending)
    def _():
        lend_first().start()

    handed(0).start()
    for piece in range(2):
        for i in (1, 2):
            across(i, (i - 1 + piece) % 2).start()
    for copy in own:
        copy.wait()
    arrived_left(partner).wait_recv()

    entries.wait()
    lax.fori_loop(0, step_count, lambda step, c: (arrange(lists_ref, table, step, slot_count), c)[1], 0)

    @pl.when(folded)
    def _():
        table_out().start()

    @pl.when(folding)
    def _():
        for q in range(q_count):
            pack(1, q)

    listed = pltpu.make_async_copy(table, code_ref.at[pl.ds(0, 2 * step_count)], local_sem.at[1 + q_count])
    listed.start()
    zero = jnp.zeros((blk, blk), jnp.float32)

    def clear(o, c):
        acc[o] = zero
        return c

    lax.fori_loop(0, jnp.where(folding, 2 * slot_count, slot_count), clear, 0)
    rhs[:, blk:, blk:] = jnp.zeros((right_blocks, blk, blk), rhs.dtype)

    def receive(place, q):
        relayed(0, q, source_of(place)).wait_recv()

    def receive_inner(place, q):
        receive(place, q)
        if place == 0:
            relayed(1, q, source_of(place)).start()
        else:
            @pl.when(odd)
            def _():
                relayed(0, q, source_of(place)).start()

            @pl.when(even)
            def _():
                pack(place, q)

    def first_halves():
        for i in (1, 2):
            across(i, i - 1).wait_recv()
            half_of(i, i - 1, 3 - i).start()

        @pl.when(at_end)
        def _():
            own_panel(1, 0).start()

        @pl.when(folded & twofold)
        def _():
            lend(second_of(0), 7).start()

        @pl.when(folded)
        def _():
            own_panel(1, 1).start()

        @pl.when(folding)
        def _():
            lent(first_of(0), 0).wait_recv()
            for piece in range(2):
                for i in (1, 2):
                    extra_across(i, (i - 1 + piece) % 2).start()

    def second_halves():
        @pl.when(inner)
        def _():
            receive_inner(2, 0)

        for i in (1, 2):
            across(i, 2 - i).wait_recv()
            handed(i).start()

        for i in (1, 2):
            arrived_left(row_at(i, False)).wait_recv()

    listed.wait()

    def rest_of_left():
        half_of(3, 0, 1).wait_recv()
        half_of(3, 1, 1).wait_recv()
        handed(3).start()

        @pl.when(inner)
        def _():
            receive_inner(2, 1)

        @pl.when(inner & odd)
        def _():
            receive_inner(0, 0)

        arrived_left(row_at(3, False)).wait_recv()

        @pl.when(folded & jnp.logical_not(twofold))
        def _():
            lend(second_of(3), 10).start()

    def own_second():
        @pl.when(twofold)
        def _():
            lent(second_of(0), 7).wait_recv()
            second_to(1, 0).start()
            second_to(2, 0).start()

    def lists_of_end():
        table_out().wait_recv()
        fetched = pltpu.make_async_copy(table_in, code_ref.at[pl.ds(2 * step_count, 2 * step_count)], local_sem.at[2 + q_count])
        fetched.start()
        fetched.wait()

    def first_pieces():
        for i in (1, 2):
            extra_across(i, i - 1).wait_recv()
            extra_half(i, i - 1, 3 - i).start()

    def own_second():
        lent(second_of(0), 7).wait_recv()
        second_to(1, 0).start()
        second_to(2, 0).start()

    def second_pieces():
        for i in (1, 2):
            extra_across(i, 2 - i).wait_recv()

    def diagonal():
        extra_half(3, 0, 1).wait_recv()
        extra_half(3, 1, 1).wait_recv()

    def side_second():
        second_to(1, 1).wait_recv()

    def far_second_direct():
        second_to(2, 2).wait_recv()

    def far_second_lent():
        lent(second_of(3), 10).wait_recv()

    single = jnp.logical_not(twofold)
    right = {(place, q): functools.partial(receive_inner, place, q) for place in (0, 3) for q in range(2)}
    events = (
        (single, -1, lists_of_end),
        (twofold, 0, lists_of_end),
        (True, 1, right[0, 0]),
        (True, 3, first_pieces),
        (twofold, 3, own_second),
        (single, 4, second_pieces),
        (single, 4, right[0, 1]),
        (twofold, 5, second_pieces),
        (twofold, 5, right[0, 1]),
        (True, 6, right[3, 0]),
        (single, 8, side_second),
        (single, 7, diagonal),
        (twofold, 9, diagonal),
        (single, 9, far_second_lent),
        (single, 10, right[3, 1]),
        (twofold, 11, far_second_direct),
        (twofold, 12, right[3, 1]),
    )

    late = [(q * col_count + source_of(1)) // 2 == group_at(3) for q in range(2)]
    head = (jnp.where(late[0], 5, 1), jnp.where(late[0] | late[1], 2, 5), jnp.where(late[0], 1, jnp.where(late[1], 5, 2)))
    q_own = group // 2
    q_far = 1 - q_own
    near_first = q_own == 0
    twofold_jobs = head + (0, 6, 9 + 4 * q_own, 10 + 4 * q_own, 4, 3, 11, 9 + 4 * q_far, 10 + 4 * q_far, 15, 7)
    single_jobs = (
        1 + 4 * q_own,
        9 + 4 * q_own,
        1 + 4 * q_far,
        jnp.where(near_first, 2, 0),
        jnp.where(near_first, 0, 2),
        6,
        9 + 4 * q_far,
        4,
        3,
        11,
        10 + 4 * q_own,
        10 + 4 * q_far,
        15,
        7,
    )
    early = jnp.where(folding & single, 2, 0)

    unroll = next(u for u in (48, 32, 16, 8, 4, 2, 1) if pair_count % u == 0)

    def job(item, carry):
        def pick(choices):
            value = jnp.int32(choices[-1])
            for at in range(len(choices) - 1):
                value = jnp.where(item + early == at, choices[at], value)
            return value

        code = jnp.where(
            at_end,
            pick(END_JOBS),
            jnp.where(even, jnp.where(twofold, pick(twofold_jobs), pick(single_jobs)), pick(head + INNER_ODD)),
        )
        place, q, extra = code % 4, code // 4 % 2, code // 8
        source = source_of(place)
        kgroup = q * col_count + source
        owner = jnp.where(extra == 1, near, col)
        step = lax.rem(kgroup - row - owner + 2 * row_count, row_count)
        code_row = step + extra * 2 * step_count
        left_at = extra * row_count + kgroup
        base = extra * slot_count

        @pl.when(at_end & odd & (item == jnp.where(twofold, 4, 3)))
        def _():
            own_panel(1, 1).start()

        @pl.when(at_end & odd & (place > 0))
        def _():
            relayed(0, q, source).wait_recv()

        unpacking = folded & (place > 0)

        @pl.when(unpacking)
        def _():
            packed_copy(place, q).wait_recv()

        pl.when(item == jnp.where(early > 0, -1, 0))(first_halves)
        pl.when(item == 0)(second_halves)
        pl.when(item == jnp.where(inner, 2, 0))(rest_of_left)

        for who, at, event in events:
            pl.when(folding & who & (item == at))(event)

        for at, where in ((5, (3, 0)), (6, (0, 1)), (7, (3, 1))):
            @pl.when(inner & odd & (item == at))
            def _():
                receive_inner(*where)

        def split_left(i):
            x = left_all[left_at, i]
            high = x.astype(jnp.bfloat16)
            lhs[i, :, :blk] = high
            lhs[i, :, blk:] = (x - high.astype(jnp.float32)).astype(jnp.bfloat16)

        batched(left_blocks, split_left)

        def right_of(i, x):
            high = x.astype(jnp.bfloat16)
            rhs[i, :blk, :blk] = high
            rhs[i, blk:, :blk] = high
            rhs[i, :blk, blk:] = (x - high.astype(jnp.float32)).astype(jnp.bfloat16)

        @pl.when(jnp.logical_not(unpacking))
        def _():
            batched(right_blocks, lambda i: right_of(i, right_all[q, source, i]))

        @pl.when(unpacking)
        def _():
            def unpack(i):
                x = packed[jnp.maximum(place - 1, 0) * q_count + q, i]
                right_of(i, jnp.where(lanes < fold, 0.0, pltpu.roll(x, fold, 1)))
                right_of(pack_blocks + i, jnp.where(lanes < fold, 0.0, x))

            batched(pack_blocks, unpack, 2)

        def some(batch, carry):
            total, before = carry
            for u in range(unroll):
                p = batch * unroll + u
                entry = code_ref[code_row, p]
                both = jnp.dot(lhs[entry & 255], rhs[(entry >> 8) & 255], preferred_element_type=jnp.float32)
                slot = entry >> 16
                keep = (slot == before).astype(jnp.float32)
                total = total * keep + (both[:, :blk] + both[:, blk:])
                sums[p] = total
                before = slot
            return total, before

        lax.fori_loop(0, pair_count // unroll, some, (zero, jnp.int32(-1)))

        def put(o):
            entry = code_ref[step_count + code_row, o]
            found = ((entry >> 16) > 0).astype(jnp.float32)
            acc[base + o] = acc[base + o] + sums[jnp.maximum((entry & 65535) - 1, 0)] * found

        batched(slot_count, put)

        @pl.when(folding & (item == 12 - early))
        def _():
            for i in range(PARTS):
                def fold_sum(o, c):
                    moved = pltpu.roll(acc[slot_count + sum_blocks + o], fold, 1)
                    total_in[o] = jnp.where(lanes < fold, acc[slot_count + o], moved)
                    return c

                lax.fori_loop(i * part, (i + 1) * part, fold_sum, 0)
                partial_sum(i).start()

        return carry

    job_count = jnp.where(
        at_end,
        len(END_JOBS),
        jnp.where(even, len(twofold_jobs), 3 + len(INNER_ODD)),
    )
    lax.fori_loop(-early, job_count - early, job, 0)

    @pl.when(folded)
    def _():
        for i in range(PARTS):
            partial_sum(i).wait_recv()

            def add(o, c):
                x = total_in[o]
                out_ref[o] = acc[o] + jnp.where(lanes < fold, x, 0.0)
                out_ref[sum_blocks + o] = acc[sum_blocks + o] + jnp.where(lanes < fold, pltpu.roll(x, fold, 1), 0.0)
                return c

            lax.fori_loop(i * part, (i + 1) * part, add, 0)

    @pl.when(jnp.logical_not(folded))
    def _():
        def move(o, c):
            out_ref[o] = acc[o]
            return c

        lax.fori_loop(0, slot_count, move, 0)

    for q in range(q_count):
        own_panel(1, q).wait_send()

    @pl.when(inner)
    def _():
        for q in range(q_count):
            relayed(1, q, source_of(0)).wait_send()

    @pl.when(inner & odd)
    def _():
        for q in range(q_count):
            own_panel(0, q).wait_send()
            for place in (2, 3):
                relayed(0, q, source_of(place)).wait_send()

    @pl.when(lending)
    def _():
        lend_first().wait_send()

    @pl.when(folded)
    def _():
        table_out().wait_send()

        @pl.when(twofold)
        def _():
            lend(second_of(0), 7).wait_send()

        @pl.when(jnp.logical_not(twofold))
        def _():
            lend(second_of(3), 10).wait_send()

    @pl.when(folding)
    def _():
        for i in (1, 2):
            for piece in range(2):
                extra_across(i, piece).wait_send()
        extra_half(1, 0, 2).wait_send()
        extra_half(2, 1, 1).wait_send()

        @pl.when(twofold)
        def _():
            second_to(1, 0).wait_send()
            second_to(2, 0).wait_send()

        for place in (1, 2, 3):
            for q in range(q_count):
                packed_copy(place, q).wait_send()
        for i in range(PARTS):
            partial_sum(i).wait_send()

    for i in (1, 2):
        for piece in range(2):
            across(i, piece).wait_send()
    half_of(1, 0, 2).wait_send()
    half_of(2, 1, 1).wait_send()
    for i in range(groups):
        handed(i).wait_send()


def folded_call(row_count, col_count, lists, left_panels, right_panels, width):
    left_blocks, blk = left_panels.shape[2], left_panels.shape[3]
    q_count, right_blocks = right_panels.shape[0], right_panels.shape[3]
    step_count, pair_count = lists.shape[1], lists.shape[2]
    groups = row_count // 2
    dma = pltpu.SemaphoreType.DMA
    out = pl.pallas_call(
        functools.partial(fold_kernel, row_count, col_count),
        out_shape=jax.ShapeDtypeStruct((OCAP, blk, blk), jnp.float32),
        in_specs=[pl.BlockSpec(memory_space=pltpu.HBM)] * 3,
        out_specs=pl.BlockSpec(memory_space=pltpu.VMEM),
        scratch_shapes=[
            pltpu.VMEM((2 * row_count, left_blocks, blk, blk), jnp.float32),
            pltpu.VMEM((q_count, col_count, right_blocks, blk, blk), jnp.float32),
            pltpu.VMEM((3 * q_count, right_blocks // 2, blk, blk), jnp.float32),
            pltpu.VMEM((OCAP // 2, blk, blk), jnp.float32),
            pltpu.VMEM((left_blocks, blk, 2 * blk), jnp.bfloat16),
            pltpu.VMEM((right_blocks, 2 * blk, 2 * blk), jnp.bfloat16),
            pltpu.VMEM((pair_count, blk, blk), jnp.float32),
            pltpu.VMEM((2 * OCAP, blk, blk), jnp.float32),
            pltpu.VMEM((2 * step_count, width), jnp.int32),
            pltpu.VMEM((2 * step_count, width), jnp.int32),
            pltpu.SMEM((4 * step_count, width), jnp.int32),
            dma((2, q_count, col_count)),
            dma((q_count, col_count)),
            dma((2, 2)),
            dma((groups,)),
            dma((2,)),
            dma((row_count,)),
            dma((2, 2)),
            dma((2,)),
            dma((11,)),
            dma((8,)),
            dma((2,)),
            dma((3 * q_count,)),
            dma((3 * q_count,)),
            dma((2,)),
            dma((PARTS,)),
            dma((PARTS,)),
            dma((4 + q_count,)),
            pltpu.VMEM(lists.shape, jnp.int32),
        ],
        compiler_params=pltpu.CompilerParams(
            collective_id=0, has_side_effects=True, vmem_limit_bytes=60 * 1024 * 1024
        ),
    )(lists, left_panels, right_panels)
    return out[None, None]


def shards(row_count, col_count, left_panels, right_panels, product_lists):
    left_blocks, blk = left_panels.shape[2], left_panels.shape[3]
    q_count, right_blocks = right_panels.shape[0], right_panels.shape[3]
    pair_count = product_lists.shape[3]
    lists = jnp.transpose(product_lists[0, 0], (2, 0, 1))
    step_count = lists.shape[1]
    width = pl.cdiv(max(pair_count, OCAP), 128) * 128
    groups = row_count // 2
    if groups == 4 and col_count == 4 and q_count * col_count == row_count == step_count and OCAP % (2 * PARTS) == 0 and right_blocks % 2 == 0:
        return folded_call(row_count, col_count, lists, left_panels, right_panels, width)
    out = pl.pallas_call(
        functools.partial(kernel, row_count, col_count),
        out_shape=jax.ShapeDtypeStruct((OCAP, blk, blk), jnp.float32),
        in_specs=[pl.BlockSpec(memory_space=pltpu.VMEM)] + [pl.BlockSpec(memory_space=pltpu.HBM)] * 2,
        out_specs=pl.BlockSpec(memory_space=pltpu.VMEM),
        scratch_shapes=[
            pltpu.VMEM((row_count, left_blocks, blk, blk), jnp.float32),
            pltpu.VMEM((q_count, col_count, right_blocks, blk, blk), jnp.float32),
            pltpu.VMEM((left_blocks, blk, 2 * blk), jnp.bfloat16),
            pltpu.VMEM((right_blocks, 2 * blk, 2 * blk), jnp.bfloat16),
            pltpu.VMEM((pair_count, blk, blk), jnp.float32),
            pltpu.VMEM((2 * step_count, width), jnp.int32),
            pltpu.SMEM((2 * step_count, width), jnp.int32),
            pltpu.SemaphoreType.DMA((2, q_count, col_count)),
            pltpu.SemaphoreType.DMA((q_count, col_count)),
            pltpu.SemaphoreType.DMA((groups,)),
            pltpu.SemaphoreType.DMA((groups,)),
            pltpu.SemaphoreType.DMA((2,)),
            pltpu.SemaphoreType.DMA((row_count,)),
            pltpu.SemaphoreType.DMA((2,)),
            pltpu.SemaphoreType.DMA((2 + q_count,)),
        ],
        compiler_params=pltpu.CompilerParams(
            collective_id=0, has_side_effects=True, vmem_limit_bytes=50 * 1024 * 1024
        ),
    )(lists, left_panels, right_panels)
    return out[None, None]


def solution(mesh):
    return jax.shard_map(
        functools.partial(shards, mesh.shape["row"], mesh.shape["col"]),
        mesh=mesh,
        in_specs=(
            P("row", "col", None, None, None),
            P(None, "col", "row", None, None, None),
            P("row", "col", None, None, None),
        ),
        out_specs=P("row", "col", None, None, None),
        check_vma=False,
    )
```

```python
import functools

import jax
import jax.numpy as jnp
from jax import lax
from jax.experimental import pallas as pl
from jax.experimental.pallas import tpu as pltpu
from jax.sharding import PartitionSpec as P

OCAP = 24
UNROLL = 16
AHEAD = 3
MESH = pl.DeviceIdType.MESH
PARTS = 4
END_JOBS = (0, 4, 1, 5, 2, 6, 3, 7)
INNER_ODD = (6, 3, 0, 4, 7)


def arrange(lists_ref, table, step, slot_count):
    step_count, count = lists_ref.shape[1], lists_ref.shape[2]
    width = table.shape[1]
    left, right, out = (lists_ref[part, pl.ds(step, 1), :] for part in range(3))
    live = left >= 0
    slots = jnp.where(live, out, slot_count)
    lane = lax.broadcasted_iota(jnp.int32, (count, count), 1)
    same = lax.broadcasted_iota(jnp.int32, (count, count), 0) == lane

    def column(row):
        return jnp.sum(jnp.where(same, jnp.broadcast_to(row, (count, count)), 0), axis=1, keepdims=True)

    key = jnp.broadcast_to(slots, (count, count)) * count + lane
    key_column = jnp.sum(jnp.where(same, key, 0), axis=1, keepdims=True)
    rank = jnp.sum((key < key_column).astype(jnp.int32), axis=1, keepdims=True)
    packed = column(jnp.where(live, left + right * 256, 0) + slots * 65536)
    wide = lax.broadcasted_iota(jnp.int32, (count, width), 1)
    table[pl.ds(step, 1), :] = jnp.sum(jnp.where(rank == wide, packed, 0), axis=0, keepdims=True)
    slot_column = column(slots)
    upto = (slot_column <= wide).astype(jnp.int32) + (slot_column == wide).astype(jnp.int32) * 65536
    table[pl.ds(step_count + step, 1), :] = jnp.sum(upto, axis=0, keepdims=True)


def kernel(row_count, col_count, lists_ref, left_ref, right_ref, out_ref,
           left_all, right_all, lhs, rhs, sums, table, code_ref, zsend, zrecv, lsend, psend, hsend, lrecv, hrecv, local_sem):
    row = lax.axis_index("row")
    col = lax.axis_index("col")
    q_count = right_ref.shape[0]
    left_blocks, blk = left_ref.shape[2], left_ref.shape[3]
    right_blocks = right_ref.shape[3]
    step_count, pair_count = lists_ref.shape[1], lists_ref.shape[2]
    slot_count = out_ref.shape[0]
    groups = row_count // 2
    group, parity = row // 2, row % 2
    partner = group * 2 + 1 - parity
    square = groups == 4
    direct = (1, 2) if square else tuple(range(1, groups))

    def group_at(i):
        return (group // 2 * 2 + 1 - group % 2 if i == 1 else lax.rem(group + 2, groups)) if square and i in (1, 2) else (
            groups - 1 - group if square and i == 3 else lax.rem(group + i, groups))

    def row_at(i, same):
        return group_at(i) * 2 + (parity if same else 1 - parity)

    barrier = pltpu.get_barrier_semaphore()
    for i in direct:
        pl.semaphore_signal(barrier, inc=1, device_id=(row_at(i, True), col), device_id_type=MESH)
    pl.semaphore_signal(barrier, inc=1, device_id=(partner, col), device_id_type=MESH)

    @pl.when(col > 0)
    def _():
        pl.semaphore_signal(barrier, inc=1, device_id=(row, col - 1), device_id_type=MESH)

    @pl.when(col < col_count - 1)
    def _():
        pl.semaphore_signal(barrier, inc=1, device_id=(row, col + 1), device_id_type=MESH)

    own = [pltpu.make_async_copy(left_ref.at[0, 0], left_all.at[row], local_sem.at[0])]
    for q in range(q_count):
        own.append(pltpu.make_async_copy(right_ref.at[q, 0, 0], right_all.at[q, col], local_sem.at[1 + q]))
    for copy in own:
        copy.start()

    ends = (col == 0).astype(jnp.int32) + (col == col_count - 1).astype(jnp.int32)
    pl.semaphore_wait(barrier, len(direct) + 3 - ends)

    def along(direction, q, source, from_ref):
        return pltpu.make_async_remote_copy(
            src_ref=from_ref,
            dst_ref=right_all.at[q, source],
            send_sem=zsend.at[direction, q, source],
            recv_sem=zrecv.at[q, source],
            device_id=(row, col + (1 if direction else -1)),
            device_id_type=MESH,
        )

    def own_panel(direction, q):
        return along(direction, q, col, right_ref.at[q, 0, 0])

    def relayed(direction, q, source):
        return along(direction, q, source, right_all.at[q, source])

    def across(i):
        return pltpu.make_async_remote_copy(
            src_ref=left_ref.at[0, 0],
            dst_ref=left_all.at[row],
            send_sem=lsend.at[i],
            recv_sem=lrecv.at[row],
            device_id=(row_at(i, True), col),
            device_id_type=MESH,
        )

    def handed(i):
        source = row_at(i, True)
        return pltpu.make_async_remote_copy(
            src_ref=left_ref.at[0, 0] if i == 0 else left_all.at[source],
            dst_ref=left_all.at[source],
            send_sem=psend.at[i],
            recv_sem=lrecv.at[source],
            device_id=(partner, col),
            device_id_type=MESH,
        )

    def arrived_left(source):
        return pltpu.make_async_remote_copy(
            src_ref=left_all.at[source],
            dst_ref=left_all.at[source],
            send_sem=psend.at[0],
            recv_sem=lrecv.at[source],
            device_id=(partner, col),
            device_id_type=MESH,
        )

    half = left_blocks // 2
    pieces = (pl.ds(0, half), pl.ds(half, left_blocks - half))

    def half_of(i, piece, target):
        source = row_at(i, True)
        return pltpu.make_async_remote_copy(
            src_ref=left_all.at[source, pieces[piece]],
            dst_ref=left_all.at[source, pieces[piece]],
            send_sem=hsend.at[piece],
            recv_sem=hrecv.at[piece],
            device_id=(row_at(target, True), col),
            device_id_type=MESH,
        )

    for q in range(q_count):
        @pl.when(col > 0)
        def _():
            own_panel(0, q).start()

        @pl.when(col < col_count - 1)
        def _():
            own_panel(1, q).start()

    for i in direct:
        across(i).start()
    handed(0).start()

    lax.fori_loop(0, step_count, lambda step, c: (arrange(lists_ref, table, step, slot_count), c)[1], 0)
    out_ref[...] = jnp.zeros_like(out_ref)
    rhs[:, blk:, blk:] = jnp.zeros((right_blocks, blk, blk), rhs.dtype)
    for copy in own:
        copy.wait()

    sides = jnp.minimum(col, col_count - 1 - col)

    def item_of(item):
        rest = item - q_count
        later = rest - 2 * q_count * sides
        both = later < 0
        distance = jnp.where(both, rest // (2 * q_count) + 1, sides + 1 + later // q_count)
        q = jnp.where(both, rest % (2 * q_count) // 2, later % q_count)
        lower = jnp.where(both, rest % 2 == 0, col * 2 > col_count - 1)
        source = jnp.where(lower, col - distance, col + distance)
        own_item = rest < 0
        return jnp.where(own_item, col, source), jnp.where(own_item, item, q)

    def relay(item):
        source, q = item_of(item)

        @pl.when(source != col)
        def _():
            relayed(0, q, source).wait_recv()

        @pl.when((source < col) & (col < col_count - 1))
        def _():
            relayed(1, q, source).start()

        @pl.when((source > col) & (col > 0))
        def _():
            relayed(0, q, source).start()

    forwards = 1 - ends
    first = q_count * (2 + jnp.minimum(sides, 1))

    def relay_many(start, stop):
        lax.fori_loop(start, stop, lambda item, c: (relay(item), c)[1], 0)

    for i in direct:
        arrived_left(row_at(i, True)).wait_recv()
        if square:
            half_of(i, i - 1, 3 - i).start()
        handed(i).start()
    relay_many(q_count, first)
    listed = pltpu.make_async_copy(table, code_ref, local_sem.at[1 + q_count])
    listed.start()
    if square:
        half_of(3, 0, 1).wait_recv()
        half_of(3, 1, 1).wait_recv()
        handed(3).start()
    for i in range(groups):
        arrived_left(row_at(i, False)).wait_recv()
    listed.wait()

    def job(item, carry):
        source, q = item_of(item)
        kgroup = q * col_count + source
        step = lax.rem(kgroup - row - col + 2 * row_count, row_count)

        @pl.when(step < step_count)
        def _():
            def split_left(i, c):
                x = left_all[kgroup, i]
                high = x.astype(jnp.bfloat16)
                lhs[i, :, :blk] = high
                lhs[i, :, blk:] = (x - high.astype(jnp.float32)).astype(jnp.bfloat16)
                return c

            lax.fori_loop(0, left_blocks, split_left, 0)

        ahead = item + AHEAD * forwards

        @pl.when((ahead >= first) & (ahead < row_count))
        def _():
            relay(ahead)

        @pl.when(step < step_count)
        def _():
            def split_right(i, c):
                x = right_all[q, source, i]
                high = x.astype(jnp.bfloat16)
                rhs[i, :blk, :blk] = high
                rhs[i, blk:, :blk] = high
                rhs[i, :blk, blk:] = (x - high.astype(jnp.float32)).astype(jnp.bfloat16)
                return c

            lax.fori_loop(0, right_blocks, split_right, 0)

            def some(batch, carry):
                total, before = carry
                for u in range(UNROLL):
                    p = batch * UNROLL + u
                    code = code_ref[step, p]
                    both = jnp.dot(
                        lhs[code & 255], rhs[(code >> 8) & 255], preferred_element_type=jnp.float32
                    )
                    slot = code >> 16
                    keep = (slot == before).astype(jnp.float32)
                    total = total * keep + (both[:, :blk] + both[:, blk:])
                    sums[p] = total
                    before = slot
                return total, before

            lax.fori_loop(0, pair_count // UNROLL, some, (jnp.zeros((blk, blk), jnp.float32), jnp.int32(-1)))

            def put(o, c):
                code = code_ref[step_count + step, o]
                found = ((code >> 16) > 0).astype(jnp.float32)
                out_ref[o] = out_ref[o] + sums[jnp.maximum((code & 65535) - 1, 0)] * found
                return c

            lax.fori_loop(0, slot_count, put, 0)

        return carry

    lax.fori_loop(0, row_count, job, 0)

    for q in range(q_count):
        @pl.when(col > 0)
        def _():
            own_panel(0, q).wait_send()

        @pl.when(col < col_count - 1)
        def _():
            own_panel(1, q).wait_send()

    def sent(item, carry):
        source, q = item_of(item)

        @pl.when((source < col) & (col < col_count - 1))
        def _():
            relayed(1, q, source).wait_send()

        @pl.when((source > col) & (col > 0))
        def _():
            relayed(0, q, source).wait_send()

        return carry

    lax.fori_loop(q_count, row_count, sent, 0)
    for i in direct:
        across(i).wait_send()
    if square:
        half_of(1, 0, 2).wait_send()
        half_of(2, 1, 1).wait_send()
    for i in range(groups):
        handed(i).wait_send()


def batched(count, body, most=4):
    width = next(w for w in range(most, 0, -1) if count % w == 0)

    def batch(i, c):
        for u in range(width):
            body(i * width + u)
        return c

    lax.fori_loop(0, count // width, batch, 0)


def fold_kernel(row_count, col_count, lists_in, left_ref, right_ref, out_ref,
                left_all, right_all, packed, total_in, lhs, rhs, sums, acc, table, table_in, code_ref,
                zsend, zrecv, lsend, psend, hsend, lrecv, precv, hrecv, esend, erecv, ehrecv, bsend, brecv, tsem, ssend, srecv, local_sem, done_sem, turn_sem, lists_ref):
    row = lax.axis_index("row")
    col = lax.axis_index("col")
    q_count = right_ref.shape[0]
    left_blocks, blk = left_ref.shape[2], left_ref.shape[3]
    right_blocks = right_ref.shape[3]
    step_count, pair_count = lists_in.shape[1], lists_in.shape[2]
    slot_count = out_ref.shape[0]
    groups = row_count // 2
    group, parity = row // 2, row % 2
    partner = group * 2 + 1 - parity
    low = col * 2 < col_count
    at_end = (col == 0) | (col == col_count - 1)
    even = parity == 0
    odd = parity == 1
    inward = jnp.where(low, col + 1, col - 1)
    outward = jnp.where(low, col - 1, col + 1)
    near = jnp.where(low, 0, col_count - 1)

    def source_of(place):
        return jnp.where(low, place, col_count - 1 - place)

    def group_at(i):
        return (group, group // 2 * 2 + 1 - group % 2, lax.rem(group + 2, groups), groups - 1 - group)[i]

    def row_at(i, same):
        return group_at(i) * 2 + (parity if same else 1 - parity)

    barrier = pltpu.get_barrier_semaphore()
    for i in (1, 2):
        pl.semaphore_signal(barrier, inc=1, device_id=(row_at(i, True), col), device_id_type=MESH)
    pl.semaphore_signal(barrier, inc=1, device_id=(partner, col), device_id_type=MESH)
    pl.semaphore_signal(barrier, inc=1, device_id=(row, inward), device_id_type=MESH)

    @pl.when(jnp.logical_not(at_end))
    def _():
        pl.semaphore_signal(barrier, inc=1, device_id=(row, outward), device_id_type=MESH)

    @pl.when((col == 1) & even)
    def _():
        pl.semaphore_signal(barrier, inc=1, device_id=(row + 1, 0), device_id_type=MESH)

    own = [pltpu.make_async_copy(left_ref.at[0, 0], left_all.at[row], local_sem.at[0])]
    for q in range(q_count):
        own.append(pltpu.make_async_copy(right_ref.at[q, 0, 0], right_all.at[q, col], local_sem.at[1 + q]))
    for copy in own:
        copy.start()
    entries = pltpu.make_async_copy(lists_in, lists_ref, local_sem.at[3 + q_count])
    entries.start()
    pl.semaphore_wait(barrier, jnp.where(at_end & ((col > 0) | even), 4, 5))

    def panel(direction, q, source, from_ref):
        return pltpu.make_async_remote_copy(
            src_ref=from_ref,
            dst_ref=right_all.at[q, source],
            send_sem=zsend.at[direction, q, source],
            recv_sem=zrecv.at[q, source],
            device_id=(row, inward if direction else outward),
            device_id_type=MESH,
        )

    def own_panel(direction, q):
        return panel(direction, q, col, right_ref.at[q, 0, 0])

    def relayed(direction, q, source):
        return panel(direction, q, source, right_all.at[q, source])

    def left_copy(source_ref, index, send_sem, recv_sem, device):
        return pltpu.make_async_remote_copy(
            src_ref=source_ref,
            dst_ref=left_all.at[index],
            send_sem=send_sem,
            recv_sem=recv_sem,
            device_id=device,
            device_id_type=MESH,
        )

    def handed(i):
        source = row_at(i, True)
        return left_copy(left_ref.at[0, 0] if i == 0 else left_all.at[source], source,
                         psend.at[i], lrecv.at[source], (partner, col))

    def arrived_left(source):
        return left_copy(left_all.at[source], source, psend.at[0], lrecv.at[source], (partner, col))

    half = left_blocks // 2
    pieces = (pl.ds(0, half), pl.ds(half, left_blocks - half))

    def across(i, piece):
        return pltpu.make_async_remote_copy(
            src_ref=left_ref.at[0, 0, pieces[piece]],
            dst_ref=left_all.at[row, pieces[piece]],
            send_sem=lsend.at[i - 1, piece],
            recv_sem=precv.at[i - 1, piece],
            device_id=(row_at(i, True), col),
            device_id_type=MESH,
        )

    def half_copy(index, piece, send_sem, recv_sem, target):
        return pltpu.make_async_remote_copy(
            src_ref=left_all.at[index, pieces[piece]],
            dst_ref=left_all.at[index, pieces[piece]],
            send_sem=send_sem,
            recv_sem=recv_sem,
            device_id=(row_at(target, True), col),
            device_id_type=MESH,
        )

    def half_of(i, piece, target):
        return half_copy(row_at(i, True), piece, hsend.at[piece], hrecv.at[piece], target)

    def first_of(i):
        return group_at(i) * 2 + (near == 0).astype(jnp.int32)

    def second_of(i):
        return group_at(i) * 2 + (near != 0).astype(jnp.int32)

    def lend_first():
        index = row_count + first_of(0)
        return left_copy(left_ref.at[0, 0], index, esend.at[0], erecv.at[0], (group * 2, inward))

    def lend(index, number):
        return left_copy(left_all.at[index], row_count + index, esend.at[number], erecv.at[{7: 5, 10: 7}[number]], (row, inward))

    def lent(index, number):
        at = row_count + index
        return left_copy(left_all.at[at], at, esend.at[number], erecv.at[{0: 0, 7: 5, 10: 7}[number]], (row_at(1, True), col))

    def extra_across(i, piece):
        return half_copy(row_count + first_of(0), piece, esend.at[2 * i + piece - 1], erecv.at[2 * i + piece - 1], i)

    def extra_half(i, piece, target):
        return half_copy(row_count + first_of(i), piece, esend.at[5 + piece], ehrecv.at[piece], target)

    def second_to(i, owner):
        at = row_count + second_of(owner)
        return left_copy(left_all.at[at], at, esend.at[7 + i], erecv.at[5 + i], (row_at(i, True), col))

    fold = blk // 2
    lanes = lax.broadcasted_iota(jnp.int32, (blk, blk), 1)
    pack_blocks = right_blocks // 2

    def packed_copy(place, q):
        index = (place - 1) * q_count + q
        return pltpu.make_async_remote_copy(
            src_ref=packed.at[index],
            dst_ref=packed.at[index],
            send_sem=bsend.at[index],
            recv_sem=brecv.at[index],
            device_id=(row, near),
            device_id_type=MESH,
        )

    def pack(place, q):
        index = (place - 1) * q_count + q
        source = source_of(place)

        def one(b, c):
            moved = pltpu.roll(right_all[q, source, b], fold, 1)
            packed[index, b] = jnp.where(lanes < fold, moved, right_all[q, source, pack_blocks + b])
            return c

        lax.fori_loop(0, pack_blocks, one, 0)
        packed_copy(place, q).start()

    def table_out():
        return pltpu.make_async_remote_copy(
            src_ref=table,
            dst_ref=table_in,
            send_sem=tsem.at[0],
            recv_sem=tsem.at[1],
            device_id=(row, inward),
            device_id_type=MESH,
        )

    sum_blocks = slot_count // 2
    part = sum_blocks // PARTS

    def partial_sum(i):
        where = pl.ds(i * part, part)
        return pltpu.make_async_remote_copy(
            src_ref=total_in.at[where],
            dst_ref=total_in.at[where],
            send_sem=ssend.at[i],
            recv_sem=srecv.at[i],
            device_id=(row, near),
            device_id_type=MESH,
        )

    inner = jnp.logical_not(at_end)
    folding = inner & even
    folded = at_end & even
    lending = at_end & (row == first_of(0))
    twofold = (group % 2 == 1) == (near == 0)

    @pl.when(inner & odd)
    def _():
        for q in range(q_count):
            own_panel(0, q).start()

    @pl.when(inner)
    def _():
        for q in range(q_count):
            own_panel(1, q).start()

    @pl.when(lending)
    def _():
        lend_first().start()

    handed(0).start()
    for piece in range(2):
        for i in (1, 2):
            across(i, (i - 1 + piece) % 2).start()
    for copy in own:
        copy.wait()
    arrived_left(partner).wait_recv()

    entries.wait()
    lax.fori_loop(0, step_count, lambda step, c: (arrange(lists_ref, table, step, slot_count), c)[1], 0)

    @pl.when(folded)
    def _():
        table_out().start()

    @pl.when(lending)
    def _():
        own_panel(1, 0).start()

    @pl.when(folding)
    def _():
        for q in range(q_count):
            pack(1, q)

    listed = pltpu.make_async_copy(table, code_ref.at[pl.ds(0, 2 * step_count)], local_sem.at[1 + q_count])
    listed.start()
    zero = jnp.zeros((blk, blk), jnp.float32)

    def clear(o, c):
        acc[o] = zero
        return c

    lax.fori_loop(0, jnp.where(folding, 2 * slot_count, slot_count), clear, 0)
    rhs[:, blk:, blk:] = jnp.zeros((right_blocks, blk, blk), rhs.dtype)

    def receive(place, q):
        relayed(0, q, source_of(place)).wait_recv()

    def receive_inner(place, q):
        receive(place, q)
        if place == 0:
            relayed(1, q, source_of(place)).start()
        else:
            @pl.when(odd)
            def _():
                relayed(0, q, source_of(place)).start()

            @pl.when(even)
            def _():
                pack(place, q)

    def first_halves():
        for i in (1, 2):
            across(i, i - 1).wait_recv()
            half_of(i, i - 1, 3 - i).start()

        @pl.when(at_end & jnp.logical_not(lending))
        def _():
            own_panel(1, 0).start()

        @pl.when(folded & twofold)
        def _():
            lend(second_of(0), 7).start()
            own_panel(1, 1).start()

        @pl.when(folding)
        def _():
            lent(first_of(0), 0).wait_recv()
            for piece in range(2):
                for i in (1, 2):
                    extra_across(i, (i - 1 + piece) % 2).start()

    def second_halves():
        @pl.when(inner)
        def _():
            receive_inner(2, 0)

        for i in (1, 2):
            across(i, 2 - i).wait_recv()
            handed(i).start()

        for i in (1, 2):
            arrived_left(row_at(i, False)).wait_recv()

        @pl.when(at_end & odd & jnp.logical_not(twofold))
        def _():
            own_panel(1, 1).start()

    listed.wait()

    def rest_of_left():
        half_of(3, 0, 1).wait_recv()
        half_of(3, 1, 1).wait_recv()
        handed(3).start()

        @pl.when(inner)
        def _():
            receive_inner(2, 1)

        arrived_left(row_at(3, False)).wait_recv()

        @pl.when(folded & jnp.logical_not(twofold))
        def _():
            own_panel(1, 1).start()
            lend(second_of(3), 10).start()

    def own_second():
        @pl.when(twofold)
        def _():
            lent(second_of(0), 7).wait_recv()
            second_to(1, 0).start()
            second_to(2, 0).start()

    def lists_of_end():
        table_out().wait_recv()
        fetched = pltpu.make_async_copy(table_in, code_ref.at[pl.ds(2 * step_count, 2 * step_count)], local_sem.at[2 + q_count])
        fetched.start()
        fetched.wait()

    def first_pieces():
        for i in (1, 2):
            extra_across(i, i - 1).wait_recv()
            extra_half(i, i - 1, 3 - i).start()

    def own_second():
        lent(second_of(0), 7).wait_recv()
        second_to(1, 0).start()
        second_to(2, 0).start()

    def second_pieces():
        for i in (1, 2):
            extra_across(i, 2 - i).wait_recv()

    def diagonal():
        extra_half(3, 0, 1).wait_recv()
        extra_half(3, 1, 1).wait_recv()

    def side_second():
        second_to(1, 1).wait_recv()

    def far_second_direct():
        second_to(2, 2).wait_recv()

    def far_second_lent():
        lent(second_of(3), 10).wait_recv()

    q_own = group // 2
    q_far = 1 - q_own
    near_first = q_own == 0
    single = jnp.logical_not(twofold)
    right = {(place, q): functools.partial(receive_inner, place, q) for place in (0, 3) for q in range(2)}
    events = (
        (single, -1, lists_of_end),
        (twofold, 0, lists_of_end),
        (twofold, 3, right[0, 0]),
        (single, 1, right[0, 0]),
        (True, 3, first_pieces),
        (twofold, 3, own_second),
        (single, 4, second_pieces),
        (single, 5, functools.partial(receive, 0, 1)),
        (single, 7, lambda: relayed(1, 1, source_of(0)).start()),
        (twofold, 5, second_pieces),
        (twofold, 6, right[0, 1]),
        (single, 6, right[3, 0]),
        (twofold, 7, right[3, 0]),
        (single, 9, side_second),
        (single, 7, diagonal),
        (twofold, 9, diagonal),
        (single, 8, far_second_lent),
        (single, 9, right[3, 1]),
        (twofold, 11, far_second_direct),
        (twofold, 12, right[3, 1]),
    )

    late = [(q * col_count + source_of(1)) // 2 == group_at(3) for q in range(2)]
    head = (jnp.where(late[0], 5, 1), jnp.where(late[0] | late[1], 2, 5), jnp.where(late[0], 1, jnp.where(late[1], 5, 2)))
    twofold_jobs = head + (0, 6, 9 + 4 * q_own, 10 + 4 * q_own, 4, 3, 11, 9 + 4 * q_far, 10 + 4 * q_far, 15, 7)
    single_jobs = (
        1 + 4 * q_own,
        9 + 4 * q_own,
        1 + 4 * q_far,
        jnp.where(near_first, 2, 0),
        jnp.where(near_first, 6, 2),
        jnp.where(near_first, 0, 6),
        9 + 4 * q_far,
        4,
        3,
        11,
        10 + 4 * q_far,
        10 + 4 * q_own,
        15,
        7,
    )
    early = jnp.where(folding & single, 2, 0)

    unroll = next(u for u in (96, 48, 32, 16, 8, 4, 2, 1) if pair_count % u == 0)

    def job(item, carry):
        def pick(choices):
            value = jnp.int32(choices[-1])
            for at in range(len(choices) - 1):
                value = jnp.where(item + early == at, choices[at], value)
            return value

        code = jnp.where(
            at_end,
            pick(END_JOBS),
            jnp.where(even, jnp.where(twofold, pick(twofold_jobs), pick(single_jobs)), pick(head + INNER_ODD)),
        )
        place, q, extra = code % 4, code // 4 % 2, code // 8
        source = source_of(place)
        kgroup = q * col_count + source
        owner = jnp.where(extra == 1, near, col)
        step = lax.rem(kgroup - row - owner + 2 * row_count, row_count)
        code_row = step + extra * 2 * step_count
        left_at = extra * row_count + kgroup
        base = extra * slot_count

        @pl.when(at_end & twofold & odd & (item == 4))
        def _():
            own_panel(1, 1).start()

        @pl.when(at_end & odd & (place > 0))
        def _():
            relayed(0, q, source).wait_recv()

        unpacking = folded & (place > 0)

        @pl.when(unpacking)
        def _():
            packed_copy(place, q).wait_recv()

        pl.when(item == jnp.where(early > 0, -1, 0))(first_halves)
        pl.when(item == 0)(second_halves)
        pl.when(item == jnp.where(inner, 2, 0))(rest_of_left)

        for who, at, event in events:
            pl.when(folding & who & (item == at))(event)

        for at, where in ((1, (0, 0)), (4, (3, 0)), (5, (0, 1)), (7, (3, 1))):
            @pl.when(inner & odd & (item == at))
            def _():
                receive_inner(*where)

        def split_left(i):
            x = left_all[left_at, i]
            high = x.astype(jnp.bfloat16)
            lhs[i, :, :blk] = high
            lhs[i, :, blk:] = (x - high.astype(jnp.float32)).astype(jnp.bfloat16)

        batched(left_blocks, split_left)

        def right_of(i, x):
            high = x.astype(jnp.bfloat16)
            rhs[i, :blk, :blk] = high
            rhs[i, blk:, :blk] = high
            rhs[i, :blk, blk:] = (x - high.astype(jnp.float32)).astype(jnp.bfloat16)

        @pl.when(jnp.logical_not(unpacking))
        def _():
            batched(right_blocks, lambda i: right_of(i, right_all[q, source, i]))

        @pl.when(unpacking)
        def _():
            def unpack(i):
                x = packed[jnp.maximum(place - 1, 0) * q_count + q, i]
                right_of(i, jnp.where(lanes < fold, 0.0, pltpu.roll(x, fold, 1)))
                right_of(pack_blocks + i, jnp.where(lanes < fold, 0.0, x))

            batched(pack_blocks, unpack, 2)

        def some(batch, carry):
            total, before = carry
            for u in range(unroll):
                p = batch * unroll + u
                entry = code_ref[code_row, p]
                both = jnp.dot(lhs[entry & 255], rhs[(entry >> 8) & 255], preferred_element_type=jnp.float32)
                slot = entry >> 16
                keep = (slot == before).astype(jnp.float32)
                total = total * keep + (both[:, :blk] + both[:, blk:])
                sums[p] = total
                before = slot
            return total, before

        lax.fori_loop(0, pair_count // unroll, some, (zero, jnp.int32(-1)))

        def put(o):
            entry = code_ref[step_count + code_row, o]
            found = ((entry >> 16) > 0).astype(jnp.float32)
            acc[base + o] = acc[base + o] + sums[jnp.maximum((entry & 65535) - 1, 0)] * found

        batched(slot_count, put)

        @pl.when(folding & (item == 12 - early))
        def _():
            for i in range(PARTS):
                def fold_sum(o, c):
                    moved = pltpu.roll(acc[slot_count + sum_blocks + o], fold, 1)
                    total_in[o] = jnp.where(lanes < fold, acc[slot_count + o], moved)
                    return c

                lax.fori_loop(i * part, (i + 1) * part, fold_sum, 0)

        return carry

    job_count = jnp.where(
        at_end,
        len(END_JOBS),
        jnp.where(even, len(twofold_jobs), 3 + len(INNER_ODD)),
    )
    lax.fori_loop(-early, job_count - early, job, 0)

    @pl.when(inner & odd)
    def _():
        relayed(0, q_count - 1, source_of(3)).wait_send()
        pl.semaphore_signal(turn_sem, inc=1, device_id=(partner, col), device_id_type=MESH)

    @pl.when(folding)
    def _():
        pl.semaphore_wait(turn_sem, 1)
        for i in range(PARTS):
            partial_sum(i).start()

    def result(first, size, number):
        where = pl.ds(first, size)
        return pltpu.make_async_copy(acc.at[where], out_ref.at[where], done_sem.at[number])

    @pl.when(folded)
    def _():
        for i in range(PARTS):
            partial_sum(i).wait_recv()

            def add(o):
                x = total_in[i * part + o]
                low_at, high_at = i * part + o, sum_blocks + i * part + o
                acc[low_at] = acc[low_at] + jnp.where(lanes < fold, x, 0.0)
                acc[high_at] = acc[high_at] + jnp.where(lanes < fold, pltpu.roll(x, fold, 1), 0.0)

            batched(part, add)
            result(i * part, part, 2 * i).start()
            result(sum_blocks + i * part, part, 2 * i + 1).start()
        for i in range(PARTS):
            result(i * part, part, 2 * i).wait()
            result(sum_blocks + i * part, part, 2 * i + 1).wait()

    @pl.when(jnp.logical_not(folded))
    def _():
        result(0, slot_count, 0).start()
        result(0, slot_count, 0).wait()

    for q in range(q_count):
        own_panel(1, q).wait_send()

    @pl.when(inner)
    def _():
        for q in range(q_count):
            relayed(1, q, source_of(0)).wait_send()

    @pl.when(inner & odd)
    def _():
        for q in range(q_count):
            own_panel(0, q).wait_send()
            relayed(0, q, source_of(2)).wait_send()
        for q in range(q_count - 1):
            relayed(0, q, source_of(3)).wait_send()

    @pl.when(lending)
    def _():
        lend_first().wait_send()

    @pl.when(folded)
    def _():
        table_out().wait_send()

        @pl.when(twofold)
        def _():
            lend(second_of(0), 7).wait_send()

        @pl.when(jnp.logical_not(twofold))
        def _():
            lend(second_of(3), 10).wait_send()

    @pl.when(folding)
    def _():
        for i in (1, 2):
            for piece in range(2):
                extra_across(i, piece).wait_send()
        extra_half(1, 0, 2).wait_send()
        extra_half(2, 1, 1).wait_send()

        @pl.when(twofold)
        def _():
            second_to(1, 0).wait_send()
            second_to(2, 0).wait_send()

        for place in (1, 2, 3):
            for q in range(q_count):
                packed_copy(place, q).wait_send()
        for i in range(PARTS):
            partial_sum(i).wait_send()

    for i in (1, 2):
        for piece in range(2):
            across(i, piece).wait_send()
    half_of(1, 0, 2).wait_send()
    half_of(2, 1, 1).wait_send()
    for i in range(groups):
        handed(i).wait_send()


def folded_call(row_count, col_count, lists, left_panels, right_panels, width):
    left_blocks, blk = left_panels.shape[2], left_panels.shape[3]
    q_count, right_blocks = right_panels.shape[0], right_panels.shape[3]
    step_count, pair_count = lists.shape[1], lists.shape[2]
    groups = row_count // 2
    dma = pltpu.SemaphoreType.DMA
    out = pl.pallas_call(
        functools.partial(fold_kernel, row_count, col_count),
        out_shape=jax.ShapeDtypeStruct((OCAP, blk, blk), jnp.float32),
        in_specs=[pl.BlockSpec(memory_space=pltpu.HBM)] * 3,
        out_specs=pl.BlockSpec(memory_space=pltpu.HBM),
        scratch_shapes=[
            pltpu.VMEM((2 * row_count, left_blocks, blk, blk), jnp.float32),
            pltpu.VMEM((q_count, col_count, right_blocks, blk, blk), jnp.float32),
            pltpu.VMEM((3 * q_count, right_blocks // 2, blk, blk), jnp.float32),
            pltpu.VMEM((OCAP // 2, blk, blk), jnp.float32),
            pltpu.VMEM((left_blocks, blk, 2 * blk), jnp.bfloat16),
            pltpu.VMEM((right_blocks, 2 * blk, 2 * blk), jnp.bfloat16),
            pltpu.VMEM((pair_count, blk, blk), jnp.float32),
            pltpu.VMEM((2 * OCAP, blk, blk), jnp.float32),
            pltpu.VMEM((2 * step_count, width), jnp.int32),
            pltpu.VMEM((2 * step_count, width), jnp.int32),
            pltpu.SMEM((4 * step_count, width), jnp.int32),
            dma((2, q_count, col_count)),
            dma((q_count, col_count)),
            dma((2, 2)),
            dma((groups,)),
            dma((2,)),
            dma((row_count,)),
            dma((2, 2)),
            dma((2,)),
            dma((11,)),
            dma((8,)),
            dma((2,)),
            dma((3 * q_count,)),
            dma((3 * q_count,)),
            dma((2,)),
            dma((PARTS,)),
            dma((PARTS,)),
            dma((4 + q_count,)),
            dma((2 * PARTS,)),
            pltpu.SemaphoreType.REGULAR,
            pltpu.VMEM(lists.shape, jnp.int32),
        ],
        compiler_params=pltpu.CompilerParams(
            collective_id=0, has_side_effects=True, vmem_limit_bytes=60 * 1024 * 1024
        ),
    )(lists, left_panels, right_panels)
    return out[None, None]


def shards(row_count, col_count, left_panels, right_panels, product_lists):
    left_blocks, blk = left_panels.shape[2], left_panels.shape[3]
    q_count, right_blocks = right_panels.shape[0], right_panels.shape[3]
    pair_count = product_lists.shape[3]
    lists = jnp.transpose(product_lists[0, 0], (2, 0, 1))
    step_count = lists.shape[1]
    width = pl.cdiv(max(pair_count, OCAP), 128) * 128
    groups = row_count // 2
    if groups == 4 and col_count == 4 and q_count * col_count == row_count == step_count and OCAP % (2 * PARTS) == 0 and right_blocks % 2 == 0:
        return folded_call(row_count, col_count, lists, left_panels, right_panels, width)
    out = pl.pallas_call(
        functools.partial(kernel, row_count, col_count),
        out_shape=jax.ShapeDtypeStruct((OCAP, blk, blk), jnp.float32),
        in_specs=[pl.BlockSpec(memory_space=pltpu.VMEM)] + [pl.BlockSpec(memory_space=pltpu.HBM)] * 2,
        out_specs=pl.BlockSpec(memory_space=pltpu.VMEM),
        scratch_shapes=[
            pltpu.VMEM((row_count, left_blocks, blk, blk), jnp.float32),
            pltpu.VMEM((q_count, col_count, right_blocks, blk, blk), jnp.float32),
            pltpu.VMEM((left_blocks, blk, 2 * blk), jnp.bfloat16),
            pltpu.VMEM((right_blocks, 2 * blk, 2 * blk), jnp.bfloat16),
            pltpu.VMEM((pair_count, blk, blk), jnp.float32),
            pltpu.VMEM((2 * step_count, width), jnp.int32),
            pltpu.SMEM((2 * step_count, width), jnp.int32),
            pltpu.SemaphoreType.DMA((2, q_count, col_count)),
            pltpu.SemaphoreType.DMA((q_count, col_count)),
            pltpu.SemaphoreType.DMA((groups,)),
            pltpu.SemaphoreType.DMA((groups,)),
            pltpu.SemaphoreType.DMA((2,)),
            pltpu.SemaphoreType.DMA((row_count,)),
            pltpu.SemaphoreType.DMA((2,)),
            pltpu.SemaphoreType.DMA((2 + q_count,)),
        ],
        compiler_params=pltpu.CompilerParams(
            collective_id=0, has_side_effects=True, vmem_limit_bytes=50 * 1024 * 1024
        ),
    )(lists, left_panels, right_panels)
    return out[None, None]


def solution(mesh):
    return jax.shard_map(
        functools.partial(shards, mesh.shape["row"], mesh.shape["col"]),
        mesh=mesh,
        in_specs=(
            P("row", "col", None, None, None),
            P(None, "col", "row", None, None, None),
            P("row", "col", None, None, None),
        ),
        out_specs=P("row", "col", None, None, None),
        check_vma=False,
    )
```

```python
import functools

import jax
import jax.numpy as jnp
from jax import lax
from jax.experimental import pallas as pl
from jax.experimental.pallas import tpu as pltpu
from jax.sharding import PartitionSpec as P

OCAP = 24
UNROLL = 16
AHEAD = 3
MESH = pl.DeviceIdType.MESH
PARTS = 4
FIRST_PARTS = 1
END_JOBS = (0, 4, 1, 5, 2, 6, 3, 7)
INNER_ODD = (6, 3, 0, 4, 7)


def arrange(lists_ref, table, step, slot_count):
    step_count, count = lists_ref.shape[1], lists_ref.shape[2]
    width = table.shape[1]
    left, right, out = (lists_ref[part, pl.ds(step, 1), :] for part in range(3))
    live = left >= 0
    slots = jnp.where(live, out, slot_count)
    lane = lax.broadcasted_iota(jnp.int32, (count, count), 1)
    same = lax.broadcasted_iota(jnp.int32, (count, count), 0) == lane

    def column(row):
        return jnp.sum(jnp.where(same, jnp.broadcast_to(row, (count, count)), 0), axis=1, keepdims=True)

    key = jnp.broadcast_to(slots, (count, count)) * count + lane
    key_column = jnp.sum(jnp.where(same, key, 0), axis=1, keepdims=True)
    rank = jnp.sum((key < key_column).astype(jnp.int32), axis=1, keepdims=True)
    packed = column(jnp.where(live, left + right * 256, 0) + slots * 65536)
    wide = lax.broadcasted_iota(jnp.int32, (count, width), 1)
    table[pl.ds(step, 1), :] = jnp.sum(jnp.where(rank == wide, packed, 0), axis=0, keepdims=True)
    slot_column = column(slots)
    upto = (slot_column <= wide).astype(jnp.int32) + (slot_column == wide).astype(jnp.int32) * 65536
    table[pl.ds(step_count + step, 1), :] = jnp.sum(upto, axis=0, keepdims=True)


def kernel(row_count, col_count, lists_ref, left_ref, right_ref, out_ref,
           left_all, right_all, lhs, rhs, sums, table, code_ref, zsend, zrecv, lsend, psend, hsend, lrecv, hrecv, local_sem):
    row = lax.axis_index("row")
    col = lax.axis_index("col")
    q_count = right_ref.shape[0]
    left_blocks, blk = left_ref.shape[2], left_ref.shape[3]
    right_blocks = right_ref.shape[3]
    step_count, pair_count = lists_ref.shape[1], lists_ref.shape[2]
    slot_count = out_ref.shape[0]
    groups = row_count // 2
    group, parity = row // 2, row % 2
    partner = group * 2 + 1 - parity
    square = groups == 4
    direct = (1, 2) if square else tuple(range(1, groups))

    def group_at(i):
        return (group // 2 * 2 + 1 - group % 2 if i == 1 else lax.rem(group + 2, groups)) if square and i in (1, 2) else (
            groups - 1 - group if square and i == 3 else lax.rem(group + i, groups))

    def row_at(i, same):
        return group_at(i) * 2 + (parity if same else 1 - parity)

    barrier = pltpu.get_barrier_semaphore()
    for i in direct:
        pl.semaphore_signal(barrier, inc=1, device_id=(row_at(i, True), col), device_id_type=MESH)
    pl.semaphore_signal(barrier, inc=1, device_id=(partner, col), device_id_type=MESH)

    @pl.when(col > 0)
    def _():
        pl.semaphore_signal(barrier, inc=1, device_id=(row, col - 1), device_id_type=MESH)

    @pl.when(col < col_count - 1)
    def _():
        pl.semaphore_signal(barrier, inc=1, device_id=(row, col + 1), device_id_type=MESH)

    own = [pltpu.make_async_copy(left_ref.at[0, 0], left_all.at[row], local_sem.at[0])]
    for q in range(q_count):
        own.append(pltpu.make_async_copy(right_ref.at[q, 0, 0], right_all.at[q, col], local_sem.at[1 + q]))
    for copy in own:
        copy.start()

    ends = (col == 0).astype(jnp.int32) + (col == col_count - 1).astype(jnp.int32)
    pl.semaphore_wait(barrier, len(direct) + 3 - ends)

    def along(direction, q, source, from_ref):
        return pltpu.make_async_remote_copy(
            src_ref=from_ref,
            dst_ref=right_all.at[q, source],
            send_sem=zsend.at[direction, q, source],
            recv_sem=zrecv.at[q, source],
            device_id=(row, col + (1 if direction else -1)),
            device_id_type=MESH,
        )

    def own_panel(direction, q):
        return along(direction, q, col, right_ref.at[q, 0, 0])

    def relayed(direction, q, source):
        return along(direction, q, source, right_all.at[q, source])

    def across(i):
        return pltpu.make_async_remote_copy(
            src_ref=left_ref.at[0, 0],
            dst_ref=left_all.at[row],
            send_sem=lsend.at[i],
            recv_sem=lrecv.at[row],
            device_id=(row_at(i, True), col),
            device_id_type=MESH,
        )

    def handed(i):
        source = row_at(i, True)
        return pltpu.make_async_remote_copy(
            src_ref=left_ref.at[0, 0] if i == 0 else left_all.at[source],
            dst_ref=left_all.at[source],
            send_sem=psend.at[i],
            recv_sem=lrecv.at[source],
            device_id=(partner, col),
            device_id_type=MESH,
        )

    def arrived_left(source):
        return pltpu.make_async_remote_copy(
            src_ref=left_all.at[source],
            dst_ref=left_all.at[source],
            send_sem=psend.at[0],
            recv_sem=lrecv.at[source],
            device_id=(partner, col),
            device_id_type=MESH,
        )

    half = left_blocks // 2
    pieces = (pl.ds(0, half), pl.ds(half, left_blocks - half))

    def half_of(i, piece, target):
        source = row_at(i, True)
        return pltpu.make_async_remote_copy(
            src_ref=left_all.at[source, pieces[piece]],
            dst_ref=left_all.at[source, pieces[piece]],
            send_sem=hsend.at[piece],
            recv_sem=hrecv.at[piece],
            device_id=(row_at(target, True), col),
            device_id_type=MESH,
        )

    for q in range(q_count):
        @pl.when(col > 0)
        def _():
            own_panel(0, q).start()

        @pl.when(col < col_count - 1)
        def _():
            own_panel(1, q).start()

    for i in direct:
        across(i).start()
    handed(0).start()

    lax.fori_loop(0, step_count, lambda step, c: (arrange(lists_ref, table, step, slot_count), c)[1], 0)
    out_ref[...] = jnp.zeros_like(out_ref)
    rhs[:, blk:, blk:] = jnp.zeros((right_blocks, blk, blk), rhs.dtype)
    for copy in own:
        copy.wait()

    sides = jnp.minimum(col, col_count - 1 - col)

    def item_of(item):
        rest = item - q_count
        later = rest - 2 * q_count * sides
        both = later < 0
        distance = jnp.where(both, rest // (2 * q_count) + 1, sides + 1 + later // q_count)
        q = jnp.where(both, rest % (2 * q_count) // 2, later % q_count)
        lower = jnp.where(both, rest % 2 == 0, col * 2 > col_count - 1)
        source = jnp.where(lower, col - distance, col + distance)
        own_item = rest < 0
        return jnp.where(own_item, col, source), jnp.where(own_item, item, q)

    def relay(item):
        source, q = item_of(item)

        @pl.when(source != col)
        def _():
            relayed(0, q, source).wait_recv()

        @pl.when((source < col) & (col < col_count - 1))
        def _():
            relayed(1, q, source).start()

        @pl.when((source > col) & (col > 0))
        def _():
            relayed(0, q, source).start()

    forwards = 1 - ends
    first = q_count * (2 + jnp.minimum(sides, 1))

    def relay_many(start, stop):
        lax.fori_loop(start, stop, lambda item, c: (relay(item), c)[1], 0)

    for i in direct:
        arrived_left(row_at(i, True)).wait_recv()
        if square:
            half_of(i, i - 1, 3 - i).start()
        handed(i).start()
    relay_many(q_count, first)
    listed = pltpu.make_async_copy(table, code_ref, local_sem.at[1 + q_count])
    listed.start()
    if square:
        half_of(3, 0, 1).wait_recv()
        half_of(3, 1, 1).wait_recv()
        handed(3).start()
    for i in range(groups):
        arrived_left(row_at(i, False)).wait_recv()
    listed.wait()

    def job(item, carry):
        source, q = item_of(item)
        kgroup = q * col_count + source
        step = lax.rem(kgroup - row - col + 2 * row_count, row_count)

        @pl.when(step < step_count)
        def _():
            def split_left(i, c):
                x = left_all[kgroup, i]
                high = x.astype(jnp.bfloat16)
                lhs[i, :, :blk] = high
                lhs[i, :, blk:] = (x - high.astype(jnp.float32)).astype(jnp.bfloat16)
                return c

            lax.fori_loop(0, left_blocks, split_left, 0)

        ahead = item + AHEAD * forwards

        @pl.when((ahead >= first) & (ahead < row_count))
        def _():
            relay(ahead)

        @pl.when(step < step_count)
        def _():
            def split_right(i, c):
                x = right_all[q, source, i]
                high = x.astype(jnp.bfloat16)
                rhs[i, :blk, :blk] = high
                rhs[i, blk:, :blk] = high
                rhs[i, :blk, blk:] = (x - high.astype(jnp.float32)).astype(jnp.bfloat16)
                return c

            lax.fori_loop(0, right_blocks, split_right, 0)

            def some(batch, carry):
                total, before = carry
                for u in range(UNROLL):
                    p = batch * UNROLL + u
                    code = code_ref[step, p]
                    both = jnp.dot(
                        lhs[code & 255], rhs[(code >> 8) & 255], preferred_element_type=jnp.float32
                    )
                    slot = code >> 16
                    keep = (slot == before).astype(jnp.float32)
                    total = total * keep + (both[:, :blk] + both[:, blk:])
                    sums[p] = total
                    before = slot
                return total, before

            lax.fori_loop(0, pair_count // UNROLL, some, (jnp.zeros((blk, blk), jnp.float32), jnp.int32(-1)))

            def put(o, c):
                code = code_ref[step_count + step, o]
                found = ((code >> 16) > 0).astype(jnp.float32)
                out_ref[o] = out_ref[o] + sums[jnp.maximum((code & 65535) - 1, 0)] * found
                return c

            lax.fori_loop(0, slot_count, put, 0)

        return carry

    lax.fori_loop(0, row_count, job, 0)

    for q in range(q_count):
        @pl.when(col > 0)
        def _():
            own_panel(0, q).wait_send()

        @pl.when(col < col_count - 1)
        def _():
            own_panel(1, q).wait_send()

    def sent(item, carry):
        source, q = item_of(item)

        @pl.when((source < col) & (col < col_count - 1))
        def _():
            relayed(1, q, source).wait_send()

        @pl.when((source > col) & (col > 0))
        def _():
            relayed(0, q, source).wait_send()

        return carry

    lax.fori_loop(q_count, row_count, sent, 0)
    for i in direct:
        across(i).wait_send()
    if square:
        half_of(1, 0, 2).wait_send()
        half_of(2, 1, 1).wait_send()
    for i in range(groups):
        handed(i).wait_send()


def batched(count, body, most=4):
    width = next(w for w in range(most, 0, -1) if count % w == 0)

    def batch(i, c):
        for u in range(width):
            body(i * width + u)
        return c

    lax.fori_loop(0, count // width, batch, 0)


def fold_kernel(row_count, col_count, lists_in, left_ref, right_ref, out_ref,
                left_all, right_all, packed, total_in, lhs, rhs, sums, acc, table, table_in, code_ref,
                zsend, zrecv, lsend, psend, hsend, lrecv, precv, hrecv, esend, erecv, ehrecv, bsend, brecv, tsem, ssend, srecv, local_sem, done_sem, turn_sem, lists_ref):
    row = lax.axis_index("row")
    col = lax.axis_index("col")
    q_count = right_ref.shape[0]
    left_blocks, blk = left_ref.shape[2], left_ref.shape[3]
    right_blocks = right_ref.shape[3]
    step_count, pair_count = lists_in.shape[1], lists_in.shape[2]
    slot_count = out_ref.shape[0]
    groups = row_count // 2
    group, parity = row // 2, row % 2
    partner = group * 2 + 1 - parity
    low = col * 2 < col_count
    at_end = (col == 0) | (col == col_count - 1)
    even = parity == 0
    odd = parity == 1
    inward = jnp.where(low, col + 1, col - 1)
    outward = jnp.where(low, col - 1, col + 1)
    near = jnp.where(low, 0, col_count - 1)

    def source_of(place):
        return jnp.where(low, place, col_count - 1 - place)

    def group_at(i):
        return (group, group // 2 * 2 + 1 - group % 2, lax.rem(group + 2, groups), groups - 1 - group)[i]

    def row_at(i, same):
        return group_at(i) * 2 + (parity if same else 1 - parity)

    barrier = pltpu.get_barrier_semaphore()
    for i in (1, 2):
        pl.semaphore_signal(barrier, inc=1, device_id=(row_at(i, True), col), device_id_type=MESH)
    pl.semaphore_signal(barrier, inc=1, device_id=(partner, col), device_id_type=MESH)
    pl.semaphore_signal(barrier, inc=1, device_id=(row, inward), device_id_type=MESH)

    @pl.when(jnp.logical_not(at_end))
    def _():
        pl.semaphore_signal(barrier, inc=1, device_id=(row, outward), device_id_type=MESH)

    @pl.when((col == 1) & even)
    def _():
        pl.semaphore_signal(barrier, inc=1, device_id=(row + 1, 0), device_id_type=MESH)

    own = [pltpu.make_async_copy(left_ref.at[0, 0], left_all.at[row], local_sem.at[0])]
    for q in range(q_count):
        own.append(pltpu.make_async_copy(right_ref.at[q, 0, 0], right_all.at[q, col], local_sem.at[1 + q]))
    for copy in own:
        copy.start()
    entries = pltpu.make_async_copy(lists_in, lists_ref, local_sem.at[3 + q_count])
    entries.start()
    pl.semaphore_wait(barrier, jnp.where(at_end & ((col > 0) | even), 4, 5))

    def panel(direction, q, source, from_ref):
        return pltpu.make_async_remote_copy(
            src_ref=from_ref,
            dst_ref=right_all.at[q, source],
            send_sem=zsend.at[direction, q, source],
            recv_sem=zrecv.at[q, source],
            device_id=(row, inward if direction else outward),
            device_id_type=MESH,
        )

    def own_panel(direction, q):
        return panel(direction, q, col, right_ref.at[q, 0, 0])

    def relayed(direction, q, source):
        return panel(direction, q, source, right_all.at[q, source])

    def left_copy(source_ref, index, send_sem, recv_sem, device):
        return pltpu.make_async_remote_copy(
            src_ref=source_ref,
            dst_ref=left_all.at[index],
            send_sem=send_sem,
            recv_sem=recv_sem,
            device_id=device,
            device_id_type=MESH,
        )

    def handed(i):
        source = row_at(i, True)
        return left_copy(left_ref.at[0, 0] if i == 0 else left_all.at[source], source,
                         psend.at[i], lrecv.at[source], (partner, col))

    def arrived_left(source):
        return left_copy(left_all.at[source], source, psend.at[0], lrecv.at[source], (partner, col))

    half = left_blocks // 2
    pieces = (pl.ds(0, half), pl.ds(half, left_blocks - half))

    def across(i, piece):
        return pltpu.make_async_remote_copy(
            src_ref=left_ref.at[0, 0, pieces[piece]],
            dst_ref=left_all.at[row, pieces[piece]],
            send_sem=lsend.at[i - 1, piece],
            recv_sem=precv.at[i - 1, piece],
            device_id=(row_at(i, True), col),
            device_id_type=MESH,
        )

    def half_copy(index, piece, send_sem, recv_sem, target):
        return pltpu.make_async_remote_copy(
            src_ref=left_all.at[index, pieces[piece]],
            dst_ref=left_all.at[index, pieces[piece]],
            send_sem=send_sem,
            recv_sem=recv_sem,
            device_id=(row_at(target, True), col),
            device_id_type=MESH,
        )

    def half_of(i, piece, target):
        return half_copy(row_at(i, True), piece, hsend.at[piece], hrecv.at[piece], target)

    def first_of(i):
        return group_at(i) * 2 + (near == 0).astype(jnp.int32)

    def second_of(i):
        return group_at(i) * 2 + (near != 0).astype(jnp.int32)

    def lend_first():
        index = row_count + first_of(0)
        return left_copy(left_ref.at[0, 0], index, esend.at[0], erecv.at[0], (group * 2, inward))

    def lend(index, number):
        return left_copy(left_all.at[index], row_count + index, esend.at[number], erecv.at[{7: 5, 10: 7}[number]], (row, inward))

    def lent(index, number):
        at = row_count + index
        return left_copy(left_all.at[at], at, esend.at[number], erecv.at[{0: 0, 7: 5, 10: 7}[number]], (row_at(1, True), col))

    def extra_across(i, piece):
        return half_copy(row_count + first_of(0), piece, esend.at[2 * i + piece - 1], erecv.at[2 * i + piece - 1], i)

    def extra_half(i, piece, target):
        return half_copy(row_count + first_of(i), piece, esend.at[5 + piece], ehrecv.at[piece], target)

    def second_to(i, owner):
        at = row_count + second_of(owner)
        return left_copy(left_all.at[at], at, esend.at[7 + i], erecv.at[5 + i], (row_at(i, True), col))

    fold = blk // 2
    lanes = lax.broadcasted_iota(jnp.int32, (blk, blk), 1)
    pack_blocks = right_blocks // 2

    def packed_copy(place, q):
        index = (place - 1) * q_count + q
        return pltpu.make_async_remote_copy(
            src_ref=packed.at[index],
            dst_ref=packed.at[index],
            send_sem=bsend.at[index],
            recv_sem=brecv.at[index],
            device_id=(row, near),
            device_id_type=MESH,
        )

    def pack(place, q):
        index = (place - 1) * q_count + q
        source = source_of(place)

        def one(b, c):
            moved = pltpu.roll(right_all[q, source, b], fold, 1)
            packed[index, b] = jnp.where(lanes < fold, moved, right_all[q, source, pack_blocks + b])
            return c

        lax.fori_loop(0, pack_blocks, one, 0)
        packed_copy(place, q).start()

    def table_out():
        return pltpu.make_async_remote_copy(
            src_ref=table,
            dst_ref=table_in,
            send_sem=tsem.at[0],
            recv_sem=tsem.at[1],
            device_id=(row, inward),
            device_id_type=MESH,
        )

    sum_blocks = slot_count // 2
    part = sum_blocks // PARTS

    def partial_sum(i):
        where = pl.ds(i * part, part)
        return pltpu.make_async_remote_copy(
            src_ref=total_in.at[where],
            dst_ref=total_in.at[where],
            send_sem=ssend.at[i],
            recv_sem=srecv.at[i],
            device_id=(row, near),
            device_id_type=MESH,
        )

    inner = jnp.logical_not(at_end)
    folding = inner & even
    folded = at_end & even
    lending = at_end & (row == first_of(0))
    twofold = (group % 2 == 1) == (near == 0)

    @pl.when(inner & odd)
    def _():
        for q in range(q_count):
            own_panel(0, q).start()

    @pl.when(inner)
    def _():
        for q in range(q_count):
            own_panel(1, q).start()

    @pl.when(lending)
    def _():
        lend_first().start()

    handed(0).start()
    for piece in range(2):
        for i in (1, 2):
            across(i, (i - 1 + piece) % 2).start()
    for copy in own:
        copy.wait()
    arrived_left(partner).wait_recv()

    entries.wait()
    lax.fori_loop(0, step_count, lambda step, c: (arrange(lists_ref, table, step, slot_count), c)[1], 0)

    @pl.when(folded)
    def _():
        table_out().start()

    @pl.when(lending)
    def _():
        own_panel(1, 0).start()

    @pl.when(folding)
    def _():
        for q in range(q_count):
            pack(1, q)

    listed = pltpu.make_async_copy(table, code_ref.at[pl.ds(0, 2 * step_count)], local_sem.at[1 + q_count])
    listed.start()
    zero = jnp.zeros((blk, blk), jnp.float32)

    def clear(o, c):
        acc[o] = zero
        return c

    lax.fori_loop(0, jnp.where(folding, 2 * slot_count, slot_count), clear, 0)
    rhs[:, blk:, blk:] = jnp.zeros((right_blocks, blk, blk), rhs.dtype)

    def receive(place, q):
        relayed(0, q, source_of(place)).wait_recv()

    def receive_inner(place, q):
        receive(place, q)
        if place == 0:
            relayed(1, q, source_of(place)).start()
        else:
            @pl.when(odd)
            def _():
                relayed(0, q, source_of(place)).start()

            @pl.when(even)
            def _():
                pack(place, q)

    def first_halves():
        for i in (1, 2):
            across(i, i - 1).wait_recv()
            half_of(i, i - 1, 3 - i).start()

        @pl.when(at_end & jnp.logical_not(lending))
        def _():
            own_panel(1, 0).start()

        @pl.when(folded & twofold)
        def _():
            lend(second_of(0), 7).start()
            own_panel(1, 1).start()

        @pl.when(folding)
        def _():
            lent(first_of(0), 0).wait_recv()
            for piece in range(2):
                for i in (1, 2):
                    extra_across(i, (i - 1 + piece) % 2).start()

    def second_halves():
        @pl.when(inner)
        def _():
            receive_inner(2, 0)

        for i in (1, 2):
            across(i, 2 - i).wait_recv()
            handed(i).start()

        for i in (1, 2):
            arrived_left(row_at(i, False)).wait_recv()

        @pl.when(at_end & odd & jnp.logical_not(twofold))
        def _():
            own_panel(1, 1).start()

    listed.wait()

    def rest_of_left():
        half_of(3, 0, 1).wait_recv()
        half_of(3, 1, 1).wait_recv()
        handed(3).start()

        @pl.when(inner)
        def _():
            receive_inner(2, 1)

        arrived_left(row_at(3, False)).wait_recv()

        @pl.when(folded & jnp.logical_not(twofold))
        def _():
            own_panel(1, 1).start()
            lend(second_of(3), 10).start()

    def own_second():
        @pl.when(twofold)
        def _():
            lent(second_of(0), 7).wait_recv()
            second_to(1, 0).start()
            second_to(2, 0).start()

    def lists_of_end():
        table_out().wait_recv()
        fetched = pltpu.make_async_copy(table_in, code_ref.at[pl.ds(2 * step_count, 2 * step_count)], local_sem.at[2 + q_count])
        fetched.start()
        fetched.wait()

    def first_pieces():
        for i in (1, 2):
            extra_across(i, i - 1).wait_recv()
            extra_half(i, i - 1, 3 - i).start()

    def own_second():
        lent(second_of(0), 7).wait_recv()
        second_to(1, 0).start()
        second_to(2, 0).start()

    def second_pieces():
        for i in (1, 2):
            extra_across(i, 2 - i).wait_recv()

    def diagonal():
        extra_half(3, 0, 1).wait_recv()
        extra_half(3, 1, 1).wait_recv()

    def side_second():
        second_to(1, 1).wait_recv()

    def far_second_direct():
        second_to(2, 2).wait_recv()

    def far_second_lent():
        lent(second_of(3), 10).wait_recv()

    q_own = group // 2
    q_far = 1 - q_own
    near_first = q_own == 0
    single = jnp.logical_not(twofold)
    right = {(place, q): functools.partial(receive_inner, place, q) for place in (0, 3) for q in range(2)}
    events = (
        (single, -1, lists_of_end),
        (twofold, 0, lists_of_end),
        (twofold, 3, right[0, 0]),
        (single, 1, right[0, 0]),
        (True, 3, first_pieces),
        (twofold, 3, own_second),
        (single, 4, second_pieces),
        (single, 5, functools.partial(receive, 0, 1)),
        (single, 7, lambda: relayed(1, 1, source_of(0)).start()),
        (twofold, 5, second_pieces),
        (twofold, 5, right[0, 1]),
        (single, 6, right[3, 0]),
        (twofold, 7, right[3, 0]),
        (single, 9, side_second),
        (single, 7, diagonal),
        (twofold, 9, diagonal),
        (single, 8, far_second_lent),
        (single, 9, right[3, 1]),
        (twofold, 11, far_second_direct),
        (twofold, 12, right[3, 1]),
    )

    late = [(q * col_count + source_of(1)) // 2 == group_at(3) for q in range(2)]
    head = (jnp.where(late[0], 5, 1), jnp.where(late[0] | late[1], 2, 5), jnp.where(late[0], 1, jnp.where(late[1], 5, 2)))
    twofold_jobs = head + (0, 6, 9 + 4 * q_own, 10 + 4 * q_own, 4, 3, 11, 9 + 4 * q_far, 10 + 4 * q_far, 15, 7)
    single_jobs = (
        1 + 4 * q_own,
        9 + 4 * q_own,
        1 + 4 * q_far,
        jnp.where(near_first, 2, 0),
        jnp.where(near_first, 6, 2),
        jnp.where(near_first, 0, 6),
        9 + 4 * q_far,
        4,
        3,
        11,
        10 + 4 * q_far,
        10 + 4 * q_own,
        15,
        7,
    )
    early = jnp.where(folding & single, 2, 0)

    unroll = next(u for u in (96, 48, 32, 16, 8, 4, 2, 1) if pair_count % u == 0)

    def job(item, carry):
        def pick(choices):
            value = jnp.int32(choices[-1])
            for at in range(len(choices) - 1):
                value = jnp.where(item + early == at, choices[at], value)
            return value

        code = jnp.where(
            at_end,
            pick(END_JOBS),
            jnp.where(even, jnp.where(twofold, pick(twofold_jobs), pick(single_jobs)), pick(head + INNER_ODD)),
        )
        place, q, extra = code % 4, code // 4 % 2, code // 8
        source = source_of(place)
        kgroup = q * col_count + source
        owner = jnp.where(extra == 1, near, col)
        step = lax.rem(kgroup - row - owner + 2 * row_count, row_count)
        code_row = step + extra * 2 * step_count
        left_at = extra * row_count + kgroup
        base = extra * slot_count

        @pl.when(at_end & twofold & odd & (item == 4))
        def _():
            own_panel(1, 1).start()

        @pl.when(at_end & odd & (place > 0))
        def _():
            relayed(0, q, source).wait_recv()

        unpacking = folded & (place > 0)

        @pl.when(unpacking)
        def _():
            packed_copy(place, q).wait_recv()

        pl.when(item == jnp.where(early > 0, -1, 0))(first_halves)
        pl.when(item == 0)(second_halves)
        pl.when(item == jnp.where(inner, 2, 0))(rest_of_left)

        for who, at, event in events:
            pl.when(folding & who & (item == at))(event)

        for at, where in ((1, (0, 0)), (4, (3, 0)), (5, (0, 1)), (7, (3, 1))):
            @pl.when(inner & odd & (item == at))
            def _():
                receive_inner(*where)

        def split_left(i):
            x = left_all[left_at, i]
            high = x.astype(jnp.bfloat16)
            lhs[i, :, :blk] = high
            lhs[i, :, blk:] = (x - high.astype(jnp.float32)).astype(jnp.bfloat16)

        batched(left_blocks, split_left)

        def right_of(i, x):
            high = x.astype(jnp.bfloat16)
            rhs[i, :blk, :blk] = high
            rhs[i, blk:, :blk] = high
            rhs[i, :blk, blk:] = (x - high.astype(jnp.float32)).astype(jnp.bfloat16)

        @pl.when(jnp.logical_not(unpacking))
        def _():
            batched(right_blocks, lambda i: right_of(i, right_all[q, source, i]))

        @pl.when(unpacking)
        def _():
            def unpack(i):
                x = packed[jnp.maximum(place - 1, 0) * q_count + q, i]
                right_of(i, jnp.where(lanes < fold, 0.0, pltpu.roll(x, fold, 1)))
                right_of(pack_blocks + i, jnp.where(lanes < fold, 0.0, x))

            batched(pack_blocks, unpack, 2)

        def some(batch, carry):
            total, before = carry
            for u in range(unroll):
                p = batch * unroll + u
                entry = code_ref[code_row, p]
                both = jnp.dot(lhs[entry & 255], rhs[(entry >> 8) & 255], preferred_element_type=jnp.float32)
                slot = entry >> 16
                keep = (slot == before).astype(jnp.float32)
                total = total * keep + (both[:, :blk] + both[:, blk:])
                sums[p] = total
                before = slot
            return total, before

        lax.fori_loop(0, pair_count // unroll, some, (zero, jnp.int32(-1)))

        def put(o):
            entry = code_ref[step_count + code_row, o]
            found = ((entry >> 16) > 0).astype(jnp.float32)
            acc[base + o] = acc[base + o] + sums[jnp.maximum((entry & 65535) - 1, 0)] * found

        batched(slot_count, put)

        @pl.when(folding & (item == 12 - early))
        def _():
            for i in range(PARTS):
                def fold_sum(o, c):
                    moved = pltpu.roll(acc[slot_count + sum_blocks + o], fold, 1)
                    total_in[o] = jnp.where(lanes < fold, acc[slot_count + o], moved)
                    return c

                lax.fori_loop(i * part, (i + 1) * part, fold_sum, 0)
                if i < FIRST_PARTS:
                    partial_sum(i).start()

        return carry

    job_count = jnp.where(
        at_end,
        len(END_JOBS),
        jnp.where(even, len(twofold_jobs), 3 + len(INNER_ODD)),
    )
    lax.fori_loop(-early, job_count - early, job, 0)

    @pl.when(inner & odd)
    def _():
        relayed(0, q_count - 1, source_of(3)).wait_send()
        pl.semaphore_signal(turn_sem, inc=1, device_id=(partner, col), device_id_type=MESH)

    @pl.when(folding)
    def _():
        pl.semaphore_wait(turn_sem, 1)
        for i in range(FIRST_PARTS, PARTS):
            partial_sum(i).start()

    def result(first, size, number):
        where = pl.ds(first, size)
        return pltpu.make_async_copy(acc.at[where], out_ref.at[where], done_sem.at[number])

    @pl.when(folded)
    def _():
        for i in range(PARTS):
            partial_sum(i).wait_recv()

            def add(o):
                x = total_in[i * part + o]
                low_at, high_at = i * part + o, sum_blocks + i * part + o
                acc[low_at] = acc[low_at] + jnp.where(lanes < fold, x, 0.0)
                acc[high_at] = acc[high_at] + jnp.where(lanes < fold, pltpu.roll(x, fold, 1), 0.0)

            batched(part, add)
            result(i * part, part, 2 * i).start()
            result(sum_blocks + i * part, part, 2 * i + 1).start()
        for i in range(PARTS):
            result(i * part, part, 2 * i).wait()
            result(sum_blocks + i * part, part, 2 * i + 1).wait()

    @pl.when(jnp.logical_not(folded))
    def _():
        result(0, slot_count, 0).start()
        result(0, slot_count, 0).wait()

    for q in range(q_count):
        own_panel(1, q).wait_send()

    @pl.when(inner)
    def _():
        for q in range(q_count):
            relayed(1, q, source_of(0)).wait_send()

    @pl.when(inner & odd)
    def _():
        for q in range(q_count):
            own_panel(0, q).wait_send()
            relayed(0, q, source_of(2)).wait_send()
        for q in range(q_count - 1):
            relayed(0, q, source_of(3)).wait_send()

    @pl.when(lending)
    def _():
        lend_first().wait_send()

    @pl.when(folded)
    def _():
        table_out().wait_send()

        @pl.when(twofold)
        def _():
            lend(second_of(0), 7).wait_send()

        @pl.when(jnp.logical_not(twofold))
        def _():
            lend(second_of(3), 10).wait_send()

    @pl.when(folding)
    def _():
        for i in (1, 2):
            for piece in range(2):
                extra_across(i, piece).wait_send()
        extra_half(1, 0, 2).wait_send()
        extra_half(2, 1, 1).wait_send()

        @pl.when(twofold)
        def _():
            second_to(1, 0).wait_send()
            second_to(2, 0).wait_send()

        for place in (1, 2, 3):
            for q in range(q_count):
                packed_copy(place, q).wait_send()
        for i in range(PARTS):
            partial_sum(i).wait_send()

    for i in (1, 2):
        for piece in range(2):
            across(i, piece).wait_send()
    half_of(1, 0, 2).wait_send()
    half_of(2, 1, 1).wait_send()
    for i in range(groups):
        handed(i).wait_send()


def folded_call(row_count, col_count, lists, left_panels, right_panels, width):
    left_blocks, blk = left_panels.shape[2], left_panels.shape[3]
    q_count, right_blocks = right_panels.shape[0], right_panels.shape[3]
    step_count, pair_count = lists.shape[1], lists.shape[2]
    groups = row_count // 2
    dma = pltpu.SemaphoreType.DMA
    out = pl.pallas_call(
        functools.partial(fold_kernel, row_count, col_count),
        out_shape=jax.ShapeDtypeStruct((OCAP, blk, blk), jnp.float32),
        in_specs=[pl.BlockSpec(memory_space=pltpu.HBM)] * 3,
        out_specs=pl.BlockSpec(memory_space=pltpu.HBM),
        scratch_shapes=[
            pltpu.VMEM((2 * row_count, left_blocks, blk, blk), jnp.float32),
            pltpu.VMEM((q_count, col_count, right_blocks, blk, blk), jnp.float32),
            pltpu.VMEM((3 * q_count, right_blocks // 2, blk, blk), jnp.float32),
            pltpu.VMEM((OCAP // 2, blk, blk), jnp.float32),
            pltpu.VMEM((left_blocks, blk, 2 * blk), jnp.bfloat16),
            pltpu.VMEM((right_blocks, 2 * blk, 2 * blk), jnp.bfloat16),
            pltpu.VMEM((pair_count, blk, blk), jnp.float32),
            pltpu.VMEM((2 * OCAP, blk, blk), jnp.float32),
            pltpu.VMEM((2 * step_count, width), jnp.int32),
            pltpu.VMEM((2 * step_count, width), jnp.int32),
            pltpu.SMEM((4 * step_count, width), jnp.int32),
            dma((2, q_count, col_count)),
            dma((q_count, col_count)),
            dma((2, 2)),
            dma((groups,)),
            dma((2,)),
            dma((row_count,)),
            dma((2, 2)),
            dma((2,)),
            dma((11,)),
            dma((8,)),
            dma((2,)),
            dma((3 * q_count,)),
            dma((3 * q_count,)),
            dma((2,)),
            dma((PARTS,)),
            dma((PARTS,)),
            dma((4 + q_count,)),
            dma((2 * PARTS,)),
            pltpu.SemaphoreType.REGULAR,
            pltpu.VMEM(lists.shape, jnp.int32),
        ],
        compiler_params=pltpu.CompilerParams(
            collective_id=0, has_side_effects=True, vmem_limit_bytes=60 * 1024 * 1024
        ),
    )(lists, left_panels, right_panels)
    return out[None, None]


def shards(row_count, col_count, left_panels, right_panels, product_lists):
    left_blocks, blk = left_panels.shape[2], left_panels.shape[3]
    q_count, right_blocks = right_panels.shape[0], right_panels.shape[3]
    pair_count = product_lists.shape[3]
    lists = jnp.transpose(product_lists[0, 0], (2, 0, 1))
    step_count = lists.shape[1]
    width = pl.cdiv(max(pair_count, OCAP), 128) * 128
    groups = row_count // 2
    if groups == 4 and col_count == 4 and q_count * col_count == row_count == step_count and OCAP % (2 * PARTS) == 0 and right_blocks % 2 == 0:
        return folded_call(row_count, col_count, lists, left_panels, right_panels, width)
    out = pl.pallas_call(
        functools.partial(kernel, row_count, col_count),
        out_shape=jax.ShapeDtypeStruct((OCAP, blk, blk), jnp.float32),
        in_specs=[pl.BlockSpec(memory_space=pltpu.VMEM)] + [pl.BlockSpec(memory_space=pltpu.HBM)] * 2,
        out_specs=pl.BlockSpec(memory_space=pltpu.VMEM),
        scratch_shapes=[
            pltpu.VMEM((row_count, left_blocks, blk, blk), jnp.float32),
            pltpu.VMEM((q_count, col_count, right_blocks, blk, blk), jnp.float32),
            pltpu.VMEM((left_blocks, blk, 2 * blk), jnp.bfloat16),
            pltpu.VMEM((right_blocks, 2 * blk, 2 * blk), jnp.bfloat16),
            pltpu.VMEM((pair_count, blk, blk), jnp.float32),
            pltpu.VMEM((2 * step_count, width), jnp.int32),
            pltpu.SMEM((2 * step_count, width), jnp.int32),
            pltpu.SemaphoreType.DMA((2, q_count, col_count)),
            pltpu.SemaphoreType.DMA((q_count, col_count)),
            pltpu.SemaphoreType.DMA((groups,)),
            pltpu.SemaphoreType.DMA((groups,)),
            pltpu.SemaphoreType.DMA((2,)),
            pltpu.SemaphoreType.DMA((row_count,)),
            pltpu.SemaphoreType.DMA((2,)),
            pltpu.SemaphoreType.DMA((2 + q_count,)),
        ],
        compiler_params=pltpu.CompilerParams(
            collective_id=0, has_side_effects=True, vmem_limit_bytes=50 * 1024 * 1024
        ),
    )(lists, left_panels, right_panels)
    return out[None, None]


def solution(mesh):
    return jax.shard_map(
        functools.partial(shards, mesh.shape["row"], mesh.shape["col"]),
        mesh=mesh,
        in_specs=(
            P("row", "col", None, None, None),
            P(None, "col", "row", None, None, None),
            P("row", "col", None, None, None),
        ),
        out_specs=P("row", "col", None, None, None),
        check_vma=False,
    )
```

```python
import functools

import jax
import jax.numpy as jnp
from jax import lax
from jax.experimental import pallas as pl
from jax.experimental.pallas import tpu as pltpu
from jax.sharding import PartitionSpec as P

OCAP = 24
UNROLL = 16
AHEAD = 3
MESH = pl.DeviceIdType.MESH
PARTS = 6
FIRST_PARTS = 2
END_JOBS = (0, 4, 1, 5, 2, 6, 3, 7)
INNER_ODD = (6, 3, 0, 4, 7)


def arrange(lists_ref, table, step, slot_count):
    step_count, count = lists_ref.shape[1], lists_ref.shape[2]
    width = table.shape[1]
    left, right, out = (lists_ref[part, pl.ds(step, 1), :] for part in range(3))
    live = left >= 0
    slots = jnp.where(live, out, slot_count)
    lane = lax.broadcasted_iota(jnp.int32, (count, count), 1)
    same = lax.broadcasted_iota(jnp.int32, (count, count), 0) == lane

    def column(row):
        return jnp.sum(jnp.where(same, jnp.broadcast_to(row, (count, count)), 0), axis=1, keepdims=True)

    key = jnp.broadcast_to(slots, (count, count)) * count + lane
    key_column = jnp.sum(jnp.where(same, key, 0), axis=1, keepdims=True)
    rank = jnp.sum((key < key_column).astype(jnp.int32), axis=1, keepdims=True)
    packed = column(jnp.where(live, left + right * 256, 0) + slots * 65536)
    wide = lax.broadcasted_iota(jnp.int32, (count, width), 1)
    table[pl.ds(step, 1), :] = jnp.sum(jnp.where(rank == wide, packed, 0), axis=0, keepdims=True)
    slot_column = column(slots)
    upto = (slot_column <= wide).astype(jnp.int32) + (slot_column == wide).astype(jnp.int32) * 65536
    table[pl.ds(step_count + step, 1), :] = jnp.sum(upto, axis=0, keepdims=True)


def kernel(row_count, col_count, lists_ref, left_ref, right_ref, out_ref,
           left_all, right_all, lhs, rhs, sums, table, code_ref, zsend, zrecv, lsend, psend, hsend, lrecv, hrecv, local_sem):
    row = lax.axis_index("row")
    col = lax.axis_index("col")
    q_count = right_ref.shape[0]
    left_blocks, blk = left_ref.shape[2], left_ref.shape[3]
    right_blocks = right_ref.shape[3]
    step_count, pair_count = lists_ref.shape[1], lists_ref.shape[2]
    slot_count = out_ref.shape[0]
    groups = row_count // 2
    group, parity = row // 2, row % 2
    partner = group * 2 + 1 - parity
    square = groups == 4
    direct = (1, 2) if square else tuple(range(1, groups))

    def group_at(i):
        return (group // 2 * 2 + 1 - group % 2 if i == 1 else lax.rem(group + 2, groups)) if square and i in (1, 2) else (
            groups - 1 - group if square and i == 3 else lax.rem(group + i, groups))

    def row_at(i, same):
        return group_at(i) * 2 + (parity if same else 1 - parity)

    barrier = pltpu.get_barrier_semaphore()
    for i in direct:
        pl.semaphore_signal(barrier, inc=1, device_id=(row_at(i, True), col), device_id_type=MESH)
    pl.semaphore_signal(barrier, inc=1, device_id=(partner, col), device_id_type=MESH)

    @pl.when(col > 0)
    def _():
        pl.semaphore_signal(barrier, inc=1, device_id=(row, col - 1), device_id_type=MESH)

    @pl.when(col < col_count - 1)
    def _():
        pl.semaphore_signal(barrier, inc=1, device_id=(row, col + 1), device_id_type=MESH)

    own = [pltpu.make_async_copy(left_ref.at[0, 0], left_all.at[row], local_sem.at[0])]
    for q in range(q_count):
        own.append(pltpu.make_async_copy(right_ref.at[q, 0, 0], right_all.at[q, col], local_sem.at[1 + q]))
    for copy in own:
        copy.start()

    ends = (col == 0).astype(jnp.int32) + (col == col_count - 1).astype(jnp.int32)
    pl.semaphore_wait(barrier, len(direct) + 3 - ends)

    def along(direction, q, source, from_ref):
        return pltpu.make_async_remote_copy(
            src_ref=from_ref,
            dst_ref=right_all.at[q, source],
            send_sem=zsend.at[direction, q, source],
            recv_sem=zrecv.at[q, source],
            device_id=(row, col + (1 if direction else -1)),
            device_id_type=MESH,
        )

    def own_panel(direction, q):
        return along(direction, q, col, right_ref.at[q, 0, 0])

    def relayed(direction, q, source):
        return along(direction, q, source, right_all.at[q, source])

    def across(i):
        return pltpu.make_async_remote_copy(
            src_ref=left_ref.at[0, 0],
            dst_ref=left_all.at[row],
            send_sem=lsend.at[i],
            recv_sem=lrecv.at[row],
            device_id=(row_at(i, True), col),
            device_id_type=MESH,
        )

    def handed(i):
        source = row_at(i, True)
        return pltpu.make_async_remote_copy(
            src_ref=left_ref.at[0, 0] if i == 0 else left_all.at[source],
            dst_ref=left_all.at[source],
            send_sem=psend.at[i],
            recv_sem=lrecv.at[source],
            device_id=(partner, col),
            device_id_type=MESH,
        )

    def arrived_left(source):
        return pltpu.make_async_remote_copy(
            src_ref=left_all.at[source],
            dst_ref=left_all.at[source],
            send_sem=psend.at[0],
            recv_sem=lrecv.at[source],
            device_id=(partner, col),
            device_id_type=MESH,
        )

    half = left_blocks // 2
    pieces = (pl.ds(0, half), pl.ds(half, left_blocks - half))

    def half_of(i, piece, target):
        source = row_at(i, True)
        return pltpu.make_async_remote_copy(
            src_ref=left_all.at[source, pieces[piece]],
            dst_ref=left_all.at[source, pieces[piece]],
            send_sem=hsend.at[piece],
            recv_sem=hrecv.at[piece],
            device_id=(row_at(target, True), col),
            device_id_type=MESH,
        )

    for q in range(q_count):
        @pl.when(col > 0)
        def _():
            own_panel(0, q).start()

        @pl.when(col < col_count - 1)
        def _():
            own_panel(1, q).start()

    for i in direct:
        across(i).start()
    handed(0).start()

    lax.fori_loop(0, step_count, lambda step, c: (arrange(lists_ref, table, step, slot_count), c)[1], 0)
    out_ref[...] = jnp.zeros_like(out_ref)
    rhs[:, blk:, blk:] = jnp.zeros((right_blocks, blk, blk), rhs.dtype)
    for copy in own:
        copy.wait()

    sides = jnp.minimum(col, col_count - 1 - col)

    def item_of(item):
        rest = item - q_count
        later = rest - 2 * q_count * sides
        both = later < 0
        distance = jnp.where(both, rest // (2 * q_count) + 1, sides + 1 + later // q_count)
        q = jnp.where(both, rest % (2 * q_count) // 2, later % q_count)
        lower = jnp.where(both, rest % 2 == 0, col * 2 > col_count - 1)
        source = jnp.where(lower, col - distance, col + distance)
        own_item = rest < 0
        return jnp.where(own_item, col, source), jnp.where(own_item, item, q)

    def relay(item):
        source, q = item_of(item)

        @pl.when(source != col)
        def _():
            relayed(0, q, source).wait_recv()

        @pl.when((source < col) & (col < col_count - 1))
        def _():
            relayed(1, q, source).start()

        @pl.when((source > col) & (col > 0))
        def _():
            relayed(0, q, source).start()

    forwards = 1 - ends
    first = q_count * (2 + jnp.minimum(sides, 1))

    def relay_many(start, stop):
        lax.fori_loop(start, stop, lambda item, c: (relay(item), c)[1], 0)

    for i in direct:
        arrived_left(row_at(i, True)).wait_recv()
        if square:
            half_of(i, i - 1, 3 - i).start()
        handed(i).start()
    relay_many(q_count, first)
    listed = pltpu.make_async_copy(table, code_ref, local_sem.at[1 + q_count])
    listed.start()
    if square:
        half_of(3, 0, 1).wait_recv()
        half_of(3, 1, 1).wait_recv()
        handed(3).start()
    for i in range(groups):
        arrived_left(row_at(i, False)).wait_recv()
    listed.wait()

    def job(item, carry):
        source, q = item_of(item)
        kgroup = q * col_count + source
        step = lax.rem(kgroup - row - col + 2 * row_count, row_count)

        @pl.when(step < step_count)
        def _():
            def split_left(i, c):
                x = left_all[kgroup, i]
                high = x.astype(jnp.bfloat16)
                lhs[i, :, :blk] = high
                lhs[i, :, blk:] = (x - high.astype(jnp.float32)).astype(jnp.bfloat16)
                return c

            lax.fori_loop(0, left_blocks, split_left, 0)

        ahead = item + AHEAD * forwards

        @pl.when((ahead >= first) & (ahead < row_count))
        def _():
            relay(ahead)

        @pl.when(step < step_count)
        def _():
            def split_right(i, c):
                x = right_all[q, source, i]
                high = x.astype(jnp.bfloat16)
                rhs[i, :blk, :blk] = high
                rhs[i, blk:, :blk] = high
                rhs[i, :blk, blk:] = (x - high.astype(jnp.float32)).astype(jnp.bfloat16)
                return c

            lax.fori_loop(0, right_blocks, split_right, 0)

            def some(batch, carry):
                total, before = carry
                for u in range(UNROLL):
                    p = batch * UNROLL + u
                    code = code_ref[step, p]
                    both = jnp.dot(
                        lhs[code & 255], rhs[(code >> 8) & 255], preferred_element_type=jnp.float32
                    )
                    slot = code >> 16
                    keep = (slot == before).astype(jnp.float32)
                    total = total * keep + (both[:, :blk] + both[:, blk:])
                    sums[p] = total
                    before = slot
                return total, before

            lax.fori_loop(0, pair_count // UNROLL, some, (jnp.zeros((blk, blk), jnp.float32), jnp.int32(-1)))

            def put(o, c):
                code = code_ref[step_count + step, o]
                found = ((code >> 16) > 0).astype(jnp.float32)
                out_ref[o] = out_ref[o] + sums[jnp.maximum((code & 65535) - 1, 0)] * found
                return c

            lax.fori_loop(0, slot_count, put, 0)

        return carry

    lax.fori_loop(0, row_count, job, 0)

    for q in range(q_count):
        @pl.when(col > 0)
        def _():
            own_panel(0, q).wait_send()

        @pl.when(col < col_count - 1)
        def _():
            own_panel(1, q).wait_send()

    def sent(item, carry):
        source, q = item_of(item)

        @pl.when((source < col) & (col < col_count - 1))
        def _():
            relayed(1, q, source).wait_send()

        @pl.when((source > col) & (col > 0))
        def _():
            relayed(0, q, source).wait_send()

        return carry

    lax.fori_loop(q_count, row_count, sent, 0)
    for i in direct:
        across(i).wait_send()
    if square:
        half_of(1, 0, 2).wait_send()
        half_of(2, 1, 1).wait_send()
    for i in range(groups):
        handed(i).wait_send()


def batched(count, body, most=4):
    width = next(w for w in range(most, 0, -1) if count % w == 0)

    def batch(i, c):
        for u in range(width):
            body(i * width + u)
        return c

    lax.fori_loop(0, count // width, batch, 0)


def fold_kernel(row_count, col_count, lists_in, left_ref, right_ref, out_ref,
                left_all, right_all, packed, total_in, lhs, rhs, sums, acc, table, table_in, code_ref,
                zsend, zrecv, lsend, psend, hsend, lrecv, precv, hrecv, esend, erecv, ehrecv, bsend, brecv, tsem, ssend, srecv, local_sem, done_sem, turn_sem, lists_ref):
    row = lax.axis_index("row")
    col = lax.axis_index("col")
    q_count = right_ref.shape[0]
    left_blocks, blk = left_ref.shape[2], left_ref.shape[3]
    right_blocks = right_ref.shape[3]
    step_count, pair_count = lists_in.shape[1], lists_in.shape[2]
    slot_count = out_ref.shape[0]
    groups = row_count // 2
    group, parity = row // 2, row % 2
    partner = group * 2 + 1 - parity
    low = col * 2 < col_count
    at_end = (col == 0) | (col == col_count - 1)
    even = parity == 0
    odd = parity == 1
    inward = jnp.where(low, col + 1, col - 1)
    outward = jnp.where(low, col - 1, col + 1)
    near = jnp.where(low, 0, col_count - 1)

    def source_of(place):
        return jnp.where(low, place, col_count - 1 - place)

    def group_at(i):
        return (group, group // 2 * 2 + 1 - group % 2, lax.rem(group + 2, groups), groups - 1 - group)[i]

    def row_at(i, same):
        return group_at(i) * 2 + (parity if same else 1 - parity)

    barrier = pltpu.get_barrier_semaphore()
    for i in (1, 2):
        pl.semaphore_signal(barrier, inc=1, device_id=(row_at(i, True), col), device_id_type=MESH)
    pl.semaphore_signal(barrier, inc=1, device_id=(partner, col), device_id_type=MESH)
    pl.semaphore_signal(barrier, inc=1, device_id=(row, inward), device_id_type=MESH)

    @pl.when(jnp.logical_not(at_end))
    def _():
        pl.semaphore_signal(barrier, inc=1, device_id=(row, outward), device_id_type=MESH)

    @pl.when((col == 1) & even)
    def _():
        pl.semaphore_signal(barrier, inc=1, device_id=(row + 1, 0), device_id_type=MESH)

    own = [pltpu.make_async_copy(left_ref.at[0, 0], left_all.at[row], local_sem.at[0])]
    for q in range(q_count):
        own.append(pltpu.make_async_copy(right_ref.at[q, 0, 0], right_all.at[q, col], local_sem.at[1 + q]))
    for copy in own:
        copy.start()
    entries = pltpu.make_async_copy(lists_in, lists_ref, local_sem.at[3 + q_count])
    entries.start()
    pl.semaphore_wait(barrier, jnp.where(at_end & ((col > 0) | even), 4, 5))

    def panel(direction, q, source, from_ref):
        return pltpu.make_async_remote_copy(
            src_ref=from_ref,
            dst_ref=right_all.at[q, source],
            send_sem=zsend.at[direction, q, source],
            recv_sem=zrecv.at[q, source],
            device_id=(row, inward if direction else outward),
            device_id_type=MESH,
        )

    def own_panel(direction, q):
        return panel(direction, q, col, right_ref.at[q, 0, 0])

    def relayed(direction, q, source):
        return panel(direction, q, source, right_all.at[q, source])

    def left_copy(source_ref, index, send_sem, recv_sem, device):
        return pltpu.make_async_remote_copy(
            src_ref=source_ref,
            dst_ref=left_all.at[index],
            send_sem=send_sem,
            recv_sem=recv_sem,
            device_id=device,
            device_id_type=MESH,
        )

    def handed(i):
        source = row_at(i, True)
        return left_copy(left_ref.at[0, 0] if i == 0 else left_all.at[source], source,
                         psend.at[i], lrecv.at[source], (partner, col))

    def arrived_left(source):
        return left_copy(left_all.at[source], source, psend.at[0], lrecv.at[source], (partner, col))

    half = left_blocks // 2
    pieces = (pl.ds(0, half), pl.ds(half, left_blocks - half))

    def across(i, piece):
        return pltpu.make_async_remote_copy(
            src_ref=left_ref.at[0, 0, pieces[piece]],
            dst_ref=left_all.at[row, pieces[piece]],
            send_sem=lsend.at[i - 1, piece],
            recv_sem=precv.at[i - 1, piece],
            device_id=(row_at(i, True), col),
            device_id_type=MESH,
        )

    def half_copy(index, piece, send_sem, recv_sem, target):
        return pltpu.make_async_remote_copy(
            src_ref=left_all.at[index, pieces[piece]],
            dst_ref=left_all.at[index, pieces[piece]],
            send_sem=send_sem,
            recv_sem=recv_sem,
            device_id=(row_at(target, True), col),
            device_id_type=MESH,
        )

    def half_of(i, piece, target):
        return half_copy(row_at(i, True), piece, hsend.at[piece], hrecv.at[piece], target)

    def first_of(i):
        return group_at(i) * 2 + (near == 0).astype(jnp.int32)

    def second_of(i):
        return group_at(i) * 2 + (near != 0).astype(jnp.int32)

    def lend_first():
        index = row_count + first_of(0)
        return left_copy(left_ref.at[0, 0], index, esend.at[0], erecv.at[0], (group * 2, inward))

    def lend(index, number):
        return left_copy(left_all.at[index], row_count + index, esend.at[number], erecv.at[{7: 5, 10: 7}[number]], (row, inward))

    def lent(index, number):
        at = row_count + index
        return left_copy(left_all.at[at], at, esend.at[number], erecv.at[{0: 0, 7: 5, 10: 7}[number]], (row_at(1, True), col))

    def extra_across(i, piece):
        return half_copy(row_count + first_of(0), piece, esend.at[2 * i + piece - 1], erecv.at[2 * i + piece - 1], i)

    def extra_half(i, piece, target):
        return half_copy(row_count + first_of(i), piece, esend.at[5 + piece], ehrecv.at[piece], target)

    def second_to(i, owner):
        at = row_count + second_of(owner)
        return left_copy(left_all.at[at], at, esend.at[7 + i], erecv.at[5 + i], (row_at(i, True), col))

    fold = blk // 2
    lanes = lax.broadcasted_iota(jnp.int32, (blk, blk), 1)
    pack_blocks = right_blocks // 2

    def packed_copy(place, q):
        index = (place - 1) * q_count + q
        return pltpu.make_async_remote_copy(
            src_ref=packed.at[index],
            dst_ref=packed.at[index],
            send_sem=bsend.at[index],
            recv_sem=brecv.at[index],
            device_id=(row, near),
            device_id_type=MESH,
        )

    def pack(place, q):
        index = (place - 1) * q_count + q
        source = source_of(place)

        def one(b, c):
            moved = pltpu.roll(right_all[q, source, b], fold, 1)
            packed[index, b] = jnp.where(lanes < fold, moved, right_all[q, source, pack_blocks + b])
            return c

        lax.fori_loop(0, pack_blocks, one, 0)
        packed_copy(place, q).start()

    def table_out():
        return pltpu.make_async_remote_copy(
            src_ref=table,
            dst_ref=table_in,
            send_sem=tsem.at[0],
            recv_sem=tsem.at[1],
            device_id=(row, inward),
            device_id_type=MESH,
        )

    sum_blocks = slot_count // 2
    part = sum_blocks // PARTS

    def partial_sum(i):
        where = pl.ds(i * part, part)
        return pltpu.make_async_remote_copy(
            src_ref=total_in.at[where],
            dst_ref=total_in.at[where],
            send_sem=ssend.at[i],
            recv_sem=srecv.at[i],
            device_id=(row, near),
            device_id_type=MESH,
        )

    inner = jnp.logical_not(at_end)
    folding = inner & even
    folded = at_end & even
    lending = at_end & (row == first_of(0))
    twofold = (group % 2 == 1) == (near == 0)

    @pl.when(inner & odd)
    def _():
        for q in range(q_count):
            own_panel(0, q).start()

    @pl.when(inner)
    def _():
        for q in range(q_count):
            own_panel(1, q).start()

    @pl.when(lending)
    def _():
        lend_first().start()

    handed(0).start()
    for piece in range(2):
        for i in (1, 2):
            across(i, (i - 1 + piece) % 2).start()
    for copy in own:
        copy.wait()
    arrived_left(partner).wait_recv()

    entries.wait()
    lax.fori_loop(0, step_count, lambda step, c: (arrange(lists_ref, table, step, slot_count), c)[1], 0)

    @pl.when(folded)
    def _():
        table_out().start()

    @pl.when(lending)
    def _():
        own_panel(1, 0).start()

    @pl.when(folding)
    def _():
        for q in range(q_count):
            pack(1, q)

    listed = pltpu.make_async_copy(table, code_ref.at[pl.ds(0, 2 * step_count)], local_sem.at[1 + q_count])
    listed.start()
    zero = jnp.zeros((blk, blk), jnp.float32)

    def clear(o, c):
        acc[o] = zero
        return c

    lax.fori_loop(0, jnp.where(folding, 2 * slot_count, slot_count), clear, 0)
    rhs[:, blk:, blk:] = jnp.zeros((right_blocks, blk, blk), rhs.dtype)

    def receive(place, q):
        relayed(0, q, source_of(place)).wait_recv()

    def receive_inner(place, q):
        receive(place, q)
        if place == 0:
            relayed(1, q, source_of(place)).start()
        else:
            @pl.when(odd)
            def _():
                relayed(0, q, source_of(place)).start()

            @pl.when(even)
            def _():
                pack(place, q)

    def first_halves():
        for i in (1, 2):
            across(i, i - 1).wait_recv()
            half_of(i, i - 1, 3 - i).start()

        @pl.when(at_end & jnp.logical_not(lending))
        def _():
            own_panel(1, 0).start()

        @pl.when(folded & twofold)
        def _():
            lend(second_of(0), 7).start()
            own_panel(1, 1).start()

        @pl.when(folding)
        def _():
            lent(first_of(0), 0).wait_recv()
            for piece in range(2):
                for i in (1, 2):
                    extra_across(i, (i - 1 + piece) % 2).start()

    def second_halves():
        @pl.when(inner)
        def _():
            receive_inner(2, 0)

        for i in (1, 2):
            across(i, 2 - i).wait_recv()
            handed(i).start()

        for i in (1, 2):
            arrived_left(row_at(i, False)).wait_recv()

        @pl.when(at_end & odd & jnp.logical_not(twofold))
        def _():
            own_panel(1, 1).start()

    listed.wait()

    def rest_of_left():
        half_of(3, 0, 1).wait_recv()
        half_of(3, 1, 1).wait_recv()
        handed(3).start()

        @pl.when(inner)
        def _():
            receive_inner(2, 1)

        arrived_left(row_at(3, False)).wait_recv()

        @pl.when(folded & jnp.logical_not(twofold))
        def _():
            own_panel(1, 1).start()
            lend(second_of(3), 10).start()

    def own_second():
        @pl.when(twofold)
        def _():
            lent(second_of(0), 7).wait_recv()
            second_to(1, 0).start()
            second_to(2, 0).start()

    def lists_of_end():
        table_out().wait_recv()
        fetched = pltpu.make_async_copy(table_in, code_ref.at[pl.ds(2 * step_count, 2 * step_count)], local_sem.at[2 + q_count])
        fetched.start()
        fetched.wait()

    def first_pieces():
        for i in (1, 2):
            extra_across(i, i - 1).wait_recv()
            extra_half(i, i - 1, 3 - i).start()

    def own_second():
        lent(second_of(0), 7).wait_recv()
        second_to(1, 0).start()
        second_to(2, 0).start()

    def second_pieces():
        for i in (1, 2):
            extra_across(i, 2 - i).wait_recv()

    def diagonal():
        extra_half(3, 0, 1).wait_recv()
        extra_half(3, 1, 1).wait_recv()

    def side_second():
        second_to(1, 1).wait_recv()

    def far_second_direct():
        second_to(2, 2).wait_recv()

    def far_second_lent():
        lent(second_of(3), 10).wait_recv()

    q_own = group // 2
    q_far = 1 - q_own
    near_first = q_own == 0
    single = jnp.logical_not(twofold)
    right = {(place, q): functools.partial(receive_inner, place, q) for place in (0, 3) for q in range(2)}
    events = (
        (single, -1, lists_of_end),
        (twofold, 0, lists_of_end),
        (twofold, 3, right[0, 0]),
        (single, 1, right[0, 0]),
        (True, 3, first_pieces),
        (twofold, 3, own_second),
        (single, 4, second_pieces),
        (single, 5, functools.partial(receive, 0, 1)),
        (single, 7, lambda: relayed(1, 1, source_of(0)).start()),
        (twofold, 5, second_pieces),
        (twofold, 5, right[0, 1]),
        (single, 6, right[3, 0]),
        (twofold, 7, right[3, 0]),
        (single, 9, side_second),
        (single, 7, diagonal),
        (twofold, 9, diagonal),
        (single, 8, far_second_lent),
        (single, 9, right[3, 1]),
        (twofold, 11, far_second_direct),
        (twofold, 12, right[3, 1]),
    )

    late = [(q * col_count + source_of(1)) // 2 == group_at(3) for q in range(2)]
    head = (jnp.where(late[0], 5, 1), jnp.where(late[0] | late[1], 2, 5), jnp.where(late[0], 1, jnp.where(late[1], 5, 2)))
    twofold_jobs = head + (0, 6, 9 + 4 * q_own, 10 + 4 * q_own, 4, 3, 11, 9 + 4 * q_far, 10 + 4 * q_far, 15, 7)
    single_jobs = (
        1 + 4 * q_own,
        9 + 4 * q_own,
        1 + 4 * q_far,
        jnp.where(near_first, 2, 0),
        jnp.where(near_first, 6, 2),
        jnp.where(near_first, 0, 6),
        9 + 4 * q_far,
        4,
        3,
        11,
        10 + 4 * q_far,
        10 + 4 * q_own,
        15,
        7,
    )
    early = jnp.where(folding & single, 2, 0)

    unroll = next(u for u in (96, 48, 32, 16, 8, 4, 2, 1) if pair_count % u == 0)

    def job(item, carry):
        def pick(choices):
            value = jnp.int32(choices[-1])
            for at in range(len(choices) - 1):
                value = jnp.where(item + early == at, choices[at], value)
            return value

        code = jnp.where(
            at_end,
            pick(END_JOBS),
            jnp.where(even, jnp.where(twofold, pick(twofold_jobs), pick(single_jobs)), pick(head + INNER_ODD)),
        )
        place, q, extra = code % 4, code // 4 % 2, code // 8
        source = source_of(place)
        kgroup = q * col_count + source
        owner = jnp.where(extra == 1, near, col)
        step = lax.rem(kgroup - row - owner + 2 * row_count, row_count)
        code_row = step + extra * 2 * step_count
        left_at = extra * row_count + kgroup
        base = extra * slot_count

        @pl.when(at_end & twofold & odd & (item == 4))
        def _():
            own_panel(1, 1).start()

        @pl.when(at_end & odd & (place > 0))
        def _():
            relayed(0, q, source).wait_recv()

        unpacking = folded & (place > 0)

        @pl.when(unpacking)
        def _():
            packed_copy(place, q).wait_recv()

        pl.when(item == jnp.where(early > 0, -1, 0))(first_halves)
        pl.when(item == 0)(second_halves)
        pl.when(item == jnp.where(inner, 2, 0))(rest_of_left)

        for who, at, event in events:
            pl.when(folding & who & (item == at))(event)

        for at, where in ((1, (0, 0)), (4, (3, 0)), (5, (0, 1)), (7, (3, 1))):
            @pl.when(inner & odd & (item == at))
            def _():
                receive_inner(*where)

        def split_left(i):
            x = left_all[left_at, i]
            high = x.astype(jnp.bfloat16)
            lhs[i, :, :blk] = high
            lhs[i, :, blk:] = (x - high.astype(jnp.float32)).astype(jnp.bfloat16)

        batched(left_blocks, split_left)

        def right_of(i, x):
            high = x.astype(jnp.bfloat16)
            rhs[i, :blk, :blk] = high
            rhs[i, blk:, :blk] = high
            rhs[i, :blk, blk:] = (x - high.astype(jnp.float32)).astype(jnp.bfloat16)

        @pl.when(jnp.logical_not(unpacking))
        def _():
            batched(right_blocks, lambda i: right_of(i, right_all[q, source, i]))

        @pl.when(unpacking)
        def _():
            def unpack(i):
                x = packed[jnp.maximum(place - 1, 0) * q_count + q, i]
                right_of(i, jnp.where(lanes < fold, 0.0, pltpu.roll(x, fold, 1)))
                right_of(pack_blocks + i, jnp.where(lanes < fold, 0.0, x))

            batched(pack_blocks, unpack, 2)

        def some(batch, carry):
            total, before = carry
            for u in range(unroll):
                p = batch * unroll + u
                entry = code_ref[code_row, p]
                both = jnp.dot(lhs[entry & 255], rhs[(entry >> 8) & 255], preferred_element_type=jnp.float32)
                slot = entry >> 16
                keep = (slot == before).astype(jnp.float32)
                total = total * keep + (both[:, :blk] + both[:, blk:])
                sums[p] = total
                before = slot
            return total, before

        lax.fori_loop(0, pair_count // unroll, some, (zero, jnp.int32(-1)))

        def put(o):
            entry = code_ref[step_count + code_row, o]
            found = ((entry >> 16) > 0).astype(jnp.float32)
            acc[base + o] = acc[base + o] + sums[jnp.maximum((entry & 65535) - 1, 0)] * found

        batched(slot_count, put)

        @pl.when(folding & (item == 12 - early))
        def _():
            for i in range(PARTS):
                def fold_sum(o, c):
                    moved = pltpu.roll(acc[slot_count + sum_blocks + o], fold, 1)
                    total_in[o] = jnp.where(lanes < fold, acc[slot_count + o], moved)
                    return c

                lax.fori_loop(i * part, (i + 1) * part, fold_sum, 0)
                if i < FIRST_PARTS:
                    partial_sum(i).start()

        return carry

    job_count = jnp.where(
        at_end,
        len(END_JOBS),
        jnp.where(even, len(twofold_jobs), 3 + len(INNER_ODD)),
    )
    lax.fori_loop(-early, job_count - early, job, 0)

    @pl.when(inner & odd)
    def _():
        relayed(0, q_count - 1, source_of(3)).wait_send()
        pl.semaphore_signal(turn_sem, inc=1, device_id=(partner, col), device_id_type=MESH)

    @pl.when(folding)
    def _():
        pl.semaphore_wait(turn_sem, 1)
        for i in range(FIRST_PARTS, PARTS):
            partial_sum(i).start()

    def result(first, size, number):
        where = pl.ds(first, size)
        return pltpu.make_async_copy(acc.at[where], out_ref.at[where], done_sem.at[number])

    @pl.when(folded)
    def _():
        for i in range(PARTS):
            partial_sum(i).wait_recv()

            def add(o):
                x = total_in[i * part + o]
                low_at, high_at = i * part + o, sum_blocks + i * part + o
                acc[low_at] = acc[low_at] + jnp.where(lanes < fold, x, 0.0)
                acc[high_at] = acc[high_at] + jnp.where(lanes < fold, pltpu.roll(x, fold, 1), 0.0)

            batched(part, add)
            result(i * part, part, 2 * i).start()
            result(sum_blocks + i * part, part, 2 * i + 1).start()
        for i in range(PARTS):
            result(i * part, part, 2 * i).wait()
            result(sum_blocks + i * part, part, 2 * i + 1).wait()

    @pl.when(jnp.logical_not(folded))
    def _():
        result(0, slot_count, 0).start()
        result(0, slot_count, 0).wait()

    for q in range(q_count):
        own_panel(1, q).wait_send()

    @pl.when(inner)
    def _():
        for q in range(q_count):
            relayed(1, q, source_of(0)).wait_send()

    @pl.when(inner & odd)
    def _():
        for q in range(q_count):
            own_panel(0, q).wait_send()
            relayed(0, q, source_of(2)).wait_send()
        for q in range(q_count - 1):
            relayed(0, q, source_of(3)).wait_send()

    @pl.when(lending)
    def _():
        lend_first().wait_send()

    @pl.when(folded)
    def _():
        table_out().wait_send()

        @pl.when(twofold)
        def _():
            lend(second_of(0), 7).wait_send()

        @pl.when(jnp.logical_not(twofold))
        def _():
            lend(second_of(3), 10).wait_send()

    @pl.when(folding)
    def _():
        for i in (1, 2):
            for piece in range(2):
                extra_across(i, piece).wait_send()
        extra_half(1, 0, 2).wait_send()
        extra_half(2, 1, 1).wait_send()

        @pl.when(twofold)
        def _():
            second_to(1, 0).wait_send()
            second_to(2, 0).wait_send()

        for place in (1, 2, 3):
            for q in range(q_count):
                packed_copy(place, q).wait_send()
        for i in range(PARTS):
            partial_sum(i).wait_send()

    for i in (1, 2):
        for piece in range(2):
            across(i, piece).wait_send()
    half_of(1, 0, 2).wait_send()
    half_of(2, 1, 1).wait_send()
    for i in range(groups):
        handed(i).wait_send()


def folded_call(row_count, col_count, lists, left_panels, right_panels, width):
    left_blocks, blk = left_panels.shape[2], left_panels.shape[3]
    q_count, right_blocks = right_panels.shape[0], right_panels.shape[3]
    step_count, pair_count = lists.shape[1], lists.shape[2]
    groups = row_count // 2
    dma = pltpu.SemaphoreType.DMA
    out = pl.pallas_call(
        functools.partial(fold_kernel, row_count, col_count),
        out_shape=jax.ShapeDtypeStruct((OCAP, blk, blk), jnp.float32),
        in_specs=[pl.BlockSpec(memory_space=pltpu.HBM)] * 3,
        out_specs=pl.BlockSpec(memory_space=pltpu.HBM),
        scratch_shapes=[
            pltpu.VMEM((2 * row_count, left_blocks, blk, blk), jnp.float32),
            pltpu.VMEM((q_count, col_count, right_blocks, blk, blk), jnp.float32),
            pltpu.VMEM((3 * q_count, right_blocks // 2, blk, blk), jnp.float32),
            pltpu.VMEM((OCAP // 2, blk, blk), jnp.float32),
            pltpu.VMEM((left_blocks, blk, 2 * blk), jnp.bfloat16),
            pltpu.VMEM((right_blocks, 2 * blk, 2 * blk), jnp.bfloat16),
            pltpu.VMEM((pair_count, blk, blk), jnp.float32),
            pltpu.VMEM((2 * OCAP, blk, blk), jnp.float32),
            pltpu.VMEM((2 * step_count, width), jnp.int32),
            pltpu.VMEM((2 * step_count, width), jnp.int32),
            pltpu.SMEM((4 * step_count, width), jnp.int32),
            dma((2, q_count, col_count)),
            dma((q_count, col_count)),
            dma((2, 2)),
            dma((groups,)),
            dma((2,)),
            dma((row_count,)),
            dma((2, 2)),
            dma((2,)),
            dma((11,)),
            dma((8,)),
            dma((2,)),
            dma((3 * q_count,)),
            dma((3 * q_count,)),
            dma((2,)),
            dma((PARTS,)),
            dma((PARTS,)),
            dma((4 + q_count,)),
            dma((2 * PARTS,)),
            pltpu.SemaphoreType.REGULAR,
            pltpu.VMEM(lists.shape, jnp.int32),
        ],
        compiler_params=pltpu.CompilerParams(
            collective_id=0, has_side_effects=True, vmem_limit_bytes=60 * 1024 * 1024
        ),
    )(lists, left_panels, right_panels)
    return out[None, None]


def shards(row_count, col_count, left_panels, right_panels, product_lists):
    left_blocks, blk = left_panels.shape[2], left_panels.shape[3]
    q_count, right_blocks = right_panels.shape[0], right_panels.shape[3]
    pair_count = product_lists.shape[3]
    lists = jnp.transpose(product_lists[0, 0], (2, 0, 1))
    step_count = lists.shape[1]
    width = pl.cdiv(max(pair_count, OCAP), 128) * 128
    groups = row_count // 2
    if groups == 4 and col_count == 4 and q_count * col_count == row_count == step_count and OCAP % (2 * PARTS) == 0 and right_blocks % 2 == 0:
        return folded_call(row_count, col_count, lists, left_panels, right_panels, width)
    out = pl.pallas_call(
        functools.partial(kernel, row_count, col_count),
        out_shape=jax.ShapeDtypeStruct((OCAP, blk, blk), jnp.float32),
        in_specs=[pl.BlockSpec(memory_space=pltpu.VMEM)] + [pl.BlockSpec(memory_space=pltpu.HBM)] * 2,
        out_specs=pl.BlockSpec(memory_space=pltpu.VMEM),
        scratch_shapes=[
            pltpu.VMEM((row_count, left_blocks, blk, blk), jnp.float32),
            pltpu.VMEM((q_count, col_count, right_blocks, blk, blk), jnp.float32),
            pltpu.VMEM((left_blocks, blk, 2 * blk), jnp.bfloat16),
            pltpu.VMEM((right_blocks, 2 * blk, 2 * blk), jnp.bfloat16),
            pltpu.VMEM((pair_count, blk, blk), jnp.float32),
            pltpu.VMEM((2 * step_count, width), jnp.int32),
            pltpu.SMEM((2 * step_count, width), jnp.int32),
            pltpu.SemaphoreType.DMA((2, q_count, col_count)),
            pltpu.SemaphoreType.DMA((q_count, col_count)),
            pltpu.SemaphoreType.DMA((groups,)),
            pltpu.SemaphoreType.DMA((groups,)),
            pltpu.SemaphoreType.DMA((2,)),
            pltpu.SemaphoreType.DMA((row_count,)),
            pltpu.SemaphoreType.DMA((2,)),
            pltpu.SemaphoreType.DMA((2 + q_count,)),
        ],
        compiler_params=pltpu.CompilerParams(
            collective_id=0, has_side_effects=True, vmem_limit_bytes=50 * 1024 * 1024
        ),
    )(lists, left_panels, right_panels)
    return out[None, None]


def solution(mesh):
    return jax.shard_map(
        functools.partial(shards, mesh.shape["row"], mesh.shape["col"]),
        mesh=mesh,
        in_specs=(
            P("row", "col", None, None, None),
            P(None, "col", "row", None, None, None),
            P("row", "col", None, None, None),
        ),
        out_specs=P("row", "col", None, None, None),
        check_vma=False,
    )
```
